32 devices in a mesh: win: 2 (over y), wide: 8 (over z, core), narrow: 2 (over x).
Axes of the slice: x: 2, y: 2, z: 4, core: 2. Of those that a mesh axis runs over, the one named last changes fastest.
Arguments:
- traces: float32 [4, 8, 256, 1024], P(('win', 'narrow'), 'wide'), parts along dimension 0, may hold values from -40 to 40
- mask: int32 [4, 8, 256], P(('win', 'narrow'), 'wide'), parts along dimension 0, may hold values 0 or 1
- omega: float32 [32, 810], P('narrow'), may hold values from -6 to 6
Outputs:
- filtered: float32 [4, 8, 256, 1024], P(('win', 'narrow'), 'wide'), parts along dimension 0
The draws below stay inside these ranges and needn't reach their ends.
There are 2 independent parts, one for each index of `win`. The reference program is written for one: setup_inputs(seed, part) draws one part's arguments, and reference() takes and returns one part's arrays. A program takes and returns all parts, laid end to end along the dimension named above; an argument that names none is the same for every part. Nothing has to cross between parts.
Inputs may be any that keep to these rules, and one draw needn't show every extreme that they name: `mask`: 1 keeps a trace, 0 marks it as not recorded.
All inputs are finite; a program needn't handle non-finite values. No bound on the sum of `mask` on one device may be relied on, other than what follows from the above.
Results may differ from the reference program's by a relative error of at most 0.00027.
Values sent between devices are 32-bit elements; how exact they have to be, the bound alone decides.
No kernel may reach another device: no remote copies, remote signals or barrier semaphores. Data moves between devices by JAX's collectives and lax.ppermute only.
A program may use at most 64 MiB of HBM per device.

```python
import math
import jax
import jax.numpy as jnp
from jax import lax

G3 = 16
G4 = 16
S = 1024
FIRST_BIN = 16
RANK = 32
G1 = 2
G2 = 8
G34 = 256
NF = 8
KCELLS = 810


def draw_traces(key, part):
    base_key = jax.random.fold_in(key, 11)
    keys_list = jax.random.split(base_key, 6)
    event_total = 48
    peak_rate = (FIRST_BIN + NF / 2.0) / S
    signs = (2 * jax.random.randint(keys_list[0], (event_total,), 0, 2) - 1).astype(jnp.float32)
    amplitude = jnp.exp(jax.random.uniform(keys_list[1], (event_total,), jnp.float32, jnp.log(0.15), jnp.log(0.6))) * signs
    onset = jax.random.uniform(keys_list[2], (event_total,), jnp.float32, 0.25 * S, 0.75 * S)
    extent = jnp.array([G1, G2, G3, G4], jnp.float32)
    slopes = jax.random.uniform(keys_list[3], (event_total, 4), jnp.float32, -1.0, 1.0) * (1.5 / peak_rate) / extent
    first_axis = jnp.arange(G1, dtype=jnp.float32) - (G1 - 1) / 2.0
    second_axis = jnp.arange(G2, dtype=jnp.float32) - (G2 - 1) / 2.0
    third_axis = jnp.arange(G3, dtype=jnp.float32) - (G3 - 1) / 2.0
    fourth_axis = jnp.arange(G4, dtype=jnp.float32) - (G4 - 1) / 2.0
    times_axis = jnp.arange(S, dtype=jnp.float32)

    def add_event(event_index, running):
        delay = onset[event_index] + slopes[event_index, 0] * first_axis[:, None, None, None] + slopes[event_index, 1] * second_axis[None, :, None, None] + slopes[event_index, 2] * third_axis[None, None, :, None] + slopes[event_index, 3] * fourth_axis[None, None, None, :]
        delay = delay.reshape(G1, G2, G3 * G4, 1)
        shifted = jnp.pi * peak_rate * (times_axis - delay)
        squared = shifted * shifted
        return running + amplitude[event_index] * (1.0 - 2.0 * squared) * jnp.exp(-squared)
    signal = lax.fori_loop(0, event_total, add_event, jnp.zeros((G1, G2, G3 * G4, S), jnp.float32))
    noise = 0.5 * jax.random.truncated_normal(keys_list[5], -4.0, 4.0, (G1, G2, G3 * G4, S), jnp.float32)
    return signal + noise


def place_ends(entries, rng, least, top_value):
    place = [jax.random.randint(jax.random.fold_in(rng, axis), (), 0, length) for axis, length in enumerate(entries.shape)]
    longest = entries.shape.index(max(entries.shape))
    neighbour = place[:longest] + [(place[longest] + 1) % entries.shape[longest]] + place[longest + 1:]
    return entries.at[tuple(place)].set(least).at[tuple(neighbour)].set(top_value)


def shard_levels(stream_key, dims, shards, smallest, largest):
    def one(axis_at, blocks):
        draws = jax.random.uniform(jax.random.fold_in(jax.random.fold_in(stream_key, 6), axis_at), (blocks,), jnp.float32, smallest / len(shards), largest / len(shards))
        return jnp.repeat(jnp.exp(draws), dims[axis_at] // blocks).reshape((-1,) + (1,) * (len(dims) - axis_at - 1))

    factor_of = one(*shards[0])
    for cut in shards[1:]:
        factor_of = factor_of * one(*cut)
    return factor_of


def bell_draw(own_key, shape, scale, most, cuts=(), kind=jnp.bfloat16):
    level = shard_levels(own_key, shape, cuts, -0.22, 0.18) if cuts else 1.0
    result = jax.random.normal(own_key, shape, jnp.float32) * scale * level
    return jnp.minimum(jnp.maximum(result, -most), most).astype(kind)


def setup_inputs(seed: int = 0, part: int = 0) -> dict:
    splits = jax.random.split(jax.random.key(seed), 4)
    part_splits = jax.random.split(jax.random.fold_in(splits[3], part), 4)
    return {
        "traces": draw_traces(jax.random.fold_in(jax.random.fold_in(splits[3], part), 71), part),
        "mask": place_ends((jax.random.randint(part_splits[1], (G1, G2, G34), 0, 4) < 3).astype(jnp.int32), jax.random.fold_in(part_splits[1], 1), 0, 1),
        "omega": bell_draw(splits[2], (RANK, KCELLS), 1.0, 6.0, ((0, 2),), jnp.float32),
    }


highest = lax.Precision.HIGHEST

def phase_table(freq_total):
    bin_index = FIRST_BIN + jnp.arange(freq_total, dtype=jnp.int32)
    time_index = jnp.arange(S, dtype=jnp.int32)
    angles = 2.0 * jnp.pi / S * (bin_index[:, None] * time_index[None, :] % S).astype(jnp.float32)
    return (jnp.cos(angles), jnp.sin(angles))

def correlation(length, keep_size):
    position = jnp.arange(length, dtype=jnp.int32)
    span_size = length - keep_size + 1
    return (jnp.minimum(position, keep_size - 1) - jnp.maximum(position - span_size + 1, 0) + 1).astype(jnp.float32)

def orthonormal(real_rows, imag_rows):
    column_count = real_rows.shape[0]
    row_width = real_rows.shape[1]
    upper_half = jnp.concatenate([real_rows, imag_rows], axis=1)
    lower_half = jnp.concatenate([-imag_rows, real_rows], axis=1)
    stacked = jnp.stack([upper_half, lower_half], axis=1).reshape(2 * column_count, 2 * row_width)
    gram_matrix = jnp.dot(stacked, stacked.T, precision=highest)
    factor = jnp.linalg.cholesky(gram_matrix)
    stacked = lax.linalg.triangular_solve(factor, stacked, left_side=True, lower=True)
    chosen = stacked.reshape(column_count, 2, 2 * row_width)[:, 0]
    return (chosen[:, :row_width], chosen[:, row_width:])

def reference(traces, mask, omega):
    keep_sizes = (G1 // 2, G2 // 2, G3 // 2, G4 // 2)
    span_sizes = (G1 - keep_sizes[0] + 1, G2 - keep_sizes[1] + 1, G3 - keep_sizes[2] + 1, G4 - keep_sizes[3] + 1)
    row_count = keep_sizes[0] * keep_sizes[1] * keep_sizes[2] * keep_sizes[3]
    masked = traces * mask.astype(jnp.float32)[..., None]
    cosine, sine_table = phase_table(NF)
    flat_traces = masked.reshape(G1 * G2 * G3 * G4, S)
    norm_scale = 1.0 / math.sqrt(S)
    spec_real = jnp.dot(flat_traces, cosine.T, precision=highest) * norm_scale
    spec_imag = -jnp.dot(flat_traces, sine_table.T, precision=highest) * norm_scale
    slices_real = spec_real.T.reshape(NF, G1, G2, G3, G4)
    slices_imag = spec_imag.T.reshape(NF, G1, G2, G3, G4)
    axes_grid = (1, 2, 3, 4)
    test_grid = omega.reshape(RANK, span_sizes[0], span_sizes[1], span_sizes[2], span_sizes[3])
    test_grid = jnp.pad(test_grid, ((0, 0), (0, G1 - span_sizes[0]), (0, G2 - span_sizes[1]), (0, G3 - span_sizes[2]), (0, G4 - span_sizes[3])))
    test_hat = jnp.fft.fftn(test_grid, axes=axes_grid)
    inside = ((jnp.arange(G1) < span_sizes[0])[:, None, None, None] & (jnp.arange(G2) < span_sizes[1])[None, :, None, None] & (jnp.arange(G3) < span_sizes[2])[None, None, :, None] & (jnp.arange(G4) < span_sizes[3])[None, None, None, :]).astype(jnp.float32)
    counts = correlation(G1, keep_sizes[0])[:, None, None, None] * correlation(G2, keep_sizes[1])[None, :, None, None] * correlation(G3, keep_sizes[2])[None, None, :, None] * correlation(G4, keep_sizes[3])[None, None, None, :]

    def one_slice(slice_pair):
        field_grid = slice_pair[0] + 1j * slice_pair[1]
        field_hat = jnp.fft.fftn(field_grid)
        sketch = jnp.fft.ifftn(field_hat[None] * jnp.conj(test_hat), axes=axes_grid)
        sketch = sketch[:, :keep_sizes[0], :keep_sizes[1], :keep_sizes[2], :keep_sizes[3]].reshape(RANK, row_count)
        basis_real, basis_imag = orthonormal(jnp.real(sketch), jnp.imag(sketch))
        basis_grid = (basis_real + 1j * basis_imag).reshape(RANK, keep_sizes[0], keep_sizes[1], keep_sizes[2], keep_sizes[3])
        basis_grid = jnp.pad(basis_grid, ((0, 0), (0, G1 - keep_sizes[0]), (0, G2 - keep_sizes[1]), (0, G3 - keep_sizes[2]), (0, G4 - keep_sizes[3])))
        basis_hat = jnp.fft.fftn(basis_grid, axes=axes_grid)
        coeffs = jnp.fft.ifftn(jnp.conj(basis_hat) * field_hat[None], axes=axes_grid) * inside
        coeffs_hat = jnp.fft.fftn(coeffs, axes=axes_grid)
        rebuilt = jnp.fft.ifftn(lax.optimization_barrier(jnp.sum(basis_hat * coeffs_hat, axis=0))) / counts
        return (jnp.real(rebuilt), jnp.imag(rebuilt))
    rebuilt_real, rebuilt_imag = lax.map(one_slice, (slices_real, slices_imag))
    cells_real = rebuilt_real.reshape(NF, G1 * G2 * G3 * G4).T
    cells_imag = rebuilt_imag.reshape(NF, G1 * G2 * G3 * G4).T
    filtered = (jnp.dot(cells_real, cosine, precision=highest) - jnp.dot(cells_imag, sine_table, precision=highest)) * math.sqrt(2.0 / NF)
    return filtered.reshape(G1, G2, G3 * G4, S)
```

```python
import functools
import math

import jax
import jax.numpy as jnp
import ml_dtypes
import numpy as np
from jax import lax
from jax.experimental import pallas as pl
from jax.experimental.pallas import tpu as pltpu
from jax.sharding import PartitionSpec as P

G3 = 16
G4 = 16
S = 1024
FREQ_DEV = 1
FIRST_BIN = 16
LANES = 128
CELLS = G3 * G4
KEEP3, KEEP4 = G3 // 2, G4 // 2
SPAN3, SPAN4 = G3 - KEEP3 + 1, G4 - KEEP4 + 1
SHIFT3, SHIFT4 = (SPAN3 - 1) // 2, (SPAN4 - 1) // 2
ROWS = KEEP3 * KEEP4
COLS = SPAN3 * SPAN4
PIECES = CELLS // LANES

VMEM = pl.BlockSpec(memory_space=pltpu.VMEM)
highest = lax.Precision.HIGHEST


def halves(table):
    table = np.asarray(table, np.float32)
    high = table.astype(ml_dtypes.bfloat16)
    low = (table - high.astype(np.float32)).astype(ml_dtypes.bfloat16)
    return high, low


def phases(freq_total):
    bins = FIRST_BIN + np.arange(freq_total)
    return 2.0 * np.pi * ((bins[:, None] * np.arange(S)[None, :]) % S) / S


def cell_angles(positions3, positions4):
    wave = np.arange(CELLS)
    turns = (
        np.outer(positions3, wave // G4) % G3 / G3 + np.outer(positions4, wave % G4) % G4 / G4
    )
    return 2.0 * np.pi * turns


def correlation(length, keep_size):
    position = np.arange(length)
    span_size = length - keep_size + 1
    return (
        np.minimum(position, keep_size - 1) - np.maximum(position - span_size + 1, 0) + 1
    ).astype(np.float64)


def spectrum_table(freq_total, copies):
    angles = np.repeat(phases(freq_total), copies, 0)
    return np.concatenate([np.cos(angles), -np.sin(angles)], 0) / math.sqrt(S)


def synthesis_table(freq_total):
    angles = phases(freq_total)
    return np.concatenate([np.cos(angles), -np.sin(angles)], 0) * math.sqrt(2.0 / freq_total)


def centred_angles():
    cell = np.arange(CELLS)
    return cell_angles(cell // G4 - SHIFT3, cell % G4 - SHIFT4)


def omega_table():
    column = np.arange(COLS)
    angles = cell_angles(column // SPAN4, column % SPAN4)
    table = np.zeros((LANES, 2 * CELLS))
    table[:COLS] = np.concatenate([np.cos(angles), -np.sin(angles)], 1)
    return table


def sketch_table():
    row = np.arange(ROWS)
    angles = cell_angles(row // KEEP4 - SHIFT3, row % KEEP4 - SHIFT4).T
    real, imag = np.cos(angles) / CELLS, np.sin(angles) / CELLS
    from_real = np.concatenate([real, imag, imag, -real], 1)
    from_imag = np.concatenate([-imag, real, real, imag], 1)
    return np.concatenate([from_real, from_imag], 0)


def basis_table():
    row = np.arange(ROWS)
    angles = cell_angles(row // KEEP4, row % KEEP4)
    real, imag = np.cos(angles), np.sin(angles)
    return np.concatenate(
        [np.concatenate([real, -imag], 1), np.concatenate([imag, real], 1)], 0
    )


def window_table():
    parts = []
    for length, shift in ((G3, SHIFT3), (G4, SHIFT4)):
        wave = np.arange(length)
        turns = (wave[:, None] - wave[None, :])[:, :, None] * np.arange(-shift, shift + 1) / length
        parts.append(np.cos(2.0 * np.pi * turns).sum(-1) / length)
    return np.kron(parts[0], parts[1])


def split(value):
    high = value.astype(jnp.bfloat16)
    low = (value - high.astype(jnp.float32)).astype(jnp.bfloat16)
    return high, low


def dot(left, right):
    return jnp.dot(left, right, preferred_element_type=jnp.float32)


def wide_dot(value, high, low):
    rows = value.shape[0]
    value_high, value_low = split(value)
    main = dot(jnp.concatenate([value_high, value_low], 0), high)
    return main[:rows] + (main[rows:] + dot(value_high, low))


def spectrum_kernel(traces_ref, mask_ref, table_ref, out_ref):
    rows = table_ref.shape[0] // 2
    dests = rows // 2
    high, low = split(traces_ref[...])
    contract = (((1,), (1,)), ((), ()))
    main = lax.dot_general(table_ref[...], high, contract, preferred_element_type=jnp.float32)
    rest = lax.dot_general(table_ref[:rows], low, contract, preferred_element_type=jnp.float32)
    result = (main[:rows] + (main[rows:] + rest)) * mask_ref[...].astype(jnp.float32)
    for part in range(2):
        for piece in range(PIECES):
            out_ref[:, part * PIECES + piece, :] = result[
                part * dests : (part + 1) * dests, piece * LANES : (piece + 1) * LANES
            ]


def omega_kernel(columns, *refs):
    omega_refs = refs[:-3]
    high_ref, low_ref, out_ref = refs[-3:]
    omega = jnp.concatenate([ref[...] for ref in omega_refs], 0)
    pad = jnp.zeros((omega.shape[0], LANES - COLS), jnp.float32)
    blocks = [
        jnp.concatenate([omega[:, k * COLS : (k + 1) * COLS], pad], 1) for k in range(columns)
    ]
    out_ref[...] = wide_dot(jnp.concatenate(blocks, 0), high_ref[...], low_ref[...])


def invert(gram_real, gram_imag):
    size = gram_real.shape[0]
    row_index = lax.broadcasted_iota(jnp.int32, (size, size), 0)
    column_index = lax.broadcasted_iota(jnp.int32, (size, size), 1)
    identity = (row_index == column_index).astype(jnp.float32)
    real = jnp.concatenate([gram_real, identity], 1)
    imag = jnp.concatenate([gram_imag, jnp.zeros_like(identity)], 1)
    wide_index = lax.broadcasted_iota(jnp.int32, (size, 2 * size), 0)
    for j in range(size):
        scale = 1.0 / real[j : j + 1, j : j + 1]
        pivot_real = real[j : j + 1, :] * scale
        pivot_imag = imag[j : j + 1, :] * scale
        factor_real = real[:, j : j + 1]
        factor_imag = imag[:, j : j + 1]
        here = wide_index == j
        next_real = real - (factor_real * pivot_real - factor_imag * pivot_imag)
        next_imag = imag - (factor_real * pivot_imag + factor_imag * pivot_real)
        real = jnp.where(here, pivot_real, next_real)
        imag = jnp.where(here, pivot_imag, next_imag)
    return real[:, size:], imag[:, size:]


def core_kernel(
    dims,
    x_ref,
    omega_ref,
    analysis_high,
    analysis_low,
    sketch_high,
    sketch_low,
    basis_high,
    basis_low,
    window_high,
    window_low,
    back_high,
    back_low,
    weight_ref,
    out_ref,
    xhat,
    shat,
    bhat,
    uhat,
    dhat,
    ghat,
):
    first, second, rank = dims
    keep1, keep2 = first // 2, second // 2
    span1, span2 = first - keep1 + 1, second - keep2 + 1
    own = lax.axis_index("narrow")
    half = CELLS
    tiles = rank // 8
    pieces = CELLS // LANES
    small = keep1 * keep2 * span1 * span2 <= 64

    def sweep(count, body, carry):
        if small:
            for i in range(count):
                carry = body(i, carry)
            return carry
        return lax.fori_loop(0, count, body, carry)

    def rows(start, count=8):
        if isinstance(start, int):
            return pl.ds(start, count)
        return pl.ds(pl.multiple_of(start, 8), count)

    def lanes(part, piece):
        start = part * half + piece * LANES
        return pl.ds(start, LANES)

    planes = first * second
    spectrum = jnp.concatenate(
        [
            jnp.concatenate([x_ref[:, part * pieces + piece, :] for piece in range(pieces)], 1)
            for part in range(2)
        ],
        0,
    )
    both = wide_dot(spectrum, analysis_high[...], analysis_low[...])
    hats = (
        both[:planes, :half] + both[planes:, half:],
        both[planes:, :half] - both[:planes, half:],
    )
    for part in range(2):
        for piece in range(pieces):
            values = hats[part][:, piece * LANES : (piece + 1) * LANES]
            xhat[:, part * pieces + piece] = jnp.broadcast_to(
                values[:, None, :], (planes, 8, LANES)
            )

    def load_x(g1, g2, piece):
        row = g2 * first + g1
        return xhat[row, piece], xhat[row, pieces + piece]

    for piece in range(pieces):
        cache = {}

        def cached_x(g1, g2):
            if not small:
                return load_x(g1, g2, piece)
            if (g1, g2) not in cache:
                cache[g1, g2] = load_x(g1, g2, piece)
            return cache[g1, g2]

        def sketch_tile(tile, carry):
            def first_keep(l1, carry):
                zero = jnp.zeros((8, LANES), jnp.float32)

                def columns(k1, sums):
                    def column(k2, sums):
                        start = (k1 * span2 + k2) * rank + tile * 8
                        w_real = omega_ref[rows(start), lanes(0, piece)]
                        w_imag = omega_ref[rows(start), lanes(1, piece)]
                        sums = list(sums)
                        for l2 in range(keep2):
                            x_real, x_imag = cached_x(l1 + k1, l2 + k2)
                            real, imag = sums[l2]
                            sums[l2] = (
                                real + (x_real * w_real + x_imag * w_imag),
                                imag + (x_imag * w_real - x_real * w_imag),
                            )
                        return tuple(sums)

                    return sweep(span2, column, sums)

                sums = sweep(span1, columns, ((zero, zero),) * keep2)
                for l2 in range(keep2):
                    start = (l1 * keep2 + l2) * rank + tile * 8
                    shat[rows(start), lanes(0, piece)] = sums[l2][0]
                    shat[rows(start), lanes(1, piece)] = sums[l2][1]
                return carry

            return sweep(keep1, first_keep, carry)

        sweep(tiles, sketch_tile, 0)

    blocks = keep1 * keep2
    sketch = wide_dot(shat[...], sketch_high[...], sketch_low[...])
    straight = jnp.concatenate(
        [sketch[b * rank : (b + 1) * rank, : 2 * ROWS] for b in range(blocks)], 1
    )
    turned = jnp.concatenate(
        [sketch[b * rank : (b + 1) * rank, 2 * ROWS :] for b in range(blocks)], 1
    )
    contract = (((1,), (1,)), ((), ()))
    gram_real = lax.dot_general(
        straight, straight, contract, precision=highest, preferred_element_type=jnp.float32
    )
    gram_imag = lax.dot_general(
        straight, turned, contract, precision=highest, preferred_element_type=jnp.float32
    )
    inverse_real, inverse_imag = invert(gram_real, gram_imag)

    bhat[...] = wide_dot(sketch[:, : 2 * ROWS], basis_high[...], basis_low[...])
    mixer = jnp.concatenate([inverse_real, inverse_imag], 1)

    def mix(b, carry):
        real = bhat[rows(b * rank, rank), :half]
        imag = bhat[rows(b * rank, rank), half:]
        uhat[rows(b * rank, rank), :half] = jnp.dot(
            mixer,
            jnp.concatenate([real, imag], 0),
            precision=highest,
            preferred_element_type=jnp.float32,
        )
        uhat[rows(b * rank, rank), half:] = jnp.dot(
            mixer,
            jnp.concatenate([imag, -real], 0),
            precision=highest,
            preferred_element_type=jnp.float32,
        )
        return carry

    sweep(blocks, mix, 0)

    ghat[...] = jnp.zeros_like(ghat)

    def own_pair(a, carry):
        k1 = own - a
        valid = jnp.logical_and(k1 >= 0, k1 < span1).astype(jnp.float32)
        k1 = jnp.clip(k1, 0, span1 - 1)
        for piece in range(pieces):
            cache = {}

            def cached_x(l1, g2):
                if not small:
                    return load_x(l1 + k1, g2, piece)
                if (l1, g2) not in cache:
                    cache[l1, g2] = load_x(l1 + k1, g2, piece)
                return cache[l1, g2]

            def column_tile(tile, carry):
                zero = jnp.zeros((8, LANES), jnp.float32)

                def first_keep(l1, sums):
                    sums = list(sums)
                    for l2 in range(keep2):
                        start = (l1 * keep2 + l2) * rank + tile * 8
                        s_real = bhat[rows(start), lanes(0, piece)]
                        s_imag = bhat[rows(start), lanes(1, piece)]
                        for k2 in range(span2):
                            x_real, x_imag = cached_x(l1, l2 + k2)
                            real, imag = sums[k2]
                            sums[k2] = (
                                real + (s_real * x_real + s_imag * x_imag),
                                imag + (s_real * x_imag - s_imag * x_real),
                            )
                    return tuple(sums)

                sums = sweep(keep1, first_keep, ((zero, zero),) * span2)
                for k2 in range(span2):
                    for part in range(2):
                        start = (part * span2 + k2) * rank + tile * 8
                        dhat[rows(start), pl.ds(piece * LANES, LANES)] = sums[k2][part]
                return carry

            sweep(tiles, column_tile, 0)
        dhat[...] = wide_dot(dhat[...], window_high[...], window_low[...])
        for piece in range(pieces):

            def rebuild_tile(tile, sums):
                sums = list(sums)
                us = []
                for l2 in range(keep2):
                    start = (a * keep2 + l2) * rank + tile * 8
                    us.append(
                        (
                            uhat[rows(start), lanes(0, piece)],
                            uhat[rows(start), lanes(1, piece)],
                        )
                    )
                for k2 in range(span2):
                    d_real = dhat[rows(k2 * rank + tile * 8), pl.ds(piece * LANES, LANES)]
                    d_imag = dhat[
                        rows((span2 + k2) * rank + tile * 8), pl.ds(piece * LANES, LANES)
                    ]
                    for l2 in range(keep2):
                        u_real, u_imag = us[l2]
                        real, imag = sums[l2 + k2]
                        sums[l2 + k2] = (
                            real + (u_real * d_real - u_imag * d_imag),
                            imag + (u_real * d_imag + u_imag * d_real),
                        )
                return tuple(sums)

            zero = jnp.zeros((8, LANES), jnp.float32)
            sums = sweep(tiles, rebuild_tile, ((zero, zero),) * second)
            for part in range(2):
                summed = jnp.concatenate(
                    [jnp.sum(sums[g2][part], 0, keepdims=True) for g2 in range(second)], 0
                )
                place = pl.ds(piece * LANES, LANES)
                where = pl.ds(part * second, second)
                ghat[where, place] = ghat[where, place] + summed * valid
        return carry

    sweep(keep1, own_pair, 0)

    both = wide_dot(ghat[...], back_high[...], back_low[...])
    real = both[:second, :half] - both[second:, half:]
    imag = both[:second, half:] + both[second:, :half]
    weight = weight_ref[pl.ds(pl.multiple_of(own * second, 8), second), :]
    real = real * weight
    imag = imag * weight
    for piece in range(pieces):
        out_ref[:, piece, :] = real[:, piece * LANES : (piece + 1) * LANES]
        out_ref[:, pieces + piece, :] = imag[:, piece * LANES : (piece + 1) * LANES]


def synthesis_kernel(cells_ref, table_ref, out_ref):
    parts = [
        jnp.concatenate([cells_ref[:, part * PIECES + piece, :] for piece in range(PIECES)], 1)
        for part in range(2)
    ]
    high, low = split(jnp.concatenate(parts, 0))
    stacked = jnp.concatenate([high, low, high], 0)
    out_ref[...] = lax.dot_general(
        stacked, table_ref[...], (((0,), (0,)), ((), ())), preferred_element_type=jnp.float32
    )


def per_device(traces, mask, omega):
    narrow_count = lax.axis_size("narrow")
    wide_count = lax.axis_size("wide")
    assert traces.shape[:2] == (1, 1)
    first, second = narrow_count, wide_count
    freq_total = FREQ_DEV * wide_count
    keep1, keep2 = first // 2, second // 2
    span1, span2 = first - keep1 + 1, second - keep2 + 1
    rank = omega.shape[0] * narrow_count
    dests = wide_count * narrow_count
    lines = 2 * PIECES

    omegas = [omega]
    for step in range(1, narrow_count):
        ring = [(i, (i + step) % narrow_count) for i in range(narrow_count)]
        omegas.append(lax.ppermute(omega, "narrow", ring))

    high, low = halves(spectrum_table(freq_total, narrow_count))
    blocks = pl.pallas_call(
        spectrum_kernel,
        out_shape=jax.ShapeDtypeStruct((dests, lines, LANES), jnp.float32),
        in_specs=[VMEM] * 3,
        out_specs=VMEM,
        name="spectrum",
    )(traces.reshape(CELLS, S), mask.reshape(1, CELLS), np.concatenate([high, low], 0))
    grid = lax.all_to_all(blocks, ("wide", "narrow"), split_axis=0, concat_axis=0, tiled=True)

    if omega.shape[0] % 8:
        omegas = [jnp.concatenate(omegas, 0)]
    columns = span1 * span2
    omega_hat = pl.pallas_call(
        functools.partial(omega_kernel, columns),
        out_shape=jax.ShapeDtypeStruct((columns * rank, 2 * CELLS), jnp.float32),
        in_specs=[VMEM] * (len(omegas) + 2),
        out_specs=VMEM,
        cost_estimate=pl.CostEstimate(
            flops=6 * columns * rank * LANES * 2 * CELLS,
            bytes_accessed=4 * columns * rank * 2 * CELLS,
            transcendentals=0,
        ),
        name="omega",
    )(*omegas, *halves(omega_table()))

    angles = centred_angles()
    counts = (
        correlation(first, keep1)[:, None, None]
        * correlation(second, keep2)[None, :, None]
        * np.outer(correlation(G3, KEEP3), correlation(G4, KEEP4)).reshape(1, 1, CELLS)
    ).reshape(first * second, CELLS)
    forward = np.concatenate([np.cos(angles), np.sin(angles)], 1)
    backward = np.concatenate([np.cos(angles.T), np.sin(angles.T)], 1) / CELLS
    tables = (
        *halves(forward),
        *halves(sketch_table()),
        *halves(basis_table()),
        *halves(window_table()),
        *halves(backward),
        (1.0 / counts).astype(np.float32),
    )
    area = keep1 * keep2 * rank
    scratch = [
        (first * second, lines, 8, LANES),
        (area, 2 * CELLS),
        (area, 2 * CELLS),
        (area, 2 * CELLS),
        (2 * span2 * rank, CELLS),
        (2 * second, CELLS),
    ]
    rebuilt = pl.pallas_call(
        functools.partial(core_kernel, (first, second, rank)),
        out_shape=jax.ShapeDtypeStruct((second, lines, LANES), jnp.float32),
        in_specs=[VMEM] * (2 + len(tables)),
        out_specs=VMEM,
        scratch_shapes=[pltpu.VMEM(shape, jnp.float32) for shape in scratch],
        name="core",
    )(grid, omega_hat, *tables)
    returned = lax.all_to_all(rebuilt, "wide", split_axis=0, concat_axis=0, tiled=True)

    high, low = halves(synthesis_table(freq_total))
    filtered = pl.pallas_call(
        synthesis_kernel,
        out_shape=jax.ShapeDtypeStruct((CELLS, S), jnp.float32),
        in_specs=[VMEM] * 2,
        out_specs=VMEM,
        name="synthesis",
    )(returned, np.concatenate([high, high, low], 0))
    return filtered.reshape(traces.shape)


def solution(mesh):
    return jax.shard_map(
        per_device,
        mesh=mesh,
        in_specs=(
            P(("win", "narrow"), "wide", None, None),
            P(("win", "narrow"), "wide", None),
            P("narrow", None),
        ),
        out_specs=P(("win", "narrow"), "wide", None, None),
        check_vma=False,
    )
```

```python
import functools
import math

import jax
import jax.numpy as jnp
import ml_dtypes
import numpy as np
from jax import lax
from jax.experimental import pallas as pl
from jax.experimental.pallas import tpu as pltpu
from jax.sharding import PartitionSpec as P

G3 = 16
G4 = 16
S = 1024
FREQ_DEV = 1
FIRST_BIN = 16
LANES = 128
MIB = 1 << 20
CHUNKS = 4
CELLS = G3 * G4
KEEP3, KEEP4 = G3 // 2, G4 // 2
SPAN3, SPAN4 = G3 - KEEP3 + 1, G4 - KEEP4 + 1
SHIFT3, SHIFT4 = (SPAN3 - 1) // 2, (SPAN4 - 1) // 2
ROWS = KEEP3 * KEEP4
COLS = SPAN3 * SPAN4
PIECES = CELLS // LANES

HBM = pl.BlockSpec(memory_space=pltpu.HBM)
VMEM = pl.BlockSpec(memory_space=pltpu.VMEM)
highest = lax.Precision.HIGHEST


def halves(table):
    table = np.asarray(table, np.float32)
    high = table.astype(ml_dtypes.bfloat16)
    low = (table - high.astype(np.float32)).astype(ml_dtypes.bfloat16)
    return high, low


def phases(freq_total):
    bins = FIRST_BIN + np.arange(freq_total)
    return 2.0 * np.pi * ((bins[:, None] * np.arange(S)[None, :]) % S) / S


def cell_angles(positions3, positions4):
    wave = np.arange(CELLS)
    turns = (
        np.outer(positions3, wave // G4) % G3 / G3 + np.outer(positions4, wave % G4) % G4 / G4
    )
    return 2.0 * np.pi * turns


def correlation(length, keep_size):
    position = np.arange(length)
    span_size = length - keep_size + 1
    return (
        np.minimum(position, keep_size - 1) - np.maximum(position - span_size + 1, 0) + 1
    ).astype(np.float64)


def spectrum_table(freq_total, copies):
    angles = np.repeat(phases(freq_total), copies, 0)
    return np.concatenate([np.cos(angles), -np.sin(angles)], 0) / math.sqrt(S)


def synthesis_table(freq_total):
    angles = phases(freq_total)
    return np.concatenate([np.cos(angles), -np.sin(angles)], 0) * math.sqrt(2.0 / freq_total)


def centred_angles():
    cell = np.arange(CELLS)
    return cell_angles(cell // G4 - SHIFT3, cell % G4 - SHIFT4)


def omega_table():
    column = np.arange(COLS)
    angles = cell_angles(column // SPAN4, column % SPAN4)
    table = np.zeros((LANES, 2 * CELLS))
    table[:COLS] = np.concatenate([np.cos(angles), -np.sin(angles)], 1)
    return table


def sketch_table():
    row = np.arange(ROWS)
    angles = cell_angles(row // KEEP4 - SHIFT3, row % KEEP4 - SHIFT4).T
    real, imag = np.cos(angles) / CELLS, np.sin(angles) / CELLS
    from_real = np.concatenate([real, imag, imag, -real], 1)
    from_imag = np.concatenate([-imag, real, real, imag], 1)
    return np.concatenate([from_real, from_imag], 0)


def basis_table():
    row = np.arange(ROWS)
    angles = cell_angles(row // KEEP4, row % KEEP4)
    real, imag = np.cos(angles), np.sin(angles)
    return np.concatenate(
        [np.concatenate([real, -imag], 1), np.concatenate([imag, real], 1)], 0
    )


def window_table():
    parts = []
    for length, shift in ((G3, SHIFT3), (G4, SHIFT4)):
        wave = np.arange(length)
        turns = (wave[:, None] - wave[None, :])[:, :, None] * np.arange(-shift, shift + 1) / length
        parts.append(np.cos(2.0 * np.pi * turns).sum(-1) / length)
    return np.kron(parts[0], parts[1])


def split(value):
    high = value.astype(jnp.bfloat16)
    low = (value - high.astype(jnp.float32)).astype(jnp.bfloat16)
    return high, low


def dot(left, right):
    return jnp.dot(left, right, preferred_element_type=jnp.float32)


def wide_dot(value, high, low):
    rows = value.shape[0]
    value_high, value_low = split(value)
    main = dot(jnp.concatenate([value_high, value_low], 0), high)
    return main[:rows] + (main[rows:] + dot(value_high, low))


def spectrum_kernel(traces_ref, mask_ref, table_ref, out_ref, traces, mask, table, sems):
    rows = table.shape[0] // 2
    dests = rows // 2
    chunks, _, width = traces.shape
    copies = [
        pltpu.make_async_copy(table_ref, table, sems.at[0]),
        pltpu.make_async_copy(mask_ref, mask, sems.at[1]),
    ] + [
        pltpu.make_async_copy(
            traces_ref.at[:, pl.ds(i * width, width)], traces.at[i], sems.at[2 + i]
        )
        for i in range(chunks)
    ]
    for copy in copies:
        copy.start()
    copies[0].wait()
    contract = (((1,), (1,)), ((), ()))
    total = jnp.zeros((2 * rows, CELLS), jnp.float32)
    rest = jnp.zeros((rows, CELLS), jnp.float32)
    for i in range(chunks):
        copies[2 + i].wait()
        high, low = split(traces[i])
        place = pl.ds(i * width, width)
        total += lax.dot_general(
            table[:, place], high, contract, preferred_element_type=jnp.float32
        )
        rest += lax.dot_general(
            table[:rows, place], low, contract, preferred_element_type=jnp.float32
        )
    copies[1].wait()
    result = (total[:rows] + (total[rows:] + rest)) * mask[...].astype(jnp.float32)
    for part in range(2):
        for piece in range(PIECES):
            out_ref[:, part * PIECES + piece, :] = result[
                part * dests : (part + 1) * dests, piece * LANES : (piece + 1) * LANES
            ]


def omega_kernel(columns, *refs):
    omega_refs = refs[:-3]
    high_ref, low_ref, out_ref = refs[-3:]
    omega = jnp.concatenate([ref[...] for ref in omega_refs], 0)
    pad = jnp.zeros((omega.shape[0], LANES - COLS), jnp.float32)
    blocks = [
        jnp.concatenate([omega[:, k * COLS : (k + 1) * COLS], pad], 1) for k in range(columns)
    ]
    out_ref[...] = wide_dot(jnp.concatenate(blocks, 0), high_ref[...], low_ref[...])


def invert(gram_real, gram_imag):
    size = gram_real.shape[0]
    row_index = lax.broadcasted_iota(jnp.int32, (size, size), 0)
    column_index = lax.broadcasted_iota(jnp.int32, (size, size), 1)
    identity = (row_index == column_index).astype(jnp.float32)
    real = jnp.concatenate([gram_real, identity], 1)
    imag = jnp.concatenate([gram_imag, jnp.zeros_like(identity)], 1)
    wide_index = lax.broadcasted_iota(jnp.int32, (size, 2 * size), 0)
    for j in range(size):
        scale = 1.0 / real[j : j + 1, j : j + 1]
        pivot_real = real[j : j + 1, :] * scale
        pivot_imag = imag[j : j + 1, :] * scale
        factor_real = real[:, j : j + 1]
        factor_imag = imag[:, j : j + 1]
        here = wide_index == j
        next_real = real - (factor_real * pivot_real - factor_imag * pivot_imag)
        next_imag = imag - (factor_real * pivot_imag + factor_imag * pivot_real)
        real = jnp.where(here, pivot_real, next_real)
        imag = jnp.where(here, pivot_imag, next_imag)
    return real[:, size:], imag[:, size:]


def core_kernel(
    dims,
    x_ref,
    omega_ref,
    analysis_high,
    analysis_low,
    sketch_high,
    sketch_low,
    basis_high,
    basis_low,
    window_high,
    window_low,
    back_high,
    back_low,
    weight_ref,
    out_ref,
    xhat,
    shat,
    bhat,
    uhat,
    dhat,
    ghat,
):
    first, second, rank = dims
    keep1, keep2 = first // 2, second // 2
    span1, span2 = first - keep1 + 1, second - keep2 + 1
    own = lax.axis_index("narrow")
    half = CELLS
    tiles = rank // 8
    pieces = CELLS // LANES
    small = keep1 * keep2 * span1 * span2 <= 64

    def sweep(count, body, carry):
        if small:
            for i in range(count):
                carry = body(i, carry)
            return carry
        return lax.fori_loop(0, count, body, carry)

    def rows(start, count=8):
        if isinstance(start, int):
            return pl.ds(start, count)
        return pl.ds(pl.multiple_of(start, 8), count)

    def lanes(part, piece):
        start = part * half + piece * LANES
        return pl.ds(start, LANES)

    planes = first * second
    spectrum = jnp.concatenate(
        [
            jnp.concatenate([x_ref[:, part * pieces + piece, :] for piece in range(pieces)], 1)
            for part in range(2)
        ],
        0,
    )
    both = wide_dot(spectrum, analysis_high[...], analysis_low[...])
    hats = (
        both[:planes, :half] + both[planes:, half:],
        both[planes:, :half] - both[:planes, half:],
    )
    for part in range(2):
        for piece in range(pieces):
            values = hats[part][:, piece * LANES : (piece + 1) * LANES]
            xhat[:, part * pieces + piece] = jnp.broadcast_to(
                values[:, None, :], (planes, 8, LANES)
            )

    def load_x(g1, g2, piece):
        row = g2 * first + g1
        return xhat[row, piece], xhat[row, pieces + piece]

    for piece in range(pieces):
        cache = {}

        def cached_x(g1, g2):
            if not small:
                return load_x(g1, g2, piece)
            if (g1, g2) not in cache:
                cache[g1, g2] = load_x(g1, g2, piece)
            return cache[g1, g2]

        def sketch_tile(tile, carry):
            def first_keep(l1, carry):
                zero = jnp.zeros((8, LANES), jnp.float32)

                def columns(k1, sums):
                    def column(k2, sums):
                        start = (k1 * span2 + k2) * rank + tile * 8
                        w_real = omega_ref[rows(start), lanes(0, piece)]
                        w_imag = omega_ref[rows(start), lanes(1, piece)]
                        sums = list(sums)
                        for l2 in range(keep2):
                            x_real, x_imag = cached_x(l1 + k1, l2 + k2)
                            real, imag = sums[l2]
                            sums[l2] = (
                                real + (x_real * w_real + x_imag * w_imag),
                                imag + (x_imag * w_real - x_real * w_imag),
                            )
                        return tuple(sums)

                    return sweep(span2, column, sums)

                sums = sweep(span1, columns, ((zero, zero),) * keep2)
                for l2 in range(keep2):
                    start = (l1 * keep2 + l2) * rank + tile * 8
                    shat[rows(start), lanes(0, piece)] = sums[l2][0]
                    shat[rows(start), lanes(1, piece)] = sums[l2][1]
                return carry

            return sweep(keep1, first_keep, carry)

        sweep(tiles, sketch_tile, 0)

    blocks = keep1 * keep2
    sketch = wide_dot(shat[...], sketch_high[...], sketch_low[...])
    straight = jnp.concatenate(
        [sketch[b * rank : (b + 1) * rank, : 2 * ROWS] for b in range(blocks)], 1
    )
    turned = jnp.concatenate(
        [sketch[b * rank : (b + 1) * rank, 2 * ROWS :] for b in range(blocks)], 1
    )
    contract = (((1,), (1,)), ((), ()))
    gram_real = lax.dot_general(
        straight, straight, contract, precision=highest, preferred_element_type=jnp.float32
    )
    gram_imag = lax.dot_general(
        straight, turned, contract, precision=highest, preferred_element_type=jnp.float32
    )
    inverse_real, inverse_imag = invert(gram_real, gram_imag)

    bhat[...] = wide_dot(sketch[:, : 2 * ROWS], basis_high[...], basis_low[...])
    mixer = jnp.concatenate([inverse_real, inverse_imag], 1)

    def mix(b, carry):
        real = bhat[rows(b * rank, rank), :half]
        imag = bhat[rows(b * rank, rank), half:]
        uhat[rows(b * rank, rank), :half] = jnp.dot(
            mixer,
            jnp.concatenate([real, imag], 0),
            precision=highest,
            preferred_element_type=jnp.float32,
        )
        uhat[rows(b * rank, rank), half:] = jnp.dot(
            mixer,
            jnp.concatenate([imag, -real], 0),
            precision=highest,
            preferred_element_type=jnp.float32,
        )
        return carry

    sweep(blocks, mix, 0)

    ghat[...] = jnp.zeros_like(ghat)

    def own_pair(a, carry):
        k1 = own - a
        valid = jnp.logical_and(k1 >= 0, k1 < span1).astype(jnp.float32)
        k1 = jnp.clip(k1, 0, span1 - 1)
        for piece in range(pieces):
            cache = {}

            def cached_x(l1, g2):
                if not small:
                    return load_x(l1 + k1, g2, piece)
                if (l1, g2) not in cache:
                    cache[l1, g2] = load_x(l1 + k1, g2, piece)
                return cache[l1, g2]

            def column_tile(tile, carry):
                zero = jnp.zeros((8, LANES), jnp.float32)

                def first_keep(l1, sums):
                    sums = list(sums)
                    for l2 in range(keep2):
                        start = (l1 * keep2 + l2) * rank + tile * 8
                        s_real = bhat[rows(start), lanes(0, piece)]
                        s_imag = bhat[rows(start), lanes(1, piece)]
                        for k2 in range(span2):
                            x_real, x_imag = cached_x(l1, l2 + k2)
                            real, imag = sums[k2]
                            sums[k2] = (
                                real + (s_real * x_real + s_imag * x_imag),
                                imag + (s_real * x_imag - s_imag * x_real),
                            )
                    return tuple(sums)

                sums = sweep(keep1, first_keep, ((zero, zero),) * span2)
                for k2 in range(span2):
                    for part in range(2):
                        start = (part * span2 + k2) * rank + tile * 8
                        dhat[rows(start), pl.ds(piece * LANES, LANES)] = sums[k2][part]
                return carry

            sweep(tiles, column_tile, 0)
        dhat[...] = wide_dot(dhat[...], window_high[...], window_low[...])
        for piece in range(pieces):

            def rebuild_tile(tile, sums):
                sums = list(sums)
                us = []
                for l2 in range(keep2):
                    start = (a * keep2 + l2) * rank + tile * 8
                    us.append(
                        (
                            uhat[rows(start), lanes(0, piece)],
                            uhat[rows(start), lanes(1, piece)],
                        )
                    )
                for k2 in range(span2):
                    d_real = dhat[rows(k2 * rank + tile * 8), pl.ds(piece * LANES, LANES)]
                    d_imag = dhat[
                        rows((span2 + k2) * rank + tile * 8), pl.ds(piece * LANES, LANES)
                    ]
                    for l2 in range(keep2):
                        u_real, u_imag = us[l2]
                        real, imag = sums[l2 + k2]
                        sums[l2 + k2] = (
                            real + (u_real * d_real - u_imag * d_imag),
                            imag + (u_real * d_imag + u_imag * d_real),
                        )
                return tuple(sums)

            zero = jnp.zeros((8, LANES), jnp.float32)
            sums = sweep(tiles, rebuild_tile, ((zero, zero),) * second)
            for part in range(2):
                summed = jnp.concatenate(
                    [jnp.sum(sums[g2][part], 0, keepdims=True) for g2 in range(second)], 0
                )
                place = pl.ds(piece * LANES, LANES)
                where = pl.ds(part * second, second)
                ghat[where, place] = ghat[where, place] + summed * valid
        return carry

    sweep(keep1, own_pair, 0)

    both = wide_dot(ghat[...], back_high[...], back_low[...])
    real = both[:second, :half] - both[second:, half:]
    imag = both[:second, half:] + both[second:, :half]
    weight = weight_ref[pl.ds(pl.multiple_of(own * second, 8), second), :]
    real = real * weight
    imag = imag * weight
    for piece in range(pieces):
        out_ref[:, piece, :] = real[:, piece * LANES : (piece + 1) * LANES]
        out_ref[:, pieces + piece, :] = imag[:, piece * LANES : (piece + 1) * LANES]


def synthesis_kernel(cells_ref, table_ref, out_ref, out, sems):
    parts = [
        jnp.concatenate([cells_ref[:, part * PIECES + piece, :] for piece in range(PIECES)], 1)
        for part in range(2)
    ]
    high, low = split(jnp.concatenate(parts, 0))
    stacked = jnp.concatenate([high, low, high], 0)
    contract = (((0,), (0,)), ((), ()))
    chunks, width, _ = out.shape
    copies = []
    for i in range(chunks):
        out[i] = lax.dot_general(
            stacked[:, i * width : (i + 1) * width],
            table_ref[...],
            contract,
            preferred_element_type=jnp.float32,
        )
        copies.append(
            pltpu.make_async_copy(out.at[i], out_ref.at[pl.ds(i * width, width)], sems.at[i])
        )
        copies[-1].start()
    for copy in copies:
        copy.wait()


def per_device(traces, mask, omega):
    narrow_count = lax.axis_size("narrow")
    wide_count = lax.axis_size("wide")
    assert traces.shape[:2] == (1, 1)
    first, second = narrow_count, wide_count
    freq_total = FREQ_DEV * wide_count
    keep1, keep2 = first // 2, second // 2
    span1, span2 = first - keep1 + 1, second - keep2 + 1
    rank = omega.shape[0] * narrow_count
    dests = wide_count * narrow_count
    lines = 2 * PIECES

    omegas = [omega]
    for step in range(1, narrow_count):
        ring = [(i, (i + step) % narrow_count) for i in range(narrow_count)]
        omegas.append(lax.ppermute(omega, "narrow", ring))

    high, low = halves(spectrum_table(freq_total, narrow_count))
    blocks = pl.pallas_call(
        spectrum_kernel,
        out_shape=jax.ShapeDtypeStruct((dests, lines, LANES), jnp.float32),
        in_specs=[HBM] * 3,
        out_specs=VMEM,
        scratch_shapes=[
            pltpu.VMEM((CHUNKS, CELLS, S // CHUNKS), jnp.float32),
            pltpu.VMEM((1, CELLS), jnp.int32),
            pltpu.VMEM((4 * dests, S), jnp.bfloat16),
            pltpu.SemaphoreType.DMA((2 + CHUNKS,)),
        ],
        name="spectrum",
    )(traces.reshape(CELLS, S), mask.reshape(1, CELLS), np.concatenate([high, low], 0))
    grid = lax.all_to_all(blocks, ("wide", "narrow"), split_axis=0, concat_axis=0, tiled=True)

    if omega.shape[0] % 8:
        omegas = [jnp.concatenate(omegas, 0)]
    columns = span1 * span2
    omega_hat = pl.pallas_call(
        functools.partial(omega_kernel, columns),
        out_shape=jax.ShapeDtypeStruct((columns * rank, 2 * CELLS), jnp.float32),
        in_specs=[VMEM] * (len(omegas) + 2),
        out_specs=VMEM,
        cost_estimate=pl.CostEstimate(
            flops=6 * columns * rank * LANES * 2 * CELLS,
            bytes_accessed=4 * columns * rank * 2 * CELLS,
            transcendentals=0,
        ),
        compiler_params=pltpu.CompilerParams(vmem_limit_bytes=16 * MIB),
        name="omega",
    )(*omegas, *halves(omega_table()))

    angles = centred_angles()
    counts = (
        correlation(first, keep1)[:, None, None]
        * correlation(second, keep2)[None, :, None]
        * np.outer(correlation(G3, KEEP3), correlation(G4, KEEP4)).reshape(1, 1, CELLS)
    ).reshape(first * second, CELLS)
    forward = np.concatenate([np.cos(angles), np.sin(angles)], 1)
    backward = np.concatenate([np.cos(angles.T), np.sin(angles.T)], 1) / CELLS
    tables = (
        *halves(forward),
        *halves(sketch_table()),
        *halves(basis_table()),
        *halves(window_table()),
        *halves(backward),
        (1.0 / counts).astype(np.float32),
    )
    area = keep1 * keep2 * rank
    scratch = [
        (first * second, lines, 8, LANES),
        (area, 2 * CELLS),
        (area, 2 * CELLS),
        (area, 2 * CELLS),
        (2 * span2 * rank, CELLS),
        (2 * second, CELLS),
    ]
    rebuilt = pl.pallas_call(
        functools.partial(core_kernel, (first, second, rank)),
        out_shape=jax.ShapeDtypeStruct((second, lines, LANES), jnp.float32),
        in_specs=[VMEM] * (2 + len(tables)),
        out_specs=VMEM,
        scratch_shapes=[pltpu.VMEM(shape, jnp.float32) for shape in scratch],
        compiler_params=pltpu.CompilerParams(vmem_limit_bytes=24 * MIB),
        name="core",
    )(grid, omega_hat, *tables)
    returned = lax.all_to_all(rebuilt, "wide", split_axis=0, concat_axis=0, tiled=True)

    high, low = halves(synthesis_table(freq_total))
    filtered = pl.pallas_call(
        synthesis_kernel,
        out_shape=jax.ShapeDtypeStruct((CELLS, S), jnp.float32),
        in_specs=[VMEM] * 2,
        out_specs=HBM,
        scratch_shapes=[
            pltpu.VMEM((PIECES, LANES, S), jnp.float32),
            pltpu.SemaphoreType.DMA((PIECES,)),
        ],
        compiler_params=pltpu.CompilerParams(vmem_limit_bytes=8 * MIB),
        name="synthesis",
    )(returned, np.concatenate([high, high, low], 0))
    return filtered.reshape(traces.shape)


def solution(mesh):
    return jax.shard_map(
        per_device,
        mesh=mesh,
        in_specs=(
            P(("win", "narrow"), "wide", None, None),
            P(("win", "narrow"), "wide", None),
            P("narrow", None),
        ),
        out_specs=P(("win", "narrow"), "wide", None, None),
        check_vma=False,
    )
```

```python
import functools
import math

import jax
import jax.numpy as jnp
import ml_dtypes
import numpy as np
from jax import lax
from jax.experimental import pallas as pl
from jax.experimental.pallas import tpu as pltpu
from jax.sharding import PartitionSpec as P

G3 = 16
G4 = 16
S = 1024
FREQ_DEV = 1
FIRST_BIN = 16
LANES = 128
MIB = 1 << 20
CHUNKS = 4
PIVOTS = 4
CELLS = G3 * G4
KEEP3, KEEP4 = G3 // 2, G4 // 2
SPAN3, SPAN4 = G3 - KEEP3 + 1, G4 - KEEP4 + 1
SHIFT3, SHIFT4 = (SPAN3 - 1) // 2, (SPAN4 - 1) // 2
ROWS = KEEP3 * KEEP4
COLS = SPAN3 * SPAN4
PIECES = CELLS // LANES

HBM = pl.BlockSpec(memory_space=pltpu.HBM)
VMEM = pl.BlockSpec(memory_space=pltpu.VMEM)
highest = lax.Precision.HIGHEST


def halves(table):
    table = np.asarray(table, np.float32)
    high = table.astype(ml_dtypes.bfloat16)
    low = (table - high.astype(np.float32)).astype(ml_dtypes.bfloat16)
    return high, low


def phases(freq_total):
    bins = FIRST_BIN + np.arange(freq_total)
    return 2.0 * np.pi * ((bins[:, None] * np.arange(S)[None, :]) % S) / S


def cell_angles(positions3, positions4):
    wave = np.arange(CELLS)
    turns = (
        np.outer(positions3, wave // G4) % G3 / G3 + np.outer(positions4, wave % G4) % G4 / G4
    )
    return 2.0 * np.pi * turns


def correlation(length, keep_size):
    position = np.arange(length)
    span_size = length - keep_size + 1
    return (
        np.minimum(position, keep_size - 1) - np.maximum(position - span_size + 1, 0) + 1
    ).astype(np.float64)


def spectrum_table(freq_total, copies):
    angles = np.repeat(phases(freq_total), copies, 0)
    return np.concatenate([np.cos(angles), -np.sin(angles)], 0) / math.sqrt(S)


def synthesis_table(freq_total):
    angles = phases(freq_total)
    return np.concatenate([np.cos(angles), -np.sin(angles)], 0) * math.sqrt(2.0 / freq_total)


def centred_angles():
    cell = np.arange(CELLS)
    return cell_angles(cell // G4 - SHIFT3, cell % G4 - SHIFT4)


def omega_table():
    column = np.arange(COLS)
    angles = cell_angles(column // SPAN4, column % SPAN4)
    table = np.zeros((LANES, 2 * CELLS))
    table[:COLS] = np.concatenate([np.cos(angles), -np.sin(angles)], 1)
    return table


def sketch_table():
    row = np.arange(ROWS)
    angles = cell_angles(row // KEEP4 - SHIFT3, row % KEEP4 - SHIFT4).T
    real, imag = np.cos(angles) / CELLS, np.sin(angles) / CELLS
    from_real = np.concatenate([real, imag, imag, -real], 1)
    from_imag = np.concatenate([-imag, real, real, imag], 1)
    return np.concatenate([from_real, from_imag], 0)


def basis_table():
    row = np.arange(ROWS)
    angles = cell_angles(row // KEEP4, row % KEEP4)
    real, imag = np.cos(angles), np.sin(angles)
    return np.concatenate(
        [np.concatenate([real, -imag], 1), np.concatenate([imag, real], 1)], 0
    )


def window_table():
    parts = []
    for length, shift in ((G3, SHIFT3), (G4, SHIFT4)):
        wave = np.arange(length)
        turns = (wave[:, None] - wave[None, :])[:, :, None] * np.arange(-shift, shift + 1) / length
        parts.append(np.cos(2.0 * np.pi * turns).sum(-1) / length)
    return np.kron(parts[0], parts[1])


def split(value):
    high = value.astype(jnp.bfloat16)
    low = (value - high.astype(jnp.float32)).astype(jnp.bfloat16)
    return high, low


def dot(left, right):
    return jnp.dot(left, right, preferred_element_type=jnp.float32)


def wide_dot(value, high, low):
    rows = value.shape[0]
    value_high, value_low = split(value)
    main = dot(jnp.concatenate([value_high, value_low], 0), high)
    return main[:rows] + (main[rows:] + dot(value_high, low))


def spectrum_kernel(traces_ref, mask_ref, table_ref, out_ref, traces, mask, table, sems):
    rows = table.shape[0] // 2
    dests = rows // 2
    chunks, _, width = traces.shape
    copies = [
        pltpu.make_async_copy(table_ref, table, sems.at[0]),
        pltpu.make_async_copy(mask_ref, mask, sems.at[1]),
    ] + [
        pltpu.make_async_copy(
            traces_ref.at[:, pl.ds(i * width, width)], traces.at[i], sems.at[2 + i]
        )
        for i in range(chunks)
    ]
    for copy in copies:
        copy.start()
    copies[0].wait()
    contract = (((1,), (1,)), ((), ()))
    total = jnp.zeros((2 * rows, CELLS), jnp.float32)
    rest = jnp.zeros((rows, CELLS), jnp.float32)
    for i in range(chunks):
        copies[2 + i].wait()
        high, low = split(traces[i])
        place = pl.ds(i * width, width)
        total += lax.dot_general(
            table[:, place], high, contract, preferred_element_type=jnp.float32
        )
        rest += lax.dot_general(
            table[:rows, place], low, contract, preferred_element_type=jnp.float32
        )
    copies[1].wait()
    result = (total[:rows] + (total[rows:] + rest)) * mask[...].astype(jnp.float32)
    for part in range(2):
        for piece in range(PIECES):
            out_ref[:, part * PIECES + piece, :] = result[
                part * dests : (part + 1) * dests, piece * LANES : (piece + 1) * LANES
            ]


def omega_kernel(columns, *refs):
    omega_refs = refs[:-3]
    high_ref, low_ref, out_ref = refs[-3:]
    omega = jnp.concatenate([ref[...] for ref in omega_refs], 0)
    pad = jnp.zeros((omega.shape[0], LANES - COLS), jnp.float32)
    blocks = [
        jnp.concatenate([omega[:, k * COLS : (k + 1) * COLS], pad], 1) for k in range(columns)
    ]
    out_ref[...] = wide_dot(jnp.concatenate(blocks, 0), high_ref[...], low_ref[...])


def minus_product(value, left, right):
    return (
        value[0] - (left[0] * right[0] - left[1] * right[1]),
        value[1] - (left[0] * right[1] + left[1] * right[0]),
    )


def invert(gram_real, gram_imag, result):
    size = gram_real.shape[0]
    width = 2 * size
    row_index = lax.broadcasted_iota(jnp.int32, (size, size), 0)
    column_index = lax.broadcasted_iota(jnp.int32, (size, size), 1)
    identity = (row_index == column_index).astype(jnp.float32)
    real = jnp.concatenate([gram_real, identity], 1)
    imag = jnp.concatenate([gram_imag, jnp.zeros_like(identity)], 1)
    tiles = [(real[t : t + 8], imag[t : t + 8]) for t in range(0, size, 8)]
    sublane = lax.broadcasted_iota(jnp.int32, (8, width), 0)
    for start in range(0, size, PIVOTS):
        home, at = start // 8, start % 8
        columns = [
            [
                tuple(jnp.broadcast_to(v[:, start + b : start + b + 1], (8, width)) for v in tile)
                for b in range(PIVOTS)
            ]
            for tile in tiles
        ]
        rows = [tuple(v[at + a : at + a + 1] for v in tiles[home]) for a in range(PIVOTS)]
        block = {
            (a, b): tuple(
                jnp.broadcast_to(v[:, start + b : start + b + 1], (1, width)) for v in rows[a]
            )
            for a in range(PIVOTS)
            for b in range(PIVOTS)
        }
        for p in range(PIVOTS):
            scale = 1.0 / block[p, p][0]
            rows[p] = tuple(v * scale for v in rows[p])
            for b in range(p + 1, PIVOTS):
                block[p, b] = tuple(v * scale for v in block[p, b])
            for a in range(PIVOTS):
                if a == p:
                    continue
                rows[a] = minus_product(rows[a], block[a, p], rows[p])
                for b in range(p + 1, PIVOTS):
                    block[a, b] = minus_product(block[a, b], block[a, p], block[p, b])
        for t in range(len(tiles)):
            tile = tiles[t]
            for b in range(PIVOTS):
                tile = minus_product(tile, columns[t][b], rows[b])
            if t == home:
                for b in range(PIVOTS):
                    here = sublane == at + b
                    tile = tuple(jnp.where(here, rows[b][k], tile[k]) for k in range(2))
            tiles[t] = tile
        yield
    for part in range(2):
        result.append(jnp.concatenate([tile[part] for tile in tiles], 0)[:, size:])


def interleave(*steps):
    steps = list(steps)
    while steps:
        steps = [step for step in steps if next(step, steps) is not steps]


def core_kernel(
    dims,
    x_ref,
    omega_ref,
    analysis_high,
    analysis_low,
    sketch_high,
    sketch_low,
    basis_high,
    basis_low,
    window_high,
    window_low,
    back_high,
    back_low,
    weight_ref,
    out_ref,
    xhat,
    shat,
    bhat,
    uhat,
    dhat,
    ghat,
):
    first, second, rank = dims
    keep1, keep2 = first // 2, second // 2
    span1, span2 = first - keep1 + 1, second - keep2 + 1
    own = lax.axis_index("narrow")
    half = CELLS
    tiles = rank // 8
    pieces = CELLS // LANES
    small = keep1 * keep2 * span1 * span2 <= 64

    def sweep(count, body, carry):
        if small:
            for i in range(count):
                carry = body(i, carry)
            return carry
        return lax.fori_loop(0, count, body, carry)

    def rows(start, count=8):
        if isinstance(start, int):
            return pl.ds(start, count)
        return pl.ds(pl.multiple_of(start, 8), count)

    def lanes(part, piece):
        start = part * half + piece * LANES
        return pl.ds(start, LANES)

    planes = first * second
    spectrum = jnp.concatenate(
        [
            jnp.concatenate([x_ref[:, part * pieces + piece, :] for piece in range(pieces)], 1)
            for part in range(2)
        ],
        0,
    )
    both = wide_dot(spectrum, analysis_high[...], analysis_low[...])
    hats = (
        both[:planes, :half] + both[planes:, half:],
        both[planes:, :half] - both[:planes, half:],
    )
    for part in range(2):
        for piece in range(pieces):
            values = hats[part][:, piece * LANES : (piece + 1) * LANES]
            xhat[:, part * pieces + piece] = jnp.broadcast_to(
                values[:, None, :], (planes, 8, LANES)
            )

    def load_x(g1, g2, piece):
        row = g2 * first + g1
        return xhat[row, piece], xhat[row, pieces + piece]

    for piece in range(pieces):
        cache = {}

        def cached_x(g1, g2):
            if not small:
                return load_x(g1, g2, piece)
            if (g1, g2) not in cache:
                cache[g1, g2] = load_x(g1, g2, piece)
            return cache[g1, g2]

        def sketch_tile(tile, carry):
            def first_keep(l1, carry):
                zero = jnp.zeros((8, LANES), jnp.float32)

                def columns(k1, sums):
                    def column(k2, sums):
                        start = (k1 * span2 + k2) * rank + tile * 8
                        w_real = omega_ref[rows(start), lanes(0, piece)]
                        w_imag = omega_ref[rows(start), lanes(1, piece)]
                        sums = list(sums)
                        for l2 in range(keep2):
                            x_real, x_imag = cached_x(l1 + k1, l2 + k2)
                            real, imag = sums[l2]
                            sums[l2] = (
                                real + (x_real * w_real + x_imag * w_imag),
                                imag + (x_imag * w_real - x_real * w_imag),
                            )
                        return tuple(sums)

                    return sweep(span2, column, sums)

                sums = sweep(span1, columns, ((zero, zero),) * keep2)
                for l2 in range(keep2):
                    start = (l1 * keep2 + l2) * rank + tile * 8
                    shat[rows(start), lanes(0, piece)] = sums[l2][0]
                    shat[rows(start), lanes(1, piece)] = sums[l2][1]
                return carry

            return sweep(keep1, first_keep, carry)

        sweep(tiles, sketch_tile, 0)

    blocks = keep1 * keep2
    sketch = wide_dot(shat[...], sketch_high[...], sketch_low[...])
    straight = jnp.concatenate(
        [sketch[b * rank : (b + 1) * rank, : 2 * ROWS] for b in range(blocks)], 1
    )
    turned = jnp.concatenate(
        [sketch[b * rank : (b + 1) * rank, 2 * ROWS :] for b in range(blocks)], 1
    )
    contract = (((1,), (1,)), ((), ()))
    gram_real = lax.dot_general(
        straight, straight, contract, precision=highest, preferred_element_type=jnp.float32
    )
    gram_imag = lax.dot_general(
        straight, turned, contract, precision=highest, preferred_element_type=jnp.float32
    )
    def partner(a):
        k1 = own - a
        valid = jnp.logical_and(k1 >= 0, k1 < span1).astype(jnp.float32)
        return jnp.clip(k1, 0, span1 - 1), valid

    def own_columns(a):
        k1, _ = partner(a)
        for piece in range(pieces):
            cache = {}

            def cached_x(l1, g2):
                if not small:
                    return load_x(l1 + k1, g2, piece)
                if (l1, g2) not in cache:
                    cache[l1, g2] = load_x(l1 + k1, g2, piece)
                return cache[l1, g2]

            def column_tile(tile, carry):
                zero = jnp.zeros((8, LANES), jnp.float32)

                def first_keep(l1, sums):
                    sums = list(sums)
                    for l2 in range(keep2):
                        start = (l1 * keep2 + l2) * rank + tile * 8
                        s_real = bhat[rows(start), lanes(0, piece)]
                        s_imag = bhat[rows(start), lanes(1, piece)]
                        for k2 in range(span2):
                            x_real, x_imag = cached_x(l1, l2 + k2)
                            real, imag = sums[k2]
                            sums[k2] = (
                                real + (s_real * x_real + s_imag * x_imag),
                                imag + (s_real * x_imag - s_imag * x_real),
                            )
                    return tuple(sums)

                sums = sweep(keep1, first_keep, ((zero, zero),) * span2)
                for k2 in range(span2):
                    for part in range(2):
                        start = (part * span2 + k2) * rank + tile * 8
                        dhat[rows(start), pl.ds(piece * LANES, LANES)] = sums[k2][part]
                return carry

            if small:
                for tile in range(tiles):
                    column_tile(tile, 0)
                    yield
            else:
                sweep(tiles, column_tile, 0)
        dhat[...] = wide_dot(dhat[...], window_high[...], window_low[...])
        yield

    def own_planes(a):
        _, valid = partner(a)
        for piece in range(pieces):

            def rebuild_tile(tile, sums):
                sums = list(sums)
                us = []
                for l2 in range(keep2):
                    start = (a * keep2 + l2) * rank + tile * 8
                    us.append(
                        (
                            uhat[rows(start), lanes(0, piece)],
                            uhat[rows(start), lanes(1, piece)],
                        )
                    )
                for k2 in range(span2):
                    d_real = dhat[rows(k2 * rank + tile * 8), pl.ds(piece * LANES, LANES)]
                    d_imag = dhat[
                        rows((span2 + k2) * rank + tile * 8), pl.ds(piece * LANES, LANES)
                    ]
                    for l2 in range(keep2):
                        u_real, u_imag = us[l2]
                        real, imag = sums[l2 + k2]
                        sums[l2 + k2] = (
                            real + (u_real * d_real - u_imag * d_imag),
                            imag + (u_real * d_imag + u_imag * d_real),
                        )
                return tuple(sums)

            zero = jnp.zeros((8, LANES), jnp.float32)
            sums = sweep(tiles, rebuild_tile, ((zero, zero),) * second)
            for part in range(2):
                summed = jnp.concatenate(
                    [jnp.sum(sums[g2][part], 0, keepdims=True) for g2 in range(second)], 0
                )
                place = pl.ds(piece * LANES, LANES)
                where = pl.ds(part * second, second)
                ghat[where, place] = ghat[where, place] + summed * valid

    def own_basis():
        bhat[...] = wide_dot(sketch[:, : 2 * ROWS], basis_high[...], basis_low[...])
        yield
        if small:
            yield from own_columns(0)

    inverse = []
    interleave(invert(gram_real, gram_imag, inverse), own_basis())
    mixer = jnp.concatenate(inverse, 1)

    def mix(b, carry):
        real = bhat[rows(b * rank, rank), :half]
        imag = bhat[rows(b * rank, rank), half:]
        uhat[rows(b * rank, rank), :half] = jnp.dot(
            mixer,
            jnp.concatenate([real, imag], 0),
            precision=highest,
            preferred_element_type=jnp.float32,
        )
        uhat[rows(b * rank, rank), half:] = jnp.dot(
            mixer,
            jnp.concatenate([imag, -real], 0),
            precision=highest,
            preferred_element_type=jnp.float32,
        )
        return carry

    sweep(blocks, mix, 0)
    ghat[...] = jnp.zeros_like(ghat)

    def own_pair(a, carry):
        if not (small and isinstance(a, int) and a == 0):
            for _ in own_columns(a):
                pass
        own_planes(a)
        return carry

    sweep(keep1, own_pair, 0)

    both = wide_dot(ghat[...], back_high[...], back_low[...])
    real = both[:second, :half] - both[second:, half:]
    imag = both[:second, half:] + both[second:, :half]
    weight = weight_ref[pl.ds(pl.multiple_of(own * second, 8), second), :]
    real = real * weight
    imag = imag * weight
    for piece in range(pieces):
        out_ref[:, piece, :] = real[:, piece * LANES : (piece + 1) * LANES]
        out_ref[:, pieces + piece, :] = imag[:, piece * LANES : (piece + 1) * LANES]


def synthesis_kernel(cells_ref, table_ref, out_ref, out, sems):
    parts = [
        jnp.concatenate([cells_ref[:, part * PIECES + piece, :] for piece in range(PIECES)], 1)
        for part in range(2)
    ]
    high, low = split(jnp.concatenate(parts, 0))
    stacked = jnp.concatenate([high, low, high], 0)
    contract = (((0,), (0,)), ((), ()))
    chunks, width, _ = out.shape
    copies = []
    for i in range(chunks):
        out[i] = lax.dot_general(
            stacked[:, i * width : (i + 1) * width],
            table_ref[...],
            contract,
            preferred_element_type=jnp.float32,
        )
        copies.append(
            pltpu.make_async_copy(out.at[i], out_ref.at[pl.ds(i * width, width)], sems.at[i])
        )
        copies[-1].start()
    for copy in copies:
        copy.wait()


def per_device(traces, mask, omega):
    narrow_count = lax.axis_size("narrow")
    wide_count = lax.axis_size("wide")
    assert traces.shape[:2] == (1, 1)
    first, second = narrow_count, wide_count
    freq_total = FREQ_DEV * wide_count
    keep1, keep2 = first // 2, second // 2
    span1, span2 = first - keep1 + 1, second - keep2 + 1
    rank = omega.shape[0] * narrow_count
    dests = wide_count * narrow_count
    lines = 2 * PIECES

    omegas = [omega]
    for step in range(1, narrow_count):
        ring = [(i, (i + step) % narrow_count) for i in range(narrow_count)]
        omegas.append(lax.ppermute(omega, "narrow", ring))

    high, low = halves(spectrum_table(freq_total, narrow_count))
    blocks = pl.pallas_call(
        spectrum_kernel,
        out_shape=jax.ShapeDtypeStruct((dests, lines, LANES), jnp.float32),
        in_specs=[HBM] * 3,
        out_specs=VMEM,
        scratch_shapes=[
            pltpu.VMEM((CHUNKS, CELLS, S // CHUNKS), jnp.float32),
            pltpu.VMEM((1, CELLS), jnp.int32),
            pltpu.VMEM((4 * dests, S), jnp.bfloat16),
            pltpu.SemaphoreType.DMA((2 + CHUNKS,)),
        ],
        name="spectrum",
    )(traces.reshape(CELLS, S), mask.reshape(1, CELLS), np.concatenate([high, low], 0))
    grid = lax.all_to_all(blocks, ("wide", "narrow"), split_axis=0, concat_axis=0, tiled=True)

    if omega.shape[0] % 8:
        omegas = [jnp.concatenate(omegas, 0)]
    columns = span1 * span2
    omega_hat = pl.pallas_call(
        functools.partial(omega_kernel, columns),
        out_shape=jax.ShapeDtypeStruct((columns * rank, 2 * CELLS), jnp.float32),
        in_specs=[VMEM] * (len(omegas) + 2),
        out_specs=VMEM,
        cost_estimate=pl.CostEstimate(
            flops=6 * columns * rank * LANES * 2 * CELLS,
            bytes_accessed=4 * columns * rank * 2 * CELLS,
            transcendentals=0,
        ),
        compiler_params=pltpu.CompilerParams(vmem_limit_bytes=16 * MIB),
        name="omega",
    )(*omegas, *halves(omega_table()))

    angles = centred_angles()
    counts = (
        correlation(first, keep1)[:, None, None]
        * correlation(second, keep2)[None, :, None]
        * np.outer(correlation(G3, KEEP3), correlation(G4, KEEP4)).reshape(1, 1, CELLS)
    ).reshape(first * second, CELLS)
    forward = np.concatenate([np.cos(angles), np.sin(angles)], 1)
    backward = np.concatenate([np.cos(angles.T), np.sin(angles.T)], 1) / CELLS
    tables = (
        *halves(forward),
        *halves(sketch_table()),
        *halves(basis_table()),
        *halves(window_table()),
        *halves(backward),
        (1.0 / counts).astype(np.float32),
    )
    area = keep1 * keep2 * rank
    scratch = [
        (first * second, lines, 8, LANES),
        (area, 2 * CELLS),
        (area, 2 * CELLS),
        (area, 2 * CELLS),
        (2 * span2 * rank, CELLS),
        (2 * second, CELLS),
    ]
    rebuilt = pl.pallas_call(
        functools.partial(core_kernel, (first, second, rank)),
        out_shape=jax.ShapeDtypeStruct((second, lines, LANES), jnp.float32),
        in_specs=[VMEM] * (2 + len(tables)),
        out_specs=VMEM,
        scratch_shapes=[pltpu.VMEM(shape, jnp.float32) for shape in scratch],
        compiler_params=pltpu.CompilerParams(vmem_limit_bytes=24 * MIB),
        name="core",
    )(grid, omega_hat, *tables)
    returned = lax.all_to_all(rebuilt, "wide", split_axis=0, concat_axis=0, tiled=True)

    high, low = halves(synthesis_table(freq_total))
    filtered = pl.pallas_call(
        synthesis_kernel,
        out_shape=jax.ShapeDtypeStruct((CELLS, S), jnp.float32),
        in_specs=[VMEM] * 2,
        out_specs=HBM,
        scratch_shapes=[
            pltpu.VMEM((PIECES, LANES, S), jnp.float32),
            pltpu.SemaphoreType.DMA((PIECES,)),
        ],
        compiler_params=pltpu.CompilerParams(vmem_limit_bytes=8 * MIB),
        name="synthesis",
    )(returned, np.concatenate([high, high, low], 0))
    return filtered.reshape(traces.shape)


def solution(mesh):
    return jax.shard_map(
        per_device,
        mesh=mesh,
        in_specs=(
            P(("win", "narrow"), "wide", None, None),
            P(("win", "narrow"), "wide", None),
            P("narrow", None),
        ),
        out_specs=P(("win", "narrow"), "wide", None, None),
        check_vma=False,
    )
```

```python
import functools
import math

import jax
import jax.numpy as jnp
import ml_dtypes
import numpy as np
from jax import lax
from jax.experimental import pallas as pl
from jax.experimental.pallas import tpu as pltpu
from jax.sharding import PartitionSpec as P

G3 = 16
G4 = 16
S = 1024
FREQ_DEV = 1
FIRST_BIN = 16
LANES = 128
MIB = 1 << 20
CHUNKS = 2
PIVOTS = 4
CELLS = G3 * G4
KEEP3, KEEP4 = G3 // 2, G4 // 2
SPAN3, SPAN4 = G3 - KEEP3 + 1, G4 - KEEP4 + 1
SHIFT3, SHIFT4 = (SPAN3 - 1) // 2, (SPAN4 - 1) // 2
ROWS = KEEP3 * KEEP4
COLS = SPAN3 * SPAN4
PIECES = CELLS // LANES

HBM = pl.BlockSpec(memory_space=pltpu.HBM)
VMEM = pl.BlockSpec(memory_space=pltpu.VMEM)
highest = lax.Precision.HIGHEST


def halves(table):
    table = np.asarray(table, np.float32)
    high = table.astype(ml_dtypes.bfloat16)
    low = (table - high.astype(np.float32)).astype(ml_dtypes.bfloat16)
    return high, low


def phases(freq_total):
    bins = FIRST_BIN + np.arange(freq_total)
    return 2.0 * np.pi * ((bins[:, None] * np.arange(S)[None, :]) % S) / S


def cell_angles(positions3, positions4):
    wave = np.arange(CELLS)
    turns = (
        np.outer(positions3, wave // G4) % G3 / G3 + np.outer(positions4, wave % G4) % G4 / G4
    )
    return 2.0 * np.pi * turns


def correlation(length, keep_size):
    position = np.arange(length)
    span_size = length - keep_size + 1
    return (
        np.minimum(position, keep_size - 1) - np.maximum(position - span_size + 1, 0) + 1
    ).astype(np.float64)


def spectrum_table(freq_total, copies):
    angles = np.repeat(phases(freq_total), copies, 0)
    return np.concatenate([np.cos(angles), -np.sin(angles)], 0) / math.sqrt(S)


def synthesis_table(freq_total):
    angles = phases(freq_total)
    return np.concatenate([np.cos(angles), -np.sin(angles)], 0) * math.sqrt(2.0 / freq_total)


def centred_angles():
    cell = np.arange(CELLS)
    return cell_angles(cell // G4 - SHIFT3, cell % G4 - SHIFT4)


def omega_table():
    column = np.arange(COLS)
    angles = cell_angles(column // SPAN4, column % SPAN4)
    table = np.zeros((LANES, 2 * CELLS))
    table[:COLS] = np.concatenate([np.cos(angles), -np.sin(angles)], 1)
    return table


def sketch_table():
    row = np.arange(ROWS)
    angles = cell_angles(row // KEEP4 - SHIFT3, row % KEEP4 - SHIFT4).T
    real, imag = np.cos(angles) / CELLS, np.sin(angles) / CELLS
    from_real = np.concatenate([real, imag, imag, -real], 1)
    from_imag = np.concatenate([-imag, real, real, imag], 1)
    return np.concatenate([from_real, from_imag], 0)


def basis_table():
    row = np.arange(ROWS)
    angles = cell_angles(row // KEEP4, row % KEEP4)
    real, imag = np.cos(angles), np.sin(angles)
    return np.concatenate(
        [np.concatenate([real, -imag], 1), np.concatenate([imag, real], 1)], 0
    )


def window_table():
    parts = []
    for length, shift in ((G3, SHIFT3), (G4, SHIFT4)):
        wave = np.arange(length)
        turns = (wave[:, None] - wave[None, :])[:, :, None] * np.arange(-shift, shift + 1) / length
        parts.append(np.cos(2.0 * np.pi * turns).sum(-1) / length)
    return np.kron(parts[0], parts[1])


def split(value):
    high = value.astype(jnp.bfloat16)
    low = (value - high.astype(jnp.float32)).astype(jnp.bfloat16)
    return high, low


def dot(left, right):
    return jnp.dot(left, right, preferred_element_type=jnp.float32)


def wide_dot(value, high, low):
    rows = value.shape[0]
    value_high, value_low = split(value)
    main = dot(jnp.concatenate([value_high, value_low], 0), high)
    return main[:rows] + (main[rows:] + dot(value_high, low))


def spectrum_kernel(traces_ref, mask_ref, table_ref, out_ref, traces, mask, table, sems):
    rows = table.shape[0] // 2
    dests = rows // 2
    chunks, _, width = traces.shape
    copies = [
        pltpu.make_async_copy(table_ref, table, sems.at[0]),
        pltpu.make_async_copy(mask_ref, mask, sems.at[1]),
    ] + [
        pltpu.make_async_copy(
            traces_ref.at[:, pl.ds(i * width, width)], traces.at[i], sems.at[2 + i]
        )
        for i in range(chunks)
    ]
    for copy in copies:
        copy.start()
    copies[0].wait()
    contract = (((1,), (1,)), ((), ()))
    total = jnp.zeros((2 * rows, CELLS), jnp.float32)
    rest = jnp.zeros((rows, CELLS), jnp.float32)
    for i in range(chunks):
        copies[2 + i].wait()
        high, low = split(traces[i])
        place = pl.ds(i * width, width)
        total += lax.dot_general(
            table[:, place], high, contract, preferred_element_type=jnp.float32
        )
        rest += lax.dot_general(
            table[:rows, place], low, contract, preferred_element_type=jnp.float32
        )
    copies[1].wait()
    result = (total[:rows] + (total[rows:] + rest)) * mask[...].astype(jnp.float32)
    for part in range(2):
        for piece in range(PIECES):
            out_ref[:, part * PIECES + piece, :] = result[
                part * dests : (part + 1) * dests, piece * LANES : (piece + 1) * LANES
            ]


def omega_kernel(columns, *refs):
    omega_refs = refs[:-3]
    high_ref, low_ref, out_ref = refs[-3:]
    omega = jnp.concatenate([ref[...] for ref in omega_refs], 0)
    pad = jnp.zeros((omega.shape[0], LANES - COLS), jnp.float32)
    blocks = [
        jnp.concatenate([omega[:, k * COLS : (k + 1) * COLS], pad], 1) for k in range(columns)
    ]
    out_ref[...] = wide_dot(jnp.concatenate(blocks, 0), high_ref[...], low_ref[...])


def minus_product(value, left, right):
    return (
        value[0] - (left[0] * right[0] - left[1] * right[1]),
        value[1] - (left[0] * right[1] + left[1] * right[0]),
    )


def pivot_pair(upper, lower, corner, other, cross, scale):
    turned = (cross[0], -cross[1])
    first = minus_product(tuple(other * v for v in upper), cross, lower)
    second = minus_product(tuple(corner * v for v in lower), turned, upper)
    return tuple(v * scale for v in first), tuple(v * scale for v in second)


def invert(real, imag, result):
    size = real.shape[0]
    width = 2 * size
    tiles = [(real[t : t + 8], imag[t : t + 8]) for t in range(0, size, 8)]
    sublane = lax.broadcasted_iota(jnp.int32, (8, width), 0)
    for start in range(0, size, PIVOTS):
        home, at = start // 8, start % 8
        lane = size + start

        def spread(value, b, height):
            return jnp.broadcast_to(value[:, lane + b : lane + b + 1], (height, width))

        rows = [tuple(v[at + a : at + a + 1] for v in tiles[home]) for a in range(PIVOTS)]
        block = {}
        for a in range(PIVOTS):
            block[a, a] = (spread(rows[a][0], a, 1),)
            for b in range(a + 1, PIVOTS):
                block[a, b] = tuple(spread(v, b, 1) for v in rows[a])
                block[b, a] = (block[a, b][0], -block[a, b][1])
        columns = [
            [tuple(spread(v, b, 8) for v in tile) for b in range(PIVOTS)] for tile in tiles
        ]
        for p in range(0, PIVOTS, 2):
            q = p + 1
            corner, other, cross = block[p, p][0], block[q, q][0], block[p, q]
            scale = 1.0 / (corner * other - (cross[0] * cross[0] + cross[1] * cross[1]))
            pair = (corner, other, cross, scale)
            rows[p], rows[q] = pivot_pair(rows[p], rows[q], *pair)
            later = range(p + 2, PIVOTS)
            done = {}
            for c in later:
                done[p, c], done[q, c] = pivot_pair(block[p, c], block[q, c], *pair)
            for o in range(PIVOTS):
                if o in (p, q):
                    continue
                left, right = block[o, p], block[o, q]
                rows[o] = minus_product(minus_product(rows[o], left, rows[p]), right, rows[q])
                for c in later:
                    if o == c:
                        first, second = done[p, c], done[q, c]
                        value = block[o, o][0]
                        value = value - (left[0] * first[0] - left[1] * first[1])
                        value = value - (right[0] * second[0] - right[1] * second[1])
                        done[o, o] = (value,)
                    elif o < c:
                        value = minus_product(block[o, c], left, done[p, c])
                        done[o, c] = minus_product(value, right, done[q, c])
                        if o > q:
                            done[c, o] = (done[o, c][0], -done[o, c][1])
            block.update(done)
        for t in range(len(tiles)):
            tile = tiles[t]
            for b in range(PIVOTS):
                tile = minus_product(tile, columns[t][b], rows[b])
            if t == home:
                for b in range(PIVOTS):
                    here = sublane == at + b
                    tile = tuple(jnp.where(here, rows[b][k], tile[k]) for k in range(2))
            tiles[t] = tile
        yield
    for part in range(2):
        result.append(jnp.concatenate([tile[part] for tile in tiles], 0)[:, :size])


def interleave(*steps):
    steps = list(steps)
    while steps:
        steps = [step for step in steps if next(step, steps) is not steps]


def core_kernel(
    dims,
    x_ref,
    omega_ref,
    analysis_high,
    analysis_low,
    sketch_high,
    sketch_low,
    basis_high,
    basis_low,
    window_high,
    window_low,
    back_high,
    back_low,
    weight_ref,
    out_ref,
    xhat,
    shat,
    bhat,
    uhat,
    dhat,
    ghat,
):
    first, second, rank = dims
    keep1, keep2 = first // 2, second // 2
    span1, span2 = first - keep1 + 1, second - keep2 + 1
    own = lax.axis_index("narrow")
    half = CELLS
    tiles = rank // 8
    pieces = CELLS // LANES
    small = keep1 * keep2 * span1 * span2 <= 64

    def sweep(count, body, carry):
        if small:
            for i in range(count):
                carry = body(i, carry)
            return carry
        return lax.fori_loop(0, count, body, carry)

    def rows(start, count=8):
        if isinstance(start, int):
            return pl.ds(start, count)
        return pl.ds(pl.multiple_of(start, 8), count)

    def lanes(part, piece):
        start = part * half + piece * LANES
        return pl.ds(start, LANES)

    planes = first * second
    spectrum = jnp.concatenate(
        [
            jnp.concatenate([x_ref[:, part * pieces + piece, :] for piece in range(pieces)], 1)
            for part in range(2)
        ],
        0,
    )
    both = wide_dot(spectrum, analysis_high[...], analysis_low[...])
    hats = (
        both[:planes, :half] + both[planes:, half:],
        both[planes:, :half] - both[:planes, half:],
    )
    for part in range(2):
        for piece in range(pieces):
            values = hats[part][:, piece * LANES : (piece + 1) * LANES]
            xhat[:, part * pieces + piece] = jnp.broadcast_to(
                values[:, None, :], (planes, 8, LANES)
            )

    def load_x(g1, g2, piece):
        row = g2 * first + g1
        return xhat[row, piece], xhat[row, pieces + piece]

    for piece in range(pieces):
        cache = {}

        def cached_x(g1, g2):
            if not small:
                return load_x(g1, g2, piece)
            if (g1, g2) not in cache:
                cache[g1, g2] = load_x(g1, g2, piece)
            return cache[g1, g2]

        def sketch_tile(tile, carry):
            def first_keep(l1, carry):
                zero = jnp.zeros((8, LANES), jnp.float32)

                def columns(k1, sums):
                    def column(k2, sums):
                        start = (k1 * span2 + k2) * rank + tile * 8
                        w_real = omega_ref[rows(start), lanes(0, piece)]
                        w_imag = omega_ref[rows(start), lanes(1, piece)]
                        sums = list(sums)
                        for l2 in range(keep2):
                            x_real, x_imag = cached_x(l1 + k1, l2 + k2)
                            real, imag = sums[l2]
                            sums[l2] = (
                                real + (x_real * w_real + x_imag * w_imag),
                                imag + (x_imag * w_real - x_real * w_imag),
                            )
                        return tuple(sums)

                    return sweep(span2, column, sums)

                sums = sweep(span1, columns, ((zero, zero),) * keep2)
                for l2 in range(keep2):
                    start = (l1 * keep2 + l2) * rank + tile * 8
                    shat[rows(start), lanes(0, piece)] = sums[l2][0]
                    shat[rows(start), lanes(1, piece)] = sums[l2][1]
                return carry

            return sweep(keep1, first_keep, carry)

        sweep(tiles, sketch_tile, 0)

    blocks = keep1 * keep2
    sketch = wide_dot(shat[...], sketch_high[...], sketch_low[...])
    straight = jnp.concatenate(
        [sketch[b * rank : (b + 1) * rank, : 2 * ROWS] for b in range(blocks)], 1
    )
    turned = jnp.concatenate(
        [sketch[b * rank : (b + 1) * rank, 2 * ROWS :] for b in range(blocks)], 1
    )
    contract = (((1,), (1,)), ((), ()))
    space = jnp.zeros_like(straight)

    def gram(right):
        return lax.dot_general(
            straight,
            jnp.concatenate([space, right], 0),
            contract,
            precision=highest,
            preferred_element_type=jnp.float32,
        )

    row_index = lax.broadcasted_iota(jnp.int32, (rank, 2 * rank), 0)
    column_index = lax.broadcasted_iota(jnp.int32, (rank, 2 * rank), 1)
    unit = 1.0 / jnp.max(jnp.abs(spectrum), keepdims=True)
    gram_real = gram(straight) * unit * unit
    gram_imag = gram(turned) * unit * unit
    gram_real = jnp.where(row_index == column_index, 1.0, gram_real)

    def partner(a):
        k1 = own - a
        valid = jnp.logical_and(k1 >= 0, k1 < span1).astype(jnp.float32)
        return jnp.clip(k1, 0, span1 - 1), valid

    def own_columns(a):
        k1, _ = partner(a)
        for piece in range(pieces):
            cache = {}

            def cached_x(l1, g2):
                if not small:
                    return load_x(l1 + k1, g2, piece)
                if (l1, g2) not in cache:
                    cache[l1, g2] = load_x(l1 + k1, g2, piece)
                return cache[l1, g2]

            def column_tile(tile, carry):
                zero = jnp.zeros((8, LANES), jnp.float32)

                def first_keep(l1, sums):
                    sums = list(sums)
                    for l2 in range(keep2):
                        start = (l1 * keep2 + l2) * rank + tile * 8
                        s_real = bhat[rows(start), lanes(0, piece)]
                        s_imag = bhat[rows(start), lanes(1, piece)]
                        for k2 in range(span2):
                            x_real, x_imag = cached_x(l1, l2 + k2)
                            real, imag = sums[k2]
                            sums[k2] = (
                                real + (s_real * x_real + s_imag * x_imag),
                                imag + (s_real * x_imag - s_imag * x_real),
                            )
                    return tuple(sums)

                sums = sweep(keep1, first_keep, ((zero, zero),) * span2)
                for k2 in range(span2):
                    for part in range(2):
                        start = (part * span2 + k2) * rank + tile * 8
                        dhat[rows(start), pl.ds(piece * LANES, LANES)] = sums[k2][part]
                return carry

            if small:
                for tile in range(tiles):
                    column_tile(tile, 0)
                    yield
            else:
                sweep(tiles, column_tile, 0)
        dhat[...] = wide_dot(dhat[...], window_high[...], window_low[...])
        yield

    def own_planes(a):
        _, valid = partner(a)
        for piece in range(pieces):

            def rebuild_tile(tile, sums):
                sums = list(sums)
                us = []
                for l2 in range(keep2):
                    start = (a * keep2 + l2) * rank + tile * 8
                    us.append(
                        (
                            uhat[rows(start), lanes(0, piece)],
                            uhat[rows(start), lanes(1, piece)],
                        )
                    )
                for k2 in range(span2):
                    d_real = dhat[rows(k2 * rank + tile * 8), pl.ds(piece * LANES, LANES)]
                    d_imag = dhat[
                        rows((span2 + k2) * rank + tile * 8), pl.ds(piece * LANES, LANES)
                    ]
                    for l2 in range(keep2):
                        u_real, u_imag = us[l2]
                        real, imag = sums[l2 + k2]
                        sums[l2 + k2] = (
                            real + (u_real * d_real - u_imag * d_imag),
                            imag + (u_real * d_imag + u_imag * d_real),
                        )
                return tuple(sums)

            zero = jnp.zeros((8, LANES), jnp.float32)
            sums = sweep(tiles, rebuild_tile, ((zero, zero),) * second)
            for part in range(2):
                summed = jnp.concatenate(
                    [jnp.sum(sums[g2][part], 0, keepdims=True) for g2 in range(second)], 0
                )
                place = pl.ds(piece * LANES, LANES)
                where = pl.ds(part * second, second)
                ghat[where, place] = ghat[where, place] + summed * valid

    def own_basis():
        bhat[...] = wide_dot(sketch[:, : 2 * ROWS], basis_high[...], basis_low[...])
        yield
        if small:
            yield from own_columns(0)

    inverse = []
    interleave(invert(gram_real, gram_imag, inverse), own_basis())
    mixer = jnp.concatenate(inverse, 0) * unit * unit

    def mix(b, carry):
        where = rows(b * rank, rank)
        both = jnp.dot(
            mixer, bhat[where, :], precision=highest, preferred_element_type=jnp.float32
        )
        uhat[where, :half] = both[:rank, :half] + both[rank:, half:]
        uhat[where, half:] = both[:rank, half:] - both[rank:, :half]
        return carry

    sweep(blocks, mix, 0)
    ghat[...] = jnp.zeros_like(ghat)

    def own_pair(a, carry):
        if not (small and isinstance(a, int) and a == 0):
            for _ in own_columns(a):
                pass
        own_planes(a)
        return carry

    sweep(keep1, own_pair, 0)

    both = wide_dot(ghat[...], back_high[...], back_low[...])
    real = both[:second, :half] - both[second:, half:]
    imag = both[:second, half:] + both[second:, :half]
    weight = weight_ref[pl.ds(pl.multiple_of(own * second, 8), second), :]
    real = real * weight
    imag = imag * weight
    for piece in range(pieces):
        out_ref[:, piece, :] = real[:, piece * LANES : (piece + 1) * LANES]
        out_ref[:, pieces + piece, :] = imag[:, piece * LANES : (piece + 1) * LANES]


def synthesis_kernel(cells_ref, table_ref, out_ref, out, sems):
    parts = [
        jnp.concatenate([cells_ref[:, part * PIECES + piece, :] for piece in range(PIECES)], 1)
        for part in range(2)
    ]
    high, low = split(jnp.concatenate(parts, 0))
    stacked = jnp.concatenate([high, low, high], 0)
    contract = (((0,), (0,)), ((), ()))
    chunks, width, _ = out.shape
    copies = []
    for i in range(chunks):
        out[i] = lax.dot_general(
            stacked[:, i * width : (i + 1) * width],
            table_ref[...],
            contract,
            preferred_element_type=jnp.float32,
        )
        copies.append(
            pltpu.make_async_copy(out.at[i], out_ref.at[pl.ds(i * width, width)], sems.at[i])
        )
        copies[-1].start()
    for copy in copies:
        copy.wait()


def per_device(traces, mask, omega):
    narrow_count = lax.axis_size("narrow")
    wide_count = lax.axis_size("wide")
    assert traces.shape[:2] == (1, 1)
    first, second = narrow_count, wide_count
    freq_total = FREQ_DEV * wide_count
    keep1, keep2 = first // 2, second // 2
    span1, span2 = first - keep1 + 1, second - keep2 + 1
    rank = omega.shape[0] * narrow_count
    dests = wide_count * narrow_count
    lines = 2 * PIECES

    omegas = [omega]
    for step in range(1, narrow_count):
        ring = [(i, (i + step) % narrow_count) for i in range(narrow_count)]
        omegas.append(lax.ppermute(omega, "narrow", ring))

    high, low = halves(spectrum_table(freq_total, narrow_count))
    blocks = pl.pallas_call(
        spectrum_kernel,
        out_shape=jax.ShapeDtypeStruct((dests, lines, LANES), jnp.float32),
        in_specs=[HBM] * 3,
        out_specs=VMEM,
        scratch_shapes=[
            pltpu.VMEM((CHUNKS, CELLS, S // CHUNKS), jnp.float32),
            pltpu.VMEM((1, CELLS), jnp.int32),
            pltpu.VMEM((4 * dests, S), jnp.bfloat16),
            pltpu.SemaphoreType.DMA((2 + CHUNKS,)),
        ],
        name="spectrum",
    )(traces.reshape(CELLS, S), mask.reshape(1, CELLS), np.concatenate([high, low], 0))
    grid = lax.all_to_all(blocks, ("wide", "narrow"), split_axis=0, concat_axis=0, tiled=True)

    if omega.shape[0] % 8:
        omegas = [jnp.concatenate(omegas, 0)]
    columns = span1 * span2
    omega_hat = pl.pallas_call(
        functools.partial(omega_kernel, columns),
        out_shape=jax.ShapeDtypeStruct((columns * rank, 2 * CELLS), jnp.float32),
        in_specs=[VMEM] * (len(omegas) + 2),
        out_specs=VMEM,
        cost_estimate=pl.CostEstimate(
            flops=6 * columns * rank * LANES * 2 * CELLS,
            bytes_accessed=4 * columns * rank * 2 * CELLS,
            transcendentals=0,
        ),
        compiler_params=pltpu.CompilerParams(vmem_limit_bytes=16 * MIB),
        name="omega",
    )(*omegas, *halves(omega_table()))

    angles = centred_angles()
    counts = (
        correlation(first, keep1)[:, None, None]
        * correlation(second, keep2)[None, :, None]
        * np.outer(correlation(G3, KEEP3), correlation(G4, KEEP4)).reshape(1, 1, CELLS)
    ).reshape(first * second, CELLS)
    forward = np.concatenate([np.cos(angles), np.sin(angles)], 1)
    backward = np.concatenate([np.cos(angles.T), np.sin(angles.T)], 1) / CELLS
    tables = (
        *halves(forward),
        *halves(sketch_table()),
        *halves(basis_table()),
        *halves(window_table()),
        *halves(backward),
        (1.0 / counts).astype(np.float32),
    )
    area = keep1 * keep2 * rank
    scratch = [
        (first * second, lines, 8, LANES),
        (area, 2 * CELLS),
        (area, 2 * CELLS),
        (area, 2 * CELLS),
        (2 * span2 * rank, CELLS),
        (2 * second, CELLS),
    ]
    rebuilt = pl.pallas_call(
        functools.partial(core_kernel, (first, second, rank)),
        out_shape=jax.ShapeDtypeStruct((second, lines, LANES), jnp.float32),
        in_specs=[VMEM] * (2 + len(tables)),
        out_specs=VMEM,
        scratch_shapes=[pltpu.VMEM(shape, jnp.float32) for shape in scratch],
        compiler_params=pltpu.CompilerParams(vmem_limit_bytes=24 * MIB),
        name="core",
    )(grid, omega_hat, *tables)
    returned = lax.all_to_all(rebuilt, "wide", split_axis=0, concat_axis=0, tiled=True)

    high, low = halves(synthesis_table(freq_total))
    filtered = pl.pallas_call(
        synthesis_kernel,
        out_shape=jax.ShapeDtypeStruct((CELLS, S), jnp.float32),
        in_specs=[VMEM] * 2,
        out_specs=HBM,
        scratch_shapes=[
            pltpu.VMEM((PIECES, LANES, S), jnp.float32),
            pltpu.SemaphoreType.DMA((PIECES,)),
        ],
        compiler_params=pltpu.CompilerParams(vmem_limit_bytes=8 * MIB),
        name="synthesis",
    )(returned, np.concatenate([high, high, low], 0))
    return filtered.reshape(traces.shape)


def solution(mesh):
    return jax.shard_map(
        per_device,
        mesh=mesh,
        in_specs=(
            P(("win", "narrow"), "wide", None, None),
            P(("win", "narrow"), "wide", None),
            P("narrow", None),
        ),
        out_specs=P(("win", "narrow"), "wide", None, None),
        check_vma=False,
    )
```

```python
import functools
import math

import jax
import jax.numpy as jnp
import ml_dtypes
import numpy as np
from jax import lax
from jax.experimental import pallas as pl
from jax.experimental.pallas import tpu as pltpu
from jax.sharding import PartitionSpec as P

G3 = 16
G4 = 16
S = 1024
FREQ_DEV = 1
FIRST_BIN = 16
LANES = 128
MIB = 1 << 20
CHUNKS = 2
PIVOTS = 4
CELLS = G3 * G4
KEEP3, KEEP4 = G3 // 2, G4 // 2
SPAN3, SPAN4 = G3 - KEEP3 + 1, G4 - KEEP4 + 1
SHIFT3, SHIFT4 = (SPAN3 - 1) // 2, (SPAN4 - 1) // 2
ROWS = KEEP3 * KEEP4
COLS = SPAN3 * SPAN4
PIECES = CELLS // LANES

HBM = pl.BlockSpec(memory_space=pltpu.HBM)
VMEM = pl.BlockSpec(memory_space=pltpu.VMEM)
highest = lax.Precision.HIGHEST


def halves(table):
    table = np.asarray(table, np.float32)
    high = table.astype(ml_dtypes.bfloat16)
    low = (table - high.astype(np.float32)).astype(ml_dtypes.bfloat16)
    return high, low


def phases(freq_total):
    bins = FIRST_BIN + np.arange(freq_total)
    return 2.0 * np.pi * ((bins[:, None] * np.arange(S)[None, :]) % S) / S


def cell_angles(positions3, positions4):
    wave = np.arange(CELLS)
    turns = (
        np.outer(positions3, wave // G4) % G3 / G3 + np.outer(positions4, wave % G4) % G4 / G4
    )
    return 2.0 * np.pi * turns


def correlation(length, keep_size):
    position = np.arange(length)
    span_size = length - keep_size + 1
    return (
        np.minimum(position, keep_size - 1) - np.maximum(position - span_size + 1, 0) + 1
    ).astype(np.float64)


def spectrum_table(freq_total, copies):
    angles = np.repeat(phases(freq_total), copies, 0)
    return np.concatenate([np.cos(angles), -np.sin(angles)], 0) / math.sqrt(S)


def synthesis_table(freq_total):
    angles = phases(freq_total)
    return np.concatenate([np.cos(angles), -np.sin(angles)], 0) * math.sqrt(2.0 / freq_total)


def centred_angles():
    cell = np.arange(CELLS)
    return cell_angles(cell // G4 - SHIFT3, cell % G4 - SHIFT4)


def omega_table():
    column = np.arange(COLS)
    angles = cell_angles(column // SPAN4, column % SPAN4)
    table = np.zeros((LANES, 2 * CELLS))
    table[:COLS] = np.concatenate([np.cos(angles), -np.sin(angles)], 1)
    return table


def sketch_table():
    row = np.arange(ROWS)
    angles = cell_angles(row // KEEP4 - SHIFT3, row % KEEP4 - SHIFT4).T
    real, imag = np.cos(angles) / CELLS, np.sin(angles) / CELLS
    from_real = np.concatenate([real, imag, imag, -real], 1)
    from_imag = np.concatenate([-imag, real, real, imag], 1)
    return np.concatenate([from_real, from_imag], 0)


def basis_table():
    row = np.arange(ROWS)
    angles = cell_angles(row // KEEP4, row % KEEP4)
    real, imag = np.cos(angles), np.sin(angles)
    return np.concatenate(
        [np.concatenate([real, -imag], 1), np.concatenate([imag, real], 1)], 0
    )


def window_table():
    parts = []
    for length, shift in ((G3, SHIFT3), (G4, SHIFT4)):
        wave = np.arange(length)
        turns = (wave[:, None] - wave[None, :])[:, :, None] * np.arange(-shift, shift + 1) / length
        parts.append(np.cos(2.0 * np.pi * turns).sum(-1) / length)
    return np.kron(parts[0], parts[1])


def split(value):
    high = value.astype(jnp.bfloat16)
    low = (value - high.astype(jnp.float32)).astype(jnp.bfloat16)
    return high, low


def dot(left, right):
    return jnp.dot(left, right, preferred_element_type=jnp.float32)


def wide_dot(value, high, low):
    rows = value.shape[0]
    value_high, value_low = split(value)
    main = dot(jnp.concatenate([value_high, value_low], 0), high)
    return main[:rows] + (main[rows:] + dot(value_high, low))


def spectrum_kernel(traces_ref, mask_ref, table_ref, out_ref, traces, mask, table, sems):
    rows = table.shape[0] // 2
    dests = rows // 2
    chunks, _, width = traces.shape
    copies = [
        pltpu.make_async_copy(table_ref, table, sems.at[0]),
        pltpu.make_async_copy(mask_ref, mask, sems.at[1]),
    ] + [
        pltpu.make_async_copy(
            traces_ref.at[:, pl.ds(i * width, width)], traces.at[i], sems.at[2 + i]
        )
        for i in range(chunks)
    ]
    for copy in copies:
        copy.start()
    copies[0].wait()
    contract = (((1,), (1,)), ((), ()))
    total = jnp.zeros((2 * rows, CELLS), jnp.float32)
    rest = jnp.zeros((rows, CELLS), jnp.float32)
    for i in range(chunks):
        copies[2 + i].wait()
        high, low = split(traces[i])
        place = pl.ds(i * width, width)
        total += lax.dot_general(
            table[:, place], high, contract, preferred_element_type=jnp.float32
        )
        rest += lax.dot_general(
            table[:rows, place], low, contract, preferred_element_type=jnp.float32
        )
    copies[1].wait()
    result = (total[:rows] + (total[rows:] + rest)) * mask[...].astype(jnp.float32)
    for part in range(2):
        for piece in range(PIECES):
            out_ref[:, part * PIECES + piece, :] = result[
                part * dests : (part + 1) * dests, piece * LANES : (piece + 1) * LANES
            ]


def omega_kernel(columns, *refs):
    omega_refs = refs[:-3]
    high_ref, low_ref, out_ref = refs[-3:]
    omega = jnp.concatenate([ref[...] for ref in omega_refs], 0)
    pad = jnp.zeros((omega.shape[0], LANES - COLS), jnp.float32)
    blocks = [
        jnp.concatenate([omega[:, k * COLS : (k + 1) * COLS], pad], 1) for k in range(columns)
    ]
    out_ref[...] = wide_dot(jnp.concatenate(blocks, 0), high_ref[...], low_ref[...])


def minus_product(value, left, right):
    return (
        value[0] - (left[0] * right[0] - left[1] * right[1]),
        value[1] - (left[0] * right[1] + left[1] * right[0]),
    )


def pivot_pair(upper, lower, corner, other, cross, scale):
    turned = (cross[0], -cross[1])
    first = minus_product(tuple(other * v for v in upper), cross, lower)
    second = minus_product(tuple(corner * v for v in lower), turned, upper)
    return tuple(v * scale for v in first), tuple(v * scale for v in second)


def invert(real, imag, result):
    size = real.shape[0]
    width = 2 * size
    tiles = [(real[t : t + 8], imag[t : t + 8]) for t in range(0, size, 8)]
    sublane = lax.broadcasted_iota(jnp.int32, (8, width), 0)
    for start in range(0, size, PIVOTS):
        home, at = start // 8, start % 8
        lane = size + start

        def spread(value, b, height):
            return jnp.broadcast_to(value[:, lane + b : lane + b + 1], (height, width))

        rows = [tuple(v[at + a : at + a + 1] for v in tiles[home]) for a in range(PIVOTS)]
        block = {}
        for a in range(PIVOTS):
            block[a, a] = (spread(rows[a][0], a, 1),)
            for b in range(a + 1, PIVOTS):
                block[a, b] = tuple(spread(v, b, 1) for v in rows[a])
                block[b, a] = (block[a, b][0], -block[a, b][1])
        columns = [
            [tuple(spread(v, b, 8) for v in tile) for b in range(PIVOTS)] for tile in tiles
        ]
        for p in range(0, PIVOTS, 2):
            q = p + 1
            corner, other, cross = block[p, p][0], block[q, q][0], block[p, q]
            scale = 1.0 / (corner * other - (cross[0] * cross[0] + cross[1] * cross[1]))
            pair = (corner, other, cross, scale)
            rows[p], rows[q] = pivot_pair(rows[p], rows[q], *pair)
            later = range(p + 2, PIVOTS)
            done = {}
            for c in later:
                done[p, c], done[q, c] = pivot_pair(block[p, c], block[q, c], *pair)
            for o in range(PIVOTS):
                if o in (p, q):
                    continue
                left, right = block[o, p], block[o, q]
                rows[o] = minus_product(minus_product(rows[o], left, rows[p]), right, rows[q])
                for c in later:
                    if o == c:
                        first, second = done[p, c], done[q, c]
                        value = block[o, o][0]
                        value = value - (left[0] * first[0] - left[1] * first[1])
                        value = value - (right[0] * second[0] - right[1] * second[1])
                        done[o, o] = (value,)
                    elif o < c:
                        value = minus_product(block[o, c], left, done[p, c])
                        done[o, c] = minus_product(value, right, done[q, c])
                        if o > q:
                            done[c, o] = (done[o, c][0], -done[o, c][1])
            block.update(done)
        for t in range(len(tiles)):
            tile = tiles[t]
            for b in range(PIVOTS):
                tile = minus_product(tile, columns[t][b], rows[b])
            if t == home:
                for b in range(PIVOTS):
                    here = sublane == at + b
                    tile = tuple(jnp.where(here, rows[b][k], tile[k]) for k in range(2))
            tiles[t] = tile
        yield
    for part in range(2):
        result.append(jnp.concatenate([tile[part] for tile in tiles], 0)[:, :size])


def interleave(*steps):
    steps = list(steps)
    while steps:
        steps = [step for step in steps if next(step, steps) is not steps]


def core_kernel(
    dims,
    x_ref,
    omega_ref,
    analysis_high,
    analysis_low,
    sketch_high,
    sketch_low,
    basis_high,
    basis_low,
    window_high,
    window_low,
    back_high,
    back_low,
    weight_ref,
    out_ref,
    handed_ref,
    xhat,
    shat,
    bhat,
    uhat,
    dhat,
    ghat,
    sends,
):
    first, second, rank = dims
    keep1, keep2 = first // 2, second // 2
    span1, span2 = first - keep1 + 1, second - keep2 + 1
    own = lax.axis_index("narrow")
    half = CELLS
    tiles = rank // 8
    pieces = CELLS // LANES
    small = keep1 * keep2 * span1 * span2 <= 64

    def sweep(count, body, carry):
        if small:
            for i in range(count):
                carry = body(i, carry)
            return carry
        return lax.fori_loop(0, count, body, carry)

    def rows(start, count=8):
        if isinstance(start, int):
            return pl.ds(start, count)
        return pl.ds(pl.multiple_of(start, 8), count)

    def lanes(part, piece):
        start = part * half + piece * LANES
        return pl.ds(start, LANES)

    planes = first * second
    spectrum = jnp.concatenate(
        [
            jnp.concatenate([x_ref[:, part * pieces + piece, :] for piece in range(pieces)], 1)
            for part in range(2)
        ],
        0,
    )
    both = wide_dot(spectrum, analysis_high[...], analysis_low[...])
    hats = (
        both[:planes, :half] + both[planes:, half:],
        both[planes:, :half] - both[:planes, half:],
    )
    for part in range(2):
        for piece in range(pieces):
            values = hats[part][:, piece * LANES : (piece + 1) * LANES]
            xhat[:, part * pieces + piece] = jnp.broadcast_to(
                values[:, None, :], (planes, 8, LANES)
            )

    def load_x(g1, g2, piece):
        row = g2 * first + g1
        return xhat[row, piece], xhat[row, pieces + piece]

    for piece in range(pieces):
        cache = {}

        def cached_x(g1, g2):
            if not small:
                return load_x(g1, g2, piece)
            if (g1, g2) not in cache:
                cache[g1, g2] = load_x(g1, g2, piece)
            return cache[g1, g2]

        def sketch_tile(tile, carry):
            def first_keep(l1, carry):
                zero = jnp.zeros((8, LANES), jnp.float32)

                def columns(k1, sums):
                    def column(k2, sums):
                        start = (k1 * span2 + k2) * rank + tile * 8
                        w_real = omega_ref[rows(start), lanes(0, piece)]
                        w_imag = omega_ref[rows(start), lanes(1, piece)]
                        sums = list(sums)
                        for l2 in range(keep2):
                            x_real, x_imag = cached_x(l1 + k1, l2 + k2)
                            real, imag = sums[l2]
                            sums[l2] = (
                                real + (x_real * w_real + x_imag * w_imag),
                                imag + (x_imag * w_real - x_real * w_imag),
                            )
                        return tuple(sums)

                    return sweep(span2, column, sums)

                sums = sweep(span1, columns, ((zero, zero),) * keep2)
                for l2 in range(keep2):
                    start = (l1 * keep2 + l2) * rank + tile * 8
                    shat[rows(start), lanes(0, piece)] = sums[l2][0]
                    shat[rows(start), lanes(1, piece)] = sums[l2][1]
                return carry

            return sweep(keep1, first_keep, carry)

        sweep(tiles, sketch_tile, 0)

    blocks = keep1 * keep2
    sketch = wide_dot(shat[...], sketch_high[...], sketch_low[...])
    straight = jnp.concatenate(
        [sketch[b * rank : (b + 1) * rank, : 2 * ROWS] for b in range(blocks)], 1
    )
    turned = jnp.concatenate(
        [sketch[b * rank : (b + 1) * rank, 2 * ROWS :] for b in range(blocks)], 1
    )
    contract = (((1,), (1,)), ((), ()))
    space = jnp.zeros_like(straight)

    def gram(right):
        return lax.dot_general(
            straight,
            jnp.concatenate([space, right], 0),
            contract,
            precision=highest,
            preferred_element_type=jnp.float32,
        )

    row_index = lax.broadcasted_iota(jnp.int32, (rank, 2 * rank), 0)
    column_index = lax.broadcasted_iota(jnp.int32, (rank, 2 * rank), 1)
    unit = 1.0 / jnp.max(jnp.abs(spectrum), keepdims=True)
    gram_real = gram(straight) * unit * unit
    gram_imag = gram(turned) * unit * unit
    gram_real = jnp.where(row_index == column_index, 1.0, gram_real)

    def partner(a):
        k1 = own - a
        valid = jnp.logical_and(k1 >= 0, k1 < span1).astype(jnp.float32)
        return jnp.clip(k1, 0, span1 - 1), valid

    def own_columns(a):
        k1, _ = partner(a)
        for piece in range(pieces):
            cache = {}

            def cached_x(l1, g2):
                if not small:
                    return load_x(l1 + k1, g2, piece)
                if (l1, g2) not in cache:
                    cache[l1, g2] = load_x(l1 + k1, g2, piece)
                return cache[l1, g2]

            def column_tile(tile, carry):
                zero = jnp.zeros((8, LANES), jnp.float32)

                def first_keep(l1, sums):
                    sums = list(sums)
                    for l2 in range(keep2):
                        start = (l1 * keep2 + l2) * rank + tile * 8
                        s_real = bhat[rows(start), lanes(0, piece)]
                        s_imag = bhat[rows(start), lanes(1, piece)]
                        for k2 in range(span2):
                            x_real, x_imag = cached_x(l1, l2 + k2)
                            real, imag = sums[k2]
                            sums[k2] = (
                                real + (s_real * x_real + s_imag * x_imag),
                                imag + (s_real * x_imag - s_imag * x_real),
                            )
                    return tuple(sums)

                sums = sweep(keep1, first_keep, ((zero, zero),) * span2)
                for k2 in range(span2):
                    for part in range(2):
                        start = (part * span2 + k2) * rank + tile * 8
                        dhat[rows(start), pl.ds(piece * LANES, LANES)] = sums[k2][part]
                return carry

            if small:
                for tile in range(tiles):
                    column_tile(tile, 0)
                    yield
            else:
                sweep(tiles, column_tile, 0)
        dhat[...] = wide_dot(dhat[...], window_high[...], window_low[...])
        yield

    def own_planes(a):
        _, valid = partner(a)
        for piece in range(pieces):

            def rebuild_tile(tile, sums):
                sums = list(sums)
                us = []
                for l2 in range(keep2):
                    start = (a * keep2 + l2) * rank + tile * 8
                    us.append(
                        (
                            uhat[rows(start), lanes(0, piece)],
                            uhat[rows(start), lanes(1, piece)],
                        )
                    )
                for k2 in range(span2):
                    d_real = dhat[rows(k2 * rank + tile * 8), pl.ds(piece * LANES, LANES)]
                    d_imag = dhat[
                        rows((span2 + k2) * rank + tile * 8), pl.ds(piece * LANES, LANES)
                    ]
                    for l2 in range(keep2):
                        u_real, u_imag = us[l2]
                        real, imag = sums[l2 + k2]
                        sums[l2 + k2] = (
                            real + (u_real * d_real - u_imag * d_imag),
                            imag + (u_real * d_imag + u_imag * d_real),
                        )
                return tuple(sums)

            zero = jnp.zeros((8, LANES), jnp.float32)
            sums = sweep(tiles, rebuild_tile, ((zero, zero),) * second)
            for part in range(2):
                summed = jnp.concatenate(
                    [jnp.sum(sums[g2][part], 0, keepdims=True) for g2 in range(second)], 0
                )
                place = pl.ds(piece * LANES, LANES)
                where = pl.ds(part * second, second)
                ghat[where, place] = ghat[where, place] + summed * valid

    def own_basis():
        bhat[...] = wide_dot(sketch[:, : 2 * ROWS], basis_high[...], basis_low[...])
        yield
        if small:
            yield from own_columns(0)

    inverse = []
    interleave(invert(gram_real, gram_imag, inverse), own_basis())
    mixer = jnp.concatenate(inverse, 0) * unit * unit

    def mix(b, carry):
        where = rows(b * rank, rank)
        both = jnp.dot(
            mixer, bhat[where, :], precision=highest, preferred_element_type=jnp.float32
        )
        uhat[where, :half] = both[:rank, :half] + both[rank:, half:]
        uhat[where, half:] = both[:rank, half:] - both[rank:, :half]
        return carry

    sweep(blocks, mix, 0)
    ghat[...] = jnp.zeros_like(ghat)

    def own_pair(a, carry):
        if not (small and isinstance(a, int) and a == 0):
            for _ in own_columns(a):
                pass
        own_planes(a)
        return carry

    sweep(keep1, own_pair, 0)

    both = wide_dot(ghat[...], back_high[...], back_low[...])
    real = both[:second, :half] - both[second:, half:]
    imag = both[:second, half:] + both[second:, :half]
    weight = weight_ref[pl.ds(pl.multiple_of(own * second, 8), second), :]
    real = real * weight
    imag = imag * weight
    here = lax.axis_index("wide")
    for w in range(second):
        offset = jnp.bitwise_xor(here, w)
        slot = (offset % 2) * (second // 2) + offset // 2
        for piece in range(pieces):
            place = slice(piece * LANES, (piece + 1) * LANES)
            sends[slot, pl.ds(piece, 1), :] = real[w : w + 1, place]
            sends[slot, pl.ds(pieces + piece, 1), :] = imag[w : w + 1, place]
    out_ref[...] = sends[: second // 2]
    handed_ref[...] = sends[second // 2 :]


def synthesis_kernel(*refs):
    *block_refs, table_ref, out_ref, out, cells, sems = refs
    here = lax.axis_index("wide")
    for i in range(len(block_refs)):
        for j in range(2):
            cells[jnp.bitwise_xor(here, 2 * i + j)] = block_refs[i][j]
    parts = [
        jnp.concatenate([cells[:, part * PIECES + piece, :] for piece in range(PIECES)], 1)
        for part in range(2)
    ]
    high, low = split(jnp.concatenate(parts, 0))
    stacked = jnp.concatenate([high, low, high], 0)
    contract = (((0,), (0,)), ((), ()))
    chunks, width, _ = out.shape
    copies = []
    for i in range(chunks):
        out[i] = lax.dot_general(
            stacked[:, i * width : (i + 1) * width],
            table_ref[...],
            contract,
            preferred_element_type=jnp.float32,
        )
        copies.append(
            pltpu.make_async_copy(out.at[i], out_ref.at[pl.ds(i * width, width)], sems.at[i])
        )
        copies[-1].start()
    for copy in copies:
        copy.wait()


def per_device(traces, mask, omega):
    narrow_count = lax.axis_size("narrow")
    wide_count = lax.axis_size("wide")
    assert traces.shape[:2] == (1, 1)
    first, second = narrow_count, wide_count
    freq_total = FREQ_DEV * wide_count
    keep1, keep2 = first // 2, second // 2
    span1, span2 = first - keep1 + 1, second - keep2 + 1
    rank = omega.shape[0] * narrow_count
    dests = wide_count * narrow_count
    lines = 2 * PIECES

    omegas = [omega]
    for step in range(1, narrow_count):
        ring = [(i, (i + step) % narrow_count) for i in range(narrow_count)]
        omegas.append(lax.ppermute(omega, "narrow", ring))

    high, low = halves(spectrum_table(freq_total, narrow_count))
    blocks = pl.pallas_call(
        spectrum_kernel,
        out_shape=jax.ShapeDtypeStruct((dests, lines, LANES), jnp.float32),
        in_specs=[HBM] * 3,
        out_specs=VMEM,
        scratch_shapes=[
            pltpu.VMEM((CHUNKS, CELLS, S // CHUNKS), jnp.float32),
            pltpu.VMEM((1, CELLS), jnp.int32),
            pltpu.VMEM((4 * dests, S), jnp.bfloat16),
            pltpu.SemaphoreType.DMA((2 + CHUNKS,)),
        ],
        name="spectrum",
    )(traces.reshape(CELLS, S), mask.reshape(1, CELLS), np.concatenate([high, low], 0))
    grid = lax.all_to_all(blocks, ("wide", "narrow"), split_axis=0, concat_axis=0, tiled=True)

    if omega.shape[0] % 8:
        omegas = [jnp.concatenate(omegas, 0)]
    columns = span1 * span2
    omega_hat = pl.pallas_call(
        functools.partial(omega_kernel, columns),
        out_shape=jax.ShapeDtypeStruct((columns * rank, 2 * CELLS), jnp.float32),
        in_specs=[VMEM] * (len(omegas) + 2),
        out_specs=VMEM,
        cost_estimate=pl.CostEstimate(
            flops=6 * columns * rank * LANES * 2 * CELLS,
            bytes_accessed=4 * columns * rank * 2 * CELLS,
            transcendentals=0,
        ),
        compiler_params=pltpu.CompilerParams(vmem_limit_bytes=16 * MIB),
        name="omega",
    )(*omegas, *halves(omega_table()))

    angles = centred_angles()
    counts = (
        correlation(first, keep1)[:, None, None]
        * correlation(second, keep2)[None, :, None]
        * np.outer(correlation(G3, KEEP3), correlation(G4, KEEP4)).reshape(1, 1, CELLS)
    ).reshape(first * second, CELLS)
    forward = np.concatenate([np.cos(angles), np.sin(angles)], 1)
    backward = np.concatenate([np.cos(angles.T), np.sin(angles.T)], 1) / CELLS
    tables = (
        *halves(forward),
        *halves(sketch_table()),
        *halves(basis_table()),
        *halves(window_table()),
        *halves(backward),
        (1.0 / counts).astype(np.float32),
    )
    area = keep1 * keep2 * rank
    scratch = [
        (first * second, lines, 8, LANES),
        (area, 2 * CELLS),
        (area, 2 * CELLS),
        (area, 2 * CELLS),
        (2 * span2 * rank, CELLS),
        (2 * second, CELLS),
        (second, lines, LANES),
    ]
    chips = second // 2
    kept, handed = pl.pallas_call(
        functools.partial(core_kernel, (first, second, rank)),
        out_shape=[jax.ShapeDtypeStruct((chips, lines, LANES), jnp.float32)] * 2,
        in_specs=[VMEM] * (2 + len(tables)),
        out_specs=[VMEM] * 2,
        scratch_shapes=[pltpu.VMEM(shape, jnp.float32) for shape in scratch],
        compiler_params=pltpu.CompilerParams(vmem_limit_bytes=24 * MIB),
        name="core",
    )(grid, omega_hat, *tables)

    def across(value, offset):
        return lax.ppermute(value, "wide", [(i, i ^ offset) for i in range(second)])

    handed = across(handed, 1)
    joined = jnp.stack([kept, handed], 1)
    returned = [joined[0]] + [across(joined[i], 2 * i) for i in range(1, chips)]

    high, low = halves(synthesis_table(freq_total))
    filtered = pl.pallas_call(
        synthesis_kernel,
        out_shape=jax.ShapeDtypeStruct((CELLS, S), jnp.float32),
        in_specs=[VMEM] * (chips + 1),
        out_specs=HBM,
        scratch_shapes=[
            pltpu.VMEM((PIECES, LANES, S), jnp.float32),
            pltpu.VMEM((second, lines, LANES), jnp.float32),
            pltpu.SemaphoreType.DMA((PIECES,)),
        ],
        compiler_params=pltpu.CompilerParams(vmem_limit_bytes=8 * MIB),
        name="synthesis",
    )(*returned, np.concatenate([high, high, low], 0))
    return filtered.reshape(traces.shape)


def solution(mesh):
    return jax.shard_map(
        per_device,
        mesh=mesh,
        in_specs=(
            P(("win", "narrow"), "wide", None, None),
            P(("win", "narrow"), "wide", None),
            P("narrow", None),
        ),
        out_specs=P(("win", "narrow"), "wide", None, None),
        check_vma=False,
    )
```

```python
import functools
import math

import jax
import jax.numpy as jnp
import ml_dtypes
import numpy as np
from jax import lax
from jax.experimental import pallas as pl
from jax.experimental.pallas import tpu as pltpu
from jax.sharding import PartitionSpec as P

G3 = 16
G4 = 16
S = 1024
FREQ_DEV = 1
FIRST_BIN = 16
LANES = 128
MIB = 1 << 20
CHUNKS = 2
PIVOTS = 4
CELLS = G3 * G4
KEEP3, KEEP4 = G3 // 2, G4 // 2
SPAN3, SPAN4 = G3 - KEEP3 + 1, G4 - KEEP4 + 1
SHIFT3, SHIFT4 = (SPAN3 - 1) // 2, (SPAN4 - 1) // 2
ROWS = KEEP3 * KEEP4
COLS = SPAN3 * SPAN4
PIECES = CELLS // LANES

HBM = pl.BlockSpec(memory_space=pltpu.HBM)
VMEM = pl.BlockSpec(memory_space=pltpu.VMEM)
highest = lax.Precision.HIGHEST


def halves(table):
    table = np.asarray(table, np.float32)
    high = table.astype(ml_dtypes.bfloat16)
    low = (table - high.astype(np.float32)).astype(ml_dtypes.bfloat16)
    return high, low


def phases(freq_total):
    bins = FIRST_BIN + np.arange(freq_total)
    return 2.0 * np.pi * ((bins[:, None] * np.arange(S)[None, :]) % S) / S


def cell_angles(positions3, positions4):
    wave = np.arange(CELLS)
    turns = (
        np.outer(positions3, wave // G4) % G3 / G3 + np.outer(positions4, wave % G4) % G4 / G4
    )
    return 2.0 * np.pi * turns


def correlation(length, keep_size):
    position = np.arange(length)
    span_size = length - keep_size + 1
    return (
        np.minimum(position, keep_size - 1) - np.maximum(position - span_size + 1, 0) + 1
    ).astype(np.float64)


def spectrum_table(freq_total, owners):
    angles = phases(freq_total)[owners]
    return np.concatenate([np.cos(angles), -np.sin(angles)], 0) / math.sqrt(S)


def synthesis_table(freq_total):
    angles = phases(freq_total)
    return np.concatenate([np.cos(angles), -np.sin(angles)], 0) * math.sqrt(2.0 / freq_total)


def centred_angles():
    cell = np.arange(CELLS)
    return cell_angles(cell // G4 - SHIFT3, cell % G4 - SHIFT4)


def omega_table():
    column = np.arange(COLS)
    angles = cell_angles(column // SPAN4, column % SPAN4)
    table = np.zeros((LANES, 2 * CELLS))
    table[:COLS] = np.concatenate([np.cos(angles), -np.sin(angles)], 1)
    return table


def sketch_table():
    row = np.arange(ROWS)
    angles = cell_angles(row // KEEP4 - SHIFT3, row % KEEP4 - SHIFT4).T
    real, imag = np.cos(angles) / CELLS, np.sin(angles) / CELLS
    from_real = np.concatenate([real, imag, imag, -real], 1)
    from_imag = np.concatenate([-imag, real, real, imag], 1)
    return np.concatenate([from_real, from_imag], 0)


def basis_table():
    row = np.arange(ROWS)
    angles = cell_angles(row // KEEP4, row % KEEP4)
    real, imag = np.cos(angles), np.sin(angles)
    return np.concatenate(
        [np.concatenate([real, -imag], 1), np.concatenate([imag, real], 1)], 0
    )


def window_table():
    parts = []
    for length, shift in ((G3, SHIFT3), (G4, SHIFT4)):
        wave = np.arange(length)
        turns = (wave[:, None] - wave[None, :])[:, :, None] * np.arange(-shift, shift + 1) / length
        parts.append(np.cos(2.0 * np.pi * turns).sum(-1) / length)
    return np.kron(parts[0], parts[1])


def split(value):
    high = value.astype(jnp.bfloat16)
    low = (value - high.astype(jnp.float32)).astype(jnp.bfloat16)
    return high, low


def dot(left, right):
    return jnp.dot(left, right, preferred_element_type=jnp.float32)


def wide_dot(value, high, low):
    rows = value.shape[0]
    value_high, value_low = split(value)
    main = dot(jnp.concatenate([value_high, value_low], 0), high)
    return main[:rows] + (main[rows:] + dot(value_high, low))


def spectrum_kernel(traces_ref, mask_ref, table_ref, out_ref, traces, mask, table, sems):
    rows = table.shape[0] // 2
    dests = rows // 2
    chunks, _, width = traces.shape
    copies = [
        pltpu.make_async_copy(table_ref, table, sems.at[0]),
        pltpu.make_async_copy(mask_ref, mask, sems.at[1]),
    ] + [
        pltpu.make_async_copy(
            traces_ref.at[:, pl.ds(i * width, width)], traces.at[i], sems.at[2 + i]
        )
        for i in range(chunks)
    ]
    for copy in copies:
        copy.start()
    copies[0].wait()
    contract = (((1,), (1,)), ((), ()))
    total = jnp.zeros((2 * rows, CELLS), jnp.float32)
    rest = jnp.zeros((rows, CELLS), jnp.float32)
    for i in range(chunks):
        copies[2 + i].wait()
        high, low = split(traces[i])
        place = pl.ds(i * width, width)
        total += lax.dot_general(
            table[:, place], high, contract, preferred_element_type=jnp.float32
        )
        rest += lax.dot_general(
            table[:rows, place], low, contract, preferred_element_type=jnp.float32
        )
    copies[1].wait()
    result = (total[:rows] + (total[rows:] + rest)) * mask[...].astype(jnp.float32)
    for part in range(2):
        for piece in range(PIECES):
            out_ref[:, part * PIECES + piece, :] = result[
                part * dests : (part + 1) * dests, piece * LANES : (piece + 1) * LANES
            ]


def omega_kernel(columns, *refs):
    omega_refs = refs[:-3]
    high_ref, low_ref, out_ref = refs[-3:]
    omega = jnp.concatenate([ref[...] for ref in omega_refs], 0)
    pad = jnp.zeros((omega.shape[0], LANES - COLS), jnp.float32)
    blocks = [
        jnp.concatenate([omega[:, k * COLS : (k + 1) * COLS], pad], 1) for k in range(columns)
    ]
    out_ref[...] = wide_dot(jnp.concatenate(blocks, 0), high_ref[...], low_ref[...])


def minus_product(value, left, right):
    return (
        value[0] - (left[0] * right[0] - left[1] * right[1]),
        value[1] - (left[0] * right[1] + left[1] * right[0]),
    )


def pivot_pair(upper, lower, corner, other, cross, scale):
    turned = (cross[0], -cross[1])
    first = minus_product(tuple(other * v for v in upper), cross, lower)
    second = minus_product(tuple(corner * v for v in lower), turned, upper)
    return tuple(v * scale for v in first), tuple(v * scale for v in second)


def invert(real, imag, result):
    size = real.shape[0]
    width = 2 * size
    tiles = [(real[t : t + 8], imag[t : t + 8]) for t in range(0, size, 8)]
    sublane = lax.broadcasted_iota(jnp.int32, (8, width), 0)
    for start in range(0, size, PIVOTS):
        home, at = start // 8, start % 8
        lane = size + start

        def spread(value, b, height):
            return jnp.broadcast_to(value[:, lane + b : lane + b + 1], (height, width))

        rows = [tuple(v[at + a : at + a + 1] for v in tiles[home]) for a in range(PIVOTS)]
        block = {}
        for a in range(PIVOTS):
            block[a, a] = (spread(rows[a][0], a, 1),)
            for b in range(a + 1, PIVOTS):
                block[a, b] = tuple(spread(v, b, 1) for v in rows[a])
                block[b, a] = (block[a, b][0], -block[a, b][1])
        columns = [
            [tuple(spread(v, b, 8) for v in tile) for b in range(PIVOTS)] for tile in tiles
        ]
        for p in range(0, PIVOTS, 2):
            q = p + 1
            corner, other, cross = block[p, p][0], block[q, q][0], block[p, q]
            scale = 1.0 / (corner * other - (cross[0] * cross[0] + cross[1] * cross[1]))
            pair = (corner, other, cross, scale)
            rows[p], rows[q] = pivot_pair(rows[p], rows[q], *pair)
            later = range(p + 2, PIVOTS)
            done = {}
            for c in later:
                done[p, c], done[q, c] = pivot_pair(block[p, c], block[q, c], *pair)
            for o in range(PIVOTS):
                if o in (p, q):
                    continue
                left, right = block[o, p], block[o, q]
                rows[o] = minus_product(minus_product(rows[o], left, rows[p]), right, rows[q])
                for c in later:
                    if o == c:
                        first, second = done[p, c], done[q, c]
                        value = block[o, o][0]
                        value = value - (left[0] * first[0] - left[1] * first[1])
                        value = value - (right[0] * second[0] - right[1] * second[1])
                        done[o, o] = (value,)
                    elif o < c:
                        value = minus_product(block[o, c], left, done[p, c])
                        done[o, c] = minus_product(value, right, done[q, c])
                        if o > q:
                            done[c, o] = (done[o, c][0], -done[o, c][1])
            block.update(done)
        for t in range(len(tiles)):
            tile = tiles[t]
            for b in range(PIVOTS):
                tile = minus_product(tile, columns[t][b], rows[b])
            if t == home:
                for b in range(PIVOTS):
                    here = sublane == at + b
                    tile = tuple(jnp.where(here, rows[b][k], tile[k]) for k in range(2))
            tiles[t] = tile
        yield
    for part in range(2):
        result.append(jnp.concatenate([tile[part] for tile in tiles], 0)[:, :size])


def interleave(*steps):
    steps = list(steps)
    while steps:
        steps = [step for step in steps if next(step, steps) is not steps]


def core_kernel(
    dims,
    order,
    x_ref,
    omega_ref,
    analysis_high,
    analysis_low,
    sketch_high,
    sketch_low,
    basis_high,
    basis_low,
    window_high,
    window_low,
    back_high,
    back_low,
    weight_ref,
    out_ref,
    handed_ref,
    xhat,
    shat,
    bhat,
    uhat,
    dhat,
    ghat,
    sends,
):
    first, second, rank = dims
    keep1, keep2 = first // 2, second // 2
    span1, span2 = first - keep1 + 1, second - keep2 + 1
    own = lax.axis_index("narrow")
    half = CELLS
    tiles = rank // 8
    pieces = CELLS // LANES
    small = keep1 * keep2 * span1 * span2 <= 64

    def sweep(count, body, carry):
        if small:
            for i in range(count):
                carry = body(i, carry)
            return carry
        return lax.fori_loop(0, count, body, carry)

    def rows(start, count=8):
        if isinstance(start, int):
            return pl.ds(start, count)
        return pl.ds(pl.multiple_of(start, 8), count)

    def lanes(part, piece):
        start = part * half + piece * LANES
        return pl.ds(start, LANES)

    planes = first * second
    spectrum = jnp.concatenate(
        [
            jnp.concatenate([x_ref[:, part * pieces + piece, :] for piece in range(pieces)], 1)
            for part in range(2)
        ],
        0,
    )
    both = wide_dot(spectrum, analysis_high[...], analysis_low[...])
    hats = (
        both[:planes, :half] + both[planes:, half:],
        both[planes:, :half] - both[:planes, half:],
    )
    for part in range(2):
        for piece in range(pieces):
            values = hats[part][:, piece * LANES : (piece + 1) * LANES]
            for p in range(planes):
                xhat[order[p], part * pieces + piece] = jnp.broadcast_to(
                    values[p : p + 1], (8, LANES)
                )

    def load_x(g1, g2, piece):
        row = g2 * first + g1
        return xhat[row, piece], xhat[row, pieces + piece]

    for piece in range(pieces):
        cache = {}

        def cached_x(g1, g2):
            if not small:
                return load_x(g1, g2, piece)
            if (g1, g2) not in cache:
                cache[g1, g2] = load_x(g1, g2, piece)
            return cache[g1, g2]

        def sketch_tile(tile, carry):
            def first_keep(l1, carry):
                zero = jnp.zeros((8, LANES), jnp.float32)

                def columns(k1, sums):
                    def column(k2, sums):
                        start = (k1 * span2 + k2) * rank + tile * 8
                        w_real = omega_ref[rows(start), lanes(0, piece)]
                        w_imag = omega_ref[rows(start), lanes(1, piece)]
                        sums = list(sums)
                        for l2 in range(keep2):
                            x_real, x_imag = cached_x(l1 + k1, l2 + k2)
                            real, imag = sums[l2]
                            sums[l2] = (
                                real + (x_real * w_real + x_imag * w_imag),
                                imag + (x_imag * w_real - x_real * w_imag),
                            )
                        return tuple(sums)

                    return sweep(span2, column, sums)

                sums = sweep(span1, columns, ((zero, zero),) * keep2)
                for l2 in range(keep2):
                    start = (l1 * keep2 + l2) * rank + tile * 8
                    shat[rows(start), lanes(0, piece)] = sums[l2][0]
                    shat[rows(start), lanes(1, piece)] = sums[l2][1]
                return carry

            return sweep(keep1, first_keep, carry)

        sweep(tiles, sketch_tile, 0)

    blocks = keep1 * keep2
    sketch = wide_dot(shat[...], sketch_high[...], sketch_low[...])
    straight = jnp.concatenate(
        [sketch[b * rank : (b + 1) * rank, : 2 * ROWS] for b in range(blocks)], 1
    )
    turned = jnp.concatenate(
        [sketch[b * rank : (b + 1) * rank, 2 * ROWS :] for b in range(blocks)], 1
    )
    contract = (((1,), (1,)), ((), ()))
    space = jnp.zeros_like(straight)

    def gram(right):
        return lax.dot_general(
            straight,
            jnp.concatenate([space, right], 0),
            contract,
            precision=highest,
            preferred_element_type=jnp.float32,
        )

    row_index = lax.broadcasted_iota(jnp.int32, (rank, 2 * rank), 0)
    column_index = lax.broadcasted_iota(jnp.int32, (rank, 2 * rank), 1)
    unit = 1.0 / jnp.max(jnp.abs(spectrum), keepdims=True)
    gram_real = gram(straight) * unit * unit
    gram_imag = gram(turned) * unit * unit
    gram_real = jnp.where(row_index == column_index, 1.0, gram_real)

    def partner(a):
        k1 = own - a
        valid = jnp.logical_and(k1 >= 0, k1 < span1).astype(jnp.float32)
        return jnp.clip(k1, 0, span1 - 1), valid

    def own_columns(a):
        k1, _ = partner(a)
        for piece in range(pieces):
            cache = {}

            def cached_x(l1, g2):
                if not small:
                    return load_x(l1 + k1, g2, piece)
                if (l1, g2) not in cache:
                    cache[l1, g2] = load_x(l1 + k1, g2, piece)
                return cache[l1, g2]

            def column_tile(tile, carry):
                zero = jnp.zeros((8, LANES), jnp.float32)

                def first_keep(l1, sums):
                    sums = list(sums)
                    for l2 in range(keep2):
                        start = (l1 * keep2 + l2) * rank + tile * 8
                        s_real = bhat[rows(start), lanes(0, piece)]
                        s_imag = bhat[rows(start), lanes(1, piece)]
                        for k2 in range(span2):
                            x_real, x_imag = cached_x(l1, l2 + k2)
                            real, imag = sums[k2]
                            sums[k2] = (
                                real + (s_real * x_real + s_imag * x_imag),
                                imag + (s_real * x_imag - s_imag * x_real),
                            )
                    return tuple(sums)

                sums = sweep(keep1, first_keep, ((zero, zero),) * span2)
                for k2 in range(span2):
                    for part in range(2):
                        start = (part * span2 + k2) * rank + tile * 8
                        dhat[rows(start), pl.ds(piece * LANES, LANES)] = sums[k2][part]
                return carry

            if small:
                for tile in range(tiles):
                    column_tile(tile, 0)
                    yield
            else:
                sweep(tiles, column_tile, 0)
        dhat[...] = wide_dot(dhat[...], window_high[...], window_low[...])
        yield

    def own_planes(a):
        _, valid = partner(a)
        for piece in range(pieces):

            def rebuild_tile(tile, sums):
                sums = list(sums)
                us = []
                for l2 in range(keep2):
                    start = (a * keep2 + l2) * rank + tile * 8
                    us.append(
                        (
                            uhat[rows(start), lanes(0, piece)],
                            uhat[rows(start), lanes(1, piece)],
                        )
                    )
                for k2 in range(span2):
                    d_real = dhat[rows(k2 * rank + tile * 8), pl.ds(piece * LANES, LANES)]
                    d_imag = dhat[
                        rows((span2 + k2) * rank + tile * 8), pl.ds(piece * LANES, LANES)
                    ]
                    for l2 in range(keep2):
                        u_real, u_imag = us[l2]
                        real, imag = sums[l2 + k2]
                        sums[l2 + k2] = (
                            real + (u_real * d_real - u_imag * d_imag),
                            imag + (u_real * d_imag + u_imag * d_real),
                        )
                return tuple(sums)

            zero = jnp.zeros((8, LANES), jnp.float32)
            sums = sweep(tiles, rebuild_tile, ((zero, zero),) * second)
            for part in range(2):
                summed = jnp.concatenate(
                    [jnp.sum(sums[g2][part], 0, keepdims=True) for g2 in range(second)], 0
                )
                place = pl.ds(piece * LANES, LANES)
                where = pl.ds(part * second, second)
                ghat[where, place] = ghat[where, place] + summed * valid

    def own_basis():
        bhat[...] = wide_dot(sketch[:, : 2 * ROWS], basis_high[...], basis_low[...])
        yield
        if small:
            yield from own_columns(0)

    inverse = []
    interleave(invert(gram_real, gram_imag, inverse), own_basis())
    mixer = jnp.concatenate(inverse, 0) * unit * unit

    def mix(b, carry):
        where = rows(b * rank, rank)
        both = jnp.dot(
            mixer, bhat[where, :], precision=highest, preferred_element_type=jnp.float32
        )
        uhat[where, :half] = both[:rank, :half] + both[rank:, half:]
        uhat[where, half:] = both[:rank, half:] - both[rank:, :half]
        return carry

    sweep(blocks, mix, 0)
    ghat[...] = jnp.zeros_like(ghat)

    def own_pair(a, carry):
        if not (small and isinstance(a, int) and a == 0):
            for _ in own_columns(a):
                pass
        own_planes(a)
        return carry

    sweep(keep1, own_pair, 0)

    both = wide_dot(ghat[...], back_high[...], back_low[...])
    real = both[:second, :half] - both[second:, half:]
    imag = both[:second, half:] + both[second:, :half]
    weight = weight_ref[pl.ds(pl.multiple_of(own * second, 8), second), :]
    real = real * weight
    imag = imag * weight
    here = lax.axis_index("wide")
    for w in range(second):
        offset = jnp.bitwise_xor(here, w)
        slot = (offset % 2) * (second // 2) + offset // 2
        for piece in range(pieces):
            place = slice(piece * LANES, (piece + 1) * LANES)
            sends[slot, pl.ds(piece, 1), :] = real[w : w + 1, place]
            sends[slot, pl.ds(pieces + piece, 1), :] = imag[w : w + 1, place]
    out_ref[...] = sends[: second // 2]
    handed_ref[...] = sends[second // 2 :]


def synthesis_kernel(*refs):
    *block_refs, table_ref, out_ref, out, cells, sems = refs
    here = lax.axis_index("wide")
    for i in range(len(block_refs)):
        for j in range(2):
            cells[jnp.bitwise_xor(here, 2 * i + j)] = block_refs[i][j]
    parts = [
        jnp.concatenate([cells[:, part * PIECES + piece, :] for piece in range(PIECES)], 1)
        for part in range(2)
    ]
    high, low = split(jnp.concatenate(parts, 0))
    stacked = jnp.concatenate([high, low, high], 0)
    contract = (((0,), (0,)), ((), ()))
    chunks, width, _ = out.shape
    copies = []
    for i in range(chunks):
        out[i] = lax.dot_general(
            stacked[:, i * width : (i + 1) * width],
            table_ref[...],
            contract,
            preferred_element_type=jnp.float32,
        )
        copies.append(
            pltpu.make_async_copy(out.at[i], out_ref.at[pl.ds(i * width, width)], sems.at[i])
        )
        copies[-1].start()
    for copy in copies:
        copy.wait()


def per_device(traces, mask, omega):
    narrow_count = lax.axis_size("narrow")
    wide_count = lax.axis_size("wide")
    assert traces.shape[:2] == (1, 1)
    first, second = narrow_count, wide_count
    freq_total = FREQ_DEV * wide_count
    keep1, keep2 = first // 2, second // 2
    span1, span2 = first - keep1 + 1, second - keep2 + 1
    rank = omega.shape[0] * narrow_count
    dests = wide_count * narrow_count
    lines = 2 * PIECES

    omegas = [omega]
    for step in range(1, narrow_count):
        ring = [(i, (i + step) % narrow_count) for i in range(narrow_count)]
        omegas.append(lax.ppermute(omega, "narrow", ring))

    order = [(3 * dests // 4 - 1 - i) % dests for i in range(dests)]
    high, low = halves(spectrum_table(freq_total, [i // narrow_count for i in order]))
    blocks = pl.pallas_call(
        spectrum_kernel,
        out_shape=jax.ShapeDtypeStruct((dests, lines, LANES), jnp.float32),
        in_specs=[HBM] * 3,
        out_specs=VMEM,
        scratch_shapes=[
            pltpu.VMEM((CHUNKS, CELLS, S // CHUNKS), jnp.float32),
            pltpu.VMEM((1, CELLS), jnp.int32),
            pltpu.VMEM((4 * dests, S), jnp.bfloat16),
            pltpu.SemaphoreType.DMA((2 + CHUNKS,)),
        ],
        name="spectrum",
    )(traces.reshape(CELLS, S), mask.reshape(1, CELLS), np.concatenate([high, low], 0))
    grid = lax.all_to_all(
        blocks,
        ("wide", "narrow"),
        split_axis=0,
        concat_axis=0,
        axis_index_groups=[order],
        tiled=True,
    )

    if omega.shape[0] % 8:
        omegas = [jnp.concatenate(omegas, 0)]
    columns = span1 * span2
    omega_hat = pl.pallas_call(
        functools.partial(omega_kernel, columns),
        out_shape=jax.ShapeDtypeStruct((columns * rank, 2 * CELLS), jnp.float32),
        in_specs=[VMEM] * (len(omegas) + 2),
        out_specs=VMEM,
        cost_estimate=pl.CostEstimate(
            flops=6 * columns * rank * LANES * 2 * CELLS,
            bytes_accessed=4 * columns * rank * 2 * CELLS,
            transcendentals=0,
        ),
        compiler_params=pltpu.CompilerParams(vmem_limit_bytes=16 * MIB),
        name="omega",
    )(*omegas, *halves(omega_table()))

    angles = centred_angles()
    counts = (
        correlation(first, keep1)[:, None, None]
        * correlation(second, keep2)[None, :, None]
        * np.outer(correlation(G3, KEEP3), correlation(G4, KEEP4)).reshape(1, 1, CELLS)
    ).reshape(first * second, CELLS)
    forward = np.concatenate([np.cos(angles), np.sin(angles)], 1)
    backward = np.concatenate([np.cos(angles.T), np.sin(angles.T)], 1) / CELLS
    tables = (
        *halves(forward),
        *halves(sketch_table()),
        *halves(basis_table()),
        *halves(window_table()),
        *halves(backward),
        (1.0 / counts).astype(np.float32),
    )
    area = keep1 * keep2 * rank
    scratch = [
        (first * second, lines, 8, LANES),
        (area, 2 * CELLS),
        (area, 2 * CELLS),
        (area, 2 * CELLS),
        (2 * span2 * rank, CELLS),
        (2 * second, CELLS),
        (second, lines, LANES),
    ]
    chips = second // 2
    kept, handed = pl.pallas_call(
        functools.partial(core_kernel, (first, second, rank), order),
        out_shape=[jax.ShapeDtypeStruct((chips, lines, LANES), jnp.float32)] * 2,
        in_specs=[VMEM] * (2 + len(tables)),
        out_specs=[VMEM] * 2,
        scratch_shapes=[pltpu.VMEM(shape, jnp.float32) for shape in scratch],
        compiler_params=pltpu.CompilerParams(vmem_limit_bytes=24 * MIB),
        name="core",
    )(grid, omega_hat, *tables)

    def across(value, offset):
        return lax.ppermute(value, "wide", [(i, i ^ offset) for i in range(second)])

    handed = across(handed, 1)
    joined = jnp.stack([kept, handed], 1)
    returned = [joined[0]] + [across(joined[i], 2 * i) for i in range(1, chips)]

    high, low = halves(synthesis_table(freq_total))
    filtered = pl.pallas_call(
        synthesis_kernel,
        out_shape=jax.ShapeDtypeStruct((CELLS, S), jnp.float32),
        in_specs=[VMEM] * (chips + 1),
        out_specs=HBM,
        scratch_shapes=[
            pltpu.VMEM((PIECES, LANES, S), jnp.float32),
            pltpu.VMEM((second, lines, LANES), jnp.float32),
            pltpu.SemaphoreType.DMA((PIECES,)),
        ],
        compiler_params=pltpu.CompilerParams(vmem_limit_bytes=8 * MIB),
        name="synthesis",
    )(*returned, np.concatenate([high, high, low], 0))
    return filtered.reshape(traces.shape)


def solution(mesh):
    return jax.shard_map(
        per_device,
        mesh=mesh,
        in_specs=(
            P(("win", "narrow"), "wide", None, None),
            P(("win", "narrow"), "wide", None),
            P("narrow", None),
        ),
        out_specs=P(("win", "narrow"), "wide", None, None),
        check_vma=False,
    )
```

```python
import functools
import math

import jax
import jax.numpy as jnp
import ml_dtypes
import numpy as np
from jax import lax
from jax.experimental import pallas as pl
from jax.experimental.pallas import tpu as pltpu
from jax.sharding import PartitionSpec as P

G3 = 16
G4 = 16
S = 1024
FREQ_DEV = 1
FIRST_BIN = 16
LANES = 128
MIB = 1 << 20
CHUNKS = 2
PIVOTS = 4
CELLS = G3 * G4
KEEP3, KEEP4 = G3 // 2, G4 // 2
SPAN3, SPAN4 = G3 - KEEP3 + 1, G4 - KEEP4 + 1
SHIFT3, SHIFT4 = (SPAN3 - 1) // 2, (SPAN4 - 1) // 2
ROWS = KEEP3 * KEEP4
COLS = SPAN3 * SPAN4
PIECES = CELLS // LANES

HBM = pl.BlockSpec(memory_space=pltpu.HBM)
VMEM = pl.BlockSpec(memory_space=pltpu.VMEM)
highest = lax.Precision.HIGHEST


def halves(table):
    table = np.asarray(table, np.float32)
    high = table.astype(ml_dtypes.bfloat16)
    low = (table - high.astype(np.float32)).astype(ml_dtypes.bfloat16)
    return high, low


def phases(freq_total):
    bins = FIRST_BIN + np.arange(freq_total)
    return 2.0 * np.pi * ((bins[:, None] * np.arange(S)[None, :]) % S) / S


def cell_angles(positions3, positions4):
    wave = np.arange(CELLS)
    turns = (
        np.outer(positions3, wave // G4) % G3 / G3 + np.outer(positions4, wave % G4) % G4 / G4
    )
    return 2.0 * np.pi * turns


def correlation(length, keep_size):
    position = np.arange(length)
    span_size = length - keep_size + 1
    return (
        np.minimum(position, keep_size - 1) - np.maximum(position - span_size + 1, 0) + 1
    ).astype(np.float64)


def spectrum_table(freq_total, owners):
    angles = phases(freq_total)[owners]
    return np.concatenate([np.cos(angles), -np.sin(angles)], 0) / math.sqrt(S)


def synthesis_table(freq_total, order):
    angles = phases(freq_total)[order]
    return np.concatenate([np.cos(angles), -np.sin(angles)], 0) * math.sqrt(2.0 / freq_total)


def centred_angles():
    cell = np.arange(CELLS)
    return cell_angles(cell // G4 - SHIFT3, cell % G4 - SHIFT4)


def omega_table():
    column = np.arange(COLS)
    angles = cell_angles(column // SPAN4, column % SPAN4)
    table = np.zeros((LANES, 2 * CELLS))
    table[:COLS] = np.concatenate([np.cos(angles), -np.sin(angles)], 1)
    return table


def sketch_table():
    row = np.arange(ROWS)
    angles = cell_angles(row // KEEP4 - SHIFT3, row % KEEP4 - SHIFT4).T
    real, imag = np.cos(angles) / CELLS, np.sin(angles) / CELLS
    from_real = np.concatenate([real, imag, imag, -real], 1)
    from_imag = np.concatenate([-imag, real, real, imag], 1)
    return np.concatenate([from_real, from_imag], 0)


def basis_table():
    row = np.arange(ROWS)
    angles = cell_angles(row // KEEP4, row % KEEP4)
    real, imag = np.cos(angles), np.sin(angles)
    return np.concatenate(
        [np.concatenate([real, -imag], 1), np.concatenate([imag, real], 1)], 0
    )


def window_table():
    parts = []
    for length, shift in ((G3, SHIFT3), (G4, SHIFT4)):
        wave = np.arange(length)
        turns = (wave[:, None] - wave[None, :])[:, :, None] * np.arange(-shift, shift + 1) / length
        parts.append(np.cos(2.0 * np.pi * turns).sum(-1) / length)
    return np.kron(parts[0], parts[1])


def split(value):
    high = value.astype(jnp.bfloat16)
    low = (value - high.astype(jnp.float32)).astype(jnp.bfloat16)
    return high, low


def dot(left, right):
    return jnp.dot(left, right, preferred_element_type=jnp.float32)


def wide_dot(value, high, low):
    rows = value.shape[0]
    value_high, value_low = split(value)
    main = dot(jnp.concatenate([value_high, value_low], 0), high)
    return main[:rows] + (main[rows:] + dot(value_high, low))


def spectrum_kernel(traces_ref, mask_ref, table_ref, out_ref, traces, mask, table, sems):
    rows = table.shape[0] // 2
    dests = rows // 2
    chunks, _, width = traces.shape
    copies = [
        pltpu.make_async_copy(table_ref, table, sems.at[0]),
        pltpu.make_async_copy(mask_ref, mask, sems.at[1]),
    ] + [
        pltpu.make_async_copy(
            traces_ref.at[:, pl.ds(i * width, width)], traces.at[i], sems.at[2 + i]
        )
        for i in range(chunks)
    ]
    for copy in copies:
        copy.start()
    copies[0].wait()
    contract = (((1,), (1,)), ((), ()))
    total = jnp.zeros((2 * rows, CELLS), jnp.float32)
    rest = jnp.zeros((rows, CELLS), jnp.float32)
    for i in range(chunks):
        copies[2 + i].wait()
        high, low = split(traces[i])
        place = pl.ds(i * width, width)
        total += lax.dot_general(
            table[:, place], high, contract, preferred_element_type=jnp.float32
        )
        rest += lax.dot_general(
            table[:rows, place], low, contract, preferred_element_type=jnp.float32
        )
    copies[1].wait()
    result = (total[:rows] + (total[rows:] + rest)) * mask[...].astype(jnp.float32)
    for part in range(2):
        for piece in range(PIECES):
            out_ref[:, part * PIECES + piece, :] = result[
                part * dests : (part + 1) * dests, piece * LANES : (piece + 1) * LANES
            ]


def omega_kernel(columns, *refs):
    omega_refs = refs[:-3]
    high_ref, low_ref, out_ref = refs[-3:]
    omega = jnp.concatenate([ref[...] for ref in omega_refs], 0)
    pad = jnp.zeros((omega.shape[0], LANES - COLS), jnp.float32)
    blocks = [
        jnp.concatenate([omega[:, k * COLS : (k + 1) * COLS], pad], 1) for k in range(columns)
    ]
    out_ref[...] = wide_dot(jnp.concatenate(blocks, 0), high_ref[...], low_ref[...])


def minus_product(value, left, right):
    return (
        value[0] - (left[0] * right[0] - left[1] * right[1]),
        value[1] - (left[0] * right[1] + left[1] * right[0]),
    )


def pivot_pair(upper, lower, corner, other, cross, scale):
    turned = (cross[0], -cross[1])
    first = minus_product(tuple(other * v for v in upper), cross, lower)
    second = minus_product(tuple(corner * v for v in lower), turned, upper)
    return tuple(v * scale for v in first), tuple(v * scale for v in second)


def invert(real, imag, result):
    size = real.shape[0]
    width = 2 * size
    tiles = [(real[t : t + 8], imag[t : t + 8]) for t in range(0, size, 8)]
    sublane = lax.broadcasted_iota(jnp.int32, (8, width), 0)
    for start in range(0, size, PIVOTS):
        home, at = start // 8, start % 8
        lane = size + start

        def spread(value, b, height):
            return jnp.broadcast_to(value[:, lane + b : lane + b + 1], (height, width))

        rows = [tuple(v[at + a : at + a + 1] for v in tiles[home]) for a in range(PIVOTS)]
        block = {}
        for a in range(PIVOTS):
            block[a, a] = (spread(rows[a][0], a, 1),)
            for b in range(a + 1, PIVOTS):
                block[a, b] = tuple(spread(v, b, 1) for v in rows[a])
                block[b, a] = (block[a, b][0], -block[a, b][1])
        columns = [
            [tuple(spread(v, b, 8) for v in tile) for b in range(PIVOTS)] for tile in tiles
        ]
        for p in range(0, PIVOTS, 2):
            q = p + 1
            corner, other, cross = block[p, p][0], block[q, q][0], block[p, q]
            scale = 1.0 / (corner * other - (cross[0] * cross[0] + cross[1] * cross[1]))
            pair = (corner, other, cross, scale)
            rows[p], rows[q] = pivot_pair(rows[p], rows[q], *pair)
            later = range(p + 2, PIVOTS)
            done = {}
            for c in later:
                done[p, c], done[q, c] = pivot_pair(block[p, c], block[q, c], *pair)
            for o in range(PIVOTS):
                if o in (p, q):
                    continue
                left, right = block[o, p], block[o, q]
                rows[o] = minus_product(minus_product(rows[o], left, rows[p]), right, rows[q])
                for c in later:
                    if o == c:
                        first, second = done[p, c], done[q, c]
                        value = block[o, o][0]
                        value = value - (left[0] * first[0] - left[1] * first[1])
                        value = value - (right[0] * second[0] - right[1] * second[1])
                        done[o, o] = (value,)
                    elif o < c:
                        value = minus_product(block[o, c], left, done[p, c])
                        done[o, c] = minus_product(value, right, done[q, c])
                        if o > q:
                            done[c, o] = (done[o, c][0], -done[o, c][1])
            block.update(done)
        for t in range(len(tiles)):
            tile = tiles[t]
            for b in range(PIVOTS):
                tile = minus_product(tile, columns[t][b], rows[b])
            if t == home:
                for b in range(PIVOTS):
                    here = sublane == at + b
                    tile = tuple(jnp.where(here, rows[b][k], tile[k]) for k in range(2))
            tiles[t] = tile
        yield
    for part in range(2):
        result.append(jnp.concatenate([tile[part] for tile in tiles], 0)[:, :size])


def interleave(*steps):
    steps = list(steps)
    while steps:
        steps = [step for step in steps if next(step, steps) is not steps]


def core_kernel(
    dims,
    order,
    back_order,
    x_ref,
    omega_ref,
    analysis_high,
    analysis_low,
    sketch_high,
    sketch_low,
    basis_high,
    basis_low,
    window_high,
    window_low,
    back_high,
    back_low,
    weight_ref,
    out_ref,
    xhat,
    shat,
    bhat,
    uhat,
    dhat,
    ghat,
):
    first, second, rank = dims
    keep1, keep2 = first // 2, second // 2
    span1, span2 = first - keep1 + 1, second - keep2 + 1
    own = lax.axis_index("narrow")
    half = CELLS
    tiles = rank // 8
    pieces = CELLS // LANES
    small = keep1 * keep2 * span1 * span2 <= 64

    def sweep(count, body, carry):
        if small:
            for i in range(count):
                carry = body(i, carry)
            return carry
        return lax.fori_loop(0, count, body, carry)

    def rows(start, count=8):
        if isinstance(start, int):
            return pl.ds(start, count)
        return pl.ds(pl.multiple_of(start, 8), count)

    def lanes(part, piece):
        start = part * half + piece * LANES
        return pl.ds(start, LANES)

    planes = first * second
    spectrum = jnp.concatenate(
        [
            jnp.concatenate([x_ref[:, part * pieces + piece, :] for piece in range(pieces)], 1)
            for part in range(2)
        ],
        0,
    )
    both = wide_dot(spectrum, analysis_high[...], analysis_low[...])
    hats = (
        both[:planes, :half] + both[planes:, half:],
        both[planes:, :half] - both[:planes, half:],
    )
    for part in range(2):
        for piece in range(pieces):
            values = hats[part][:, piece * LANES : (piece + 1) * LANES]
            for p in range(planes):
                xhat[order[p], part * pieces + piece] = jnp.broadcast_to(
                    values[p : p + 1], (8, LANES)
                )

    def load_x(g1, g2, piece):
        row = g2 * first + g1
        return xhat[row, piece], xhat[row, pieces + piece]

    for piece in range(pieces):
        cache = {}

        def cached_x(g1, g2):
            if not small:
                return load_x(g1, g2, piece)
            if (g1, g2) not in cache:
                cache[g1, g2] = load_x(g1, g2, piece)
            return cache[g1, g2]

        def sketch_tile(tile, carry):
            def first_keep(l1, carry):
                zero = jnp.zeros((8, LANES), jnp.float32)

                def columns(k1, sums):
                    def column(k2, sums):
                        start = (k1 * span2 + k2) * rank + tile * 8
                        w_real = omega_ref[rows(start), lanes(0, piece)]
                        w_imag = omega_ref[rows(start), lanes(1, piece)]
                        sums = list(sums)
                        for l2 in range(keep2):
                            x_real, x_imag = cached_x(l1 + k1, l2 + k2)
                            real, imag = sums[l2]
                            sums[l2] = (
                                real + (x_real * w_real + x_imag * w_imag),
                                imag + (x_imag * w_real - x_real * w_imag),
                            )
                        return tuple(sums)

                    return sweep(span2, column, sums)

                sums = sweep(span1, columns, ((zero, zero),) * keep2)
                for l2 in range(keep2):
                    start = (l1 * keep2 + l2) * rank + tile * 8
                    shat[rows(start), lanes(0, piece)] = sums[l2][0]
                    shat[rows(start), lanes(1, piece)] = sums[l2][1]
                return carry

            return sweep(keep1, first_keep, carry)

        sweep(tiles, sketch_tile, 0)

    blocks = keep1 * keep2
    sketch = wide_dot(shat[...], sketch_high[...], sketch_low[...])
    straight = jnp.concatenate(
        [sketch[b * rank : (b + 1) * rank, : 2 * ROWS] for b in range(blocks)], 1
    )
    turned = jnp.concatenate(
        [sketch[b * rank : (b + 1) * rank, 2 * ROWS :] for b in range(blocks)], 1
    )
    contract = (((1,), (1,)), ((), ()))
    space = jnp.zeros_like(straight)

    def gram(right):
        return lax.dot_general(
            straight,
            jnp.concatenate([space, right], 0),
            contract,
            precision=highest,
            preferred_element_type=jnp.float32,
        )

    row_index = lax.broadcasted_iota(jnp.int32, (rank, 2 * rank), 0)
    column_index = lax.broadcasted_iota(jnp.int32, (rank, 2 * rank), 1)
    unit = 1.0 / jnp.max(jnp.abs(spectrum), keepdims=True)
    gram_real = gram(straight) * unit * unit
    gram_imag = gram(turned) * unit * unit
    gram_real = jnp.where(row_index == column_index, 1.0, gram_real)

    def partner(a):
        k1 = own - a
        valid = jnp.logical_and(k1 >= 0, k1 < span1).astype(jnp.float32)
        return jnp.clip(k1, 0, span1 - 1), valid

    def own_columns(a):
        k1, _ = partner(a)
        for piece in range(pieces):
            cache = {}

            def cached_x(l1, g2):
                if not small:
                    return load_x(l1 + k1, g2, piece)
                if (l1, g2) not in cache:
                    cache[l1, g2] = load_x(l1 + k1, g2, piece)
                return cache[l1, g2]

            def column_tile(tile, carry):
                zero = jnp.zeros((8, LANES), jnp.float32)

                def first_keep(l1, sums):
                    sums = list(sums)
                    for l2 in range(keep2):
                        start = (l1 * keep2 + l2) * rank + tile * 8
                        s_real = bhat[rows(start), lanes(0, piece)]
                        s_imag = bhat[rows(start), lanes(1, piece)]
                        for k2 in range(span2):
                            x_real, x_imag = cached_x(l1, l2 + k2)
                            real, imag = sums[k2]
                            sums[k2] = (
                                real + (s_real * x_real + s_imag * x_imag),
                                imag + (s_real * x_imag - s_imag * x_real),
                            )
                    return tuple(sums)

                sums = sweep(keep1, first_keep, ((zero, zero),) * span2)
                for k2 in range(span2):
                    for part in range(2):
                        start = (part * span2 + k2) * rank + tile * 8
                        dhat[rows(start), pl.ds(piece * LANES, LANES)] = sums[k2][part]
                return carry

            if small:
                for tile in range(tiles):
                    column_tile(tile, 0)
                    yield
            else:
                sweep(tiles, column_tile, 0)
        dhat[...] = wide_dot(dhat[...], window_high[...], window_low[...])
        yield

    def own_planes(a):
        _, valid = partner(a)
        for piece in range(pieces):

            def rebuild_tile(tile, sums):
                sums = list(sums)
                us = []
                for l2 in range(keep2):
                    start = (a * keep2 + l2) * rank + tile * 8
                    us.append(
                        (
                            uhat[rows(start), lanes(0, piece)],
                            uhat[rows(start), lanes(1, piece)],
                        )
                    )
                for k2 in range(span2):
                    d_real = dhat[rows(k2 * rank + tile * 8), pl.ds(piece * LANES, LANES)]
                    d_imag = dhat[
                        rows((span2 + k2) * rank + tile * 8), pl.ds(piece * LANES, LANES)
                    ]
                    for l2 in range(keep2):
                        u_real, u_imag = us[l2]
                        real, imag = sums[l2 + k2]
                        sums[l2 + k2] = (
                            real + (u_real * d_real - u_imag * d_imag),
                            imag + (u_real * d_imag + u_imag * d_real),
                        )
                return tuple(sums)

            zero = jnp.zeros((8, LANES), jnp.float32)
            sums = sweep(tiles, rebuild_tile, ((zero, zero),) * second)
            for part in range(2):
                summed = jnp.concatenate(
                    [jnp.sum(sums[g2][part], 0, keepdims=True) for g2 in range(second)], 0
                )
                place = pl.ds(piece * LANES, LANES)
                where = pl.ds(part * second, second)
                ghat[where, place] = ghat[where, place] + summed * valid

    def own_basis():
        bhat[...] = wide_dot(sketch[:, : 2 * ROWS], basis_high[...], basis_low[...])
        yield
        if small:
            yield from own_columns(0)

    inverse = []
    interleave(invert(gram_real, gram_imag, inverse), own_basis())
    mixer = jnp.concatenate(inverse, 0) * unit * unit

    def mix(b, carry):
        where = rows(b * rank, rank)
        both = jnp.dot(
            mixer, bhat[where, :], precision=highest, preferred_element_type=jnp.float32
        )
        uhat[where, :half] = both[:rank, :half] + both[rank:, half:]
        uhat[where, half:] = both[:rank, half:] - both[rank:, :half]
        return carry

    sweep(blocks, mix, 0)
    ghat[...] = jnp.zeros_like(ghat)

    def own_pair(a, carry):
        if not (small and isinstance(a, int) and a == 0):
            for _ in own_columns(a):
                pass
        own_planes(a)
        return carry

    sweep(keep1, own_pair, 0)

    both = wide_dot(ghat[...], back_high[...], back_low[...])
    real = both[:second, :half] - both[second:, half:]
    imag = both[:second, half:] + both[second:, :half]
    weight = weight_ref[pl.ds(pl.multiple_of(own * second, 8), second), :]
    real = real * weight
    imag = imag * weight
    for j in range(second):
        row = slice(back_order[j], back_order[j] + 1)
        for piece in range(pieces):
            place = slice(piece * LANES, (piece + 1) * LANES)
            out_ref[j, pl.ds(piece, 1), :] = real[row, place]
            out_ref[j, pl.ds(pieces + piece, 1), :] = imag[row, place]


def synthesis_kernel(cells_ref, table_ref, out_ref, out, sems):
    parts = [
        jnp.concatenate([cells_ref[:, part * PIECES + piece, :] for piece in range(PIECES)], 1)
        for part in range(2)
    ]
    high, low = split(jnp.concatenate(parts, 0))
    stacked = jnp.concatenate([high, low, high], 0)
    contract = (((0,), (0,)), ((), ()))
    chunks, width, _ = out.shape
    copies = []
    for i in range(chunks):
        out[i] = lax.dot_general(
            stacked[:, i * width : (i + 1) * width],
            table_ref[...],
            contract,
            preferred_element_type=jnp.float32,
        )
        copies.append(
            pltpu.make_async_copy(out.at[i], out_ref.at[pl.ds(i * width, width)], sems.at[i])
        )
        copies[-1].start()
    for copy in copies:
        copy.wait()


def group_order(count):
    return [(3 * count // 4 - 1 - i) % count for i in range(count)]


def per_device(traces, mask, omega):
    narrow_count = lax.axis_size("narrow")
    wide_count = lax.axis_size("wide")
    assert traces.shape[:2] == (1, 1)
    first, second = narrow_count, wide_count
    freq_total = FREQ_DEV * wide_count
    keep1, keep2 = first // 2, second // 2
    span1, span2 = first - keep1 + 1, second - keep2 + 1
    rank = omega.shape[0] * narrow_count
    dests = wide_count * narrow_count
    lines = 2 * PIECES

    omegas = [omega]
    for step in range(1, narrow_count):
        ring = [(i, (i + step) % narrow_count) for i in range(narrow_count)]
        omegas.append(lax.ppermute(omega, "narrow", ring))

    order = group_order(dests)
    high, low = halves(spectrum_table(freq_total, [i // narrow_count for i in order]))
    blocks = pl.pallas_call(
        spectrum_kernel,
        out_shape=jax.ShapeDtypeStruct((dests, lines, LANES), jnp.float32),
        in_specs=[HBM] * 3,
        out_specs=VMEM,
        scratch_shapes=[
            pltpu.VMEM((CHUNKS, CELLS, S // CHUNKS), jnp.float32),
            pltpu.VMEM((1, CELLS), jnp.int32),
            pltpu.VMEM((4 * dests, S), jnp.bfloat16),
            pltpu.SemaphoreType.DMA((2 + CHUNKS,)),
        ],
        name="spectrum",
    )(traces.reshape(CELLS, S), mask.reshape(1, CELLS), np.concatenate([high, low], 0))
    grid = lax.all_to_all(
        blocks,
        ("wide", "narrow"),
        split_axis=0,
        concat_axis=0,
        axis_index_groups=[order],
        tiled=True,
    )

    if omega.shape[0] % 8:
        omegas = [jnp.concatenate(omegas, 0)]
    columns = span1 * span2
    omega_hat = pl.pallas_call(
        functools.partial(omega_kernel, columns),
        out_shape=jax.ShapeDtypeStruct((columns * rank, 2 * CELLS), jnp.float32),
        in_specs=[VMEM] * (len(omegas) + 2),
        out_specs=VMEM,
        cost_estimate=pl.CostEstimate(
            flops=6 * columns * rank * LANES * 2 * CELLS,
            bytes_accessed=4 * columns * rank * 2 * CELLS,
            transcendentals=0,
        ),
        compiler_params=pltpu.CompilerParams(vmem_limit_bytes=16 * MIB),
        name="omega",
    )(*omegas, *halves(omega_table()))

    angles = centred_angles()
    counts = (
        correlation(first, keep1)[:, None, None]
        * correlation(second, keep2)[None, :, None]
        * np.outer(correlation(G3, KEEP3), correlation(G4, KEEP4)).reshape(1, 1, CELLS)
    ).reshape(first * second, CELLS)
    forward = np.concatenate([np.cos(angles), np.sin(angles)], 1)
    backward = np.concatenate([np.cos(angles.T), np.sin(angles.T)], 1) / CELLS
    tables = (
        *halves(forward),
        *halves(sketch_table()),
        *halves(basis_table()),
        *halves(window_table()),
        *halves(backward),
        (1.0 / counts).astype(np.float32),
    )
    area = keep1 * keep2 * rank
    scratch = [
        (first * second, lines, 8, LANES),
        (area, 2 * CELLS),
        (area, 2 * CELLS),
        (area, 2 * CELLS),
        (2 * span2 * rank, CELLS),
        (2 * second, CELLS),
    ]
    back_order = group_order(second)
    rebuilt = pl.pallas_call(
        functools.partial(core_kernel, (first, second, rank), order, back_order),
        out_shape=jax.ShapeDtypeStruct((second, lines, LANES), jnp.float32),
        in_specs=[VMEM] * (2 + len(tables)),
        out_specs=VMEM,
        scratch_shapes=[pltpu.VMEM(shape, jnp.float32) for shape in scratch],
        compiler_params=pltpu.CompilerParams(vmem_limit_bytes=24 * MIB),
        name="core",
    )(grid, omega_hat, *tables)
    returned = lax.all_to_all(
        rebuilt,
        "wide",
        split_axis=0,
        concat_axis=0,
        axis_index_groups=[back_order],
        tiled=True,
    )

    high, low = halves(synthesis_table(freq_total, back_order))
    filtered = pl.pallas_call(
        synthesis_kernel,
        out_shape=jax.ShapeDtypeStruct((CELLS, S), jnp.float32),
        in_specs=[VMEM] * 2,
        out_specs=HBM,
        scratch_shapes=[
            pltpu.VMEM((PIECES, LANES, S), jnp.float32),
            pltpu.SemaphoreType.DMA((PIECES,)),
        ],
        compiler_params=pltpu.CompilerParams(vmem_limit_bytes=8 * MIB),
        name="synthesis",
    )(returned, np.concatenate([high, high, low], 0))
    return filtered.reshape(traces.shape)


def solution(mesh):
    return jax.shard_map(
        per_device,
        mesh=mesh,
        in_specs=(
            P(("win", "narrow"), "wide", None, None),
            P(("win", "narrow"), "wide", None),
            P("narrow", None),
        ),
        out_specs=P(("win", "narrow"), "wide", None, None),
        check_vma=False,
    )
```

```python
import functools
import math

import jax
import jax.numpy as jnp
import ml_dtypes
import numpy as np
from jax import lax
from jax.experimental import pallas as pl
from jax.experimental.pallas import tpu as pltpu
from jax.sharding import PartitionSpec as P

G3 = 16
G4 = 16
S = 1024
FREQ_DEV = 1
FIRST_BIN = 16
LANES = 128
MIB = 1 << 20
CHUNKS = 2
PIVOTS = 4
CELLS = G3 * G4
KEEP3, KEEP4 = G3 // 2, G4 // 2
SPAN3, SPAN4 = G3 - KEEP3 + 1, G4 - KEEP4 + 1
SHIFT3, SHIFT4 = (SPAN3 - 1) // 2, (SPAN4 - 1) // 2
ROWS = KEEP3 * KEEP4
COLS = SPAN3 * SPAN4
PIECES = CELLS // LANES

HBM = pl.BlockSpec(memory_space=pltpu.HBM)
VMEM = pl.BlockSpec(memory_space=pltpu.VMEM)
highest = lax.Precision.HIGHEST


def halves(table):
    table = np.asarray(table, np.float32)
    high = table.astype(ml_dtypes.bfloat16)
    low = (table - high.astype(np.float32)).astype(ml_dtypes.bfloat16)
    return high, low


def phases(freq_total):
    bins = FIRST_BIN + np.arange(freq_total)
    return 2.0 * np.pi * ((bins[:, None] * np.arange(S)[None, :]) % S) / S


def cell_angles(positions3, positions4):
    wave = np.arange(CELLS)
    turns = (
        np.outer(positions3, wave // G4) % G3 / G3 + np.outer(positions4, wave % G4) % G4 / G4
    )
    return 2.0 * np.pi * turns


def correlation(length, keep_size):
    position = np.arange(length)
    span_size = length - keep_size + 1
    return (
        np.minimum(position, keep_size - 1) - np.maximum(position - span_size + 1, 0) + 1
    ).astype(np.float64)


def spectrum_table(freq_total, owners):
    angles = phases(freq_total)[owners]
    return np.concatenate([np.cos(angles), -np.sin(angles)], 0) / math.sqrt(S)


def synthesis_table(freq_total, order):
    angles = phases(freq_total)[order]
    return np.concatenate([np.cos(angles), -np.sin(angles)], 0) * math.sqrt(2.0 / freq_total)


def centred_angles():
    cell = np.arange(CELLS)
    return cell_angles(cell // G4 - SHIFT3, cell % G4 - SHIFT4)


def omega_table():
    column = np.arange(COLS)
    angles = cell_angles(column // SPAN4, column % SPAN4)
    table = np.zeros((LANES, 2 * CELLS))
    table[:COLS] = np.concatenate([np.cos(angles), -np.sin(angles)], 1)
    return table


def sketch_table():
    row = np.arange(ROWS)
    angles = cell_angles(row // KEEP4 - SHIFT3, row % KEEP4 - SHIFT4).T
    real, imag = np.cos(angles) / CELLS, np.sin(angles) / CELLS
    from_real = np.concatenate([real, imag, imag, -real], 1)
    from_imag = np.concatenate([-imag, real, real, imag], 1)
    return np.concatenate([from_real, from_imag], 0)


def basis_table():
    row = np.arange(ROWS)
    angles = cell_angles(row // KEEP4, row % KEEP4)
    real, imag = np.cos(angles), np.sin(angles)
    return np.concatenate(
        [np.concatenate([real, -imag], 1), np.concatenate([imag, real], 1)], 0
    )


def window_table():
    parts = []
    for length, shift in ((G3, SHIFT3), (G4, SHIFT4)):
        wave = np.arange(length)
        turns = (wave[:, None] - wave[None, :])[:, :, None] * np.arange(-shift, shift + 1) / length
        parts.append(np.cos(2.0 * np.pi * turns).sum(-1) / length)
    return np.kron(parts[0], parts[1])


def split(value):
    high = value.astype(jnp.bfloat16)
    low = (value - high.astype(jnp.float32)).astype(jnp.bfloat16)
    return high, low


def dot(left, right):
    return jnp.dot(left, right, preferred_element_type=jnp.float32)


def wide_dot(value, high, low):
    rows = value.shape[0]
    value_high, value_low = split(value)
    main = dot(jnp.concatenate([value_high, value_low], 0), high)
    return main[:rows] + (main[rows:] + dot(value_high, low))


def spectrum_kernel(traces_ref, mask_ref, table_ref, out_ref, traces, mask, table, sems):
    rows = table.shape[0] // 2
    dests = rows // 2
    chunks, _, width = traces.shape
    copies = [
        pltpu.make_async_copy(table_ref, table, sems.at[0]),
        pltpu.make_async_copy(mask_ref, mask, sems.at[1]),
    ] + [
        pltpu.make_async_copy(
            traces_ref.at[:, pl.ds(i * width, width)], traces.at[i], sems.at[2 + i]
        )
        for i in range(chunks)
    ]
    for copy in copies:
        copy.start()
    copies[0].wait()
    contract = (((1,), (1,)), ((), ()))
    total = jnp.zeros((2 * rows, CELLS), jnp.float32)
    rest = jnp.zeros((rows, CELLS), jnp.float32)
    for i in range(chunks):
        copies[2 + i].wait()
        high, low = split(traces[i])
        place = pl.ds(i * width, width)
        total += lax.dot_general(
            table[:, place], high, contract, preferred_element_type=jnp.float32
        )
        rest += lax.dot_general(
            table[:rows, place], low, contract, preferred_element_type=jnp.float32
        )
    copies[1].wait()
    result = (total[:rows] + (total[rows:] + rest)) * mask[...].astype(jnp.float32)
    for part in range(2):
        for piece in range(PIECES):
            out_ref[:, part * PIECES + piece, :] = result[
                part * dests : (part + 1) * dests, piece * LANES : (piece + 1) * LANES
            ]


def omega_kernel(columns, *refs):
    omega_refs = refs[:-3]
    high_ref, low_ref, out_ref = refs[-3:]
    omega = jnp.concatenate([ref[...] for ref in omega_refs], 0)
    pad = jnp.zeros((omega.shape[0], LANES - COLS), jnp.float32)
    blocks = [
        jnp.concatenate([omega[:, k * COLS : (k + 1) * COLS], pad], 1) for k in range(columns)
    ]
    hats = wide_dot(jnp.concatenate(blocks, 0), high_ref[...], low_ref[...])
    real, imag = hats[:, :CELLS], hats[:, CELLS:]
    out_ref[:, :CELLS] = real
    out_ref[:, CELLS : 2 * CELLS] = real - imag
    out_ref[:, 2 * CELLS :] = real + imag


def minus_product(value, left, right):
    return (
        value[0] - (left[0] * right[0] - left[1] * right[1]),
        value[1] - (left[0] * right[1] + left[1] * right[0]),
    )


def pivot_pair(upper, lower, corner, other, cross, scale):
    turned = (cross[0], -cross[1])
    first = minus_product(tuple(other * v for v in upper), cross, lower)
    second = minus_product(tuple(corner * v for v in lower), turned, upper)
    return tuple(v * scale for v in first), tuple(v * scale for v in second)


def invert(real, imag, result):
    size = real.shape[0]
    width = 2 * size
    tiles = [(real[t : t + 8], imag[t : t + 8]) for t in range(0, size, 8)]
    sublane = lax.broadcasted_iota(jnp.int32, (8, width), 0)
    for start in range(0, size, PIVOTS):
        home, at = start // 8, start % 8
        lane = size + start

        def spread(value, b, height):
            return jnp.broadcast_to(value[:, lane + b : lane + b + 1], (height, width))

        rows = [tuple(v[at + a : at + a + 1] for v in tiles[home]) for a in range(PIVOTS)]
        block = {}
        for a in range(PIVOTS):
            block[a, a] = (spread(rows[a][0], a, 1),)
            for b in range(a + 1, PIVOTS):
                block[a, b] = tuple(spread(v, b, 1) for v in rows[a])
                block[b, a] = (block[a, b][0], -block[a, b][1])
        columns = [
            [tuple(spread(v, b, 8) for v in tile) for b in range(PIVOTS)] for tile in tiles
        ]
        for p in range(0, PIVOTS, 2):
            q = p + 1
            corner, other, cross = block[p, p][0], block[q, q][0], block[p, q]
            scale = 1.0 / (corner * other - (cross[0] * cross[0] + cross[1] * cross[1]))
            pair = (corner, other, cross, scale)
            rows[p], rows[q] = pivot_pair(rows[p], rows[q], *pair)
            later = range(p + 2, PIVOTS)
            done = {}
            for c in later:
                done[p, c], done[q, c] = pivot_pair(block[p, c], block[q, c], *pair)
            for o in range(PIVOTS):
                if o in (p, q):
                    continue
                left, right = block[o, p], block[o, q]
                rows[o] = minus_product(minus_product(rows[o], left, rows[p]), right, rows[q])
                for c in later:
                    if o == c:
                        first, second = done[p, c], done[q, c]
                        value = block[o, o][0]
                        value = value - (left[0] * first[0] - left[1] * first[1])
                        value = value - (right[0] * second[0] - right[1] * second[1])
                        done[o, o] = (value,)
                    elif o < c:
                        value = minus_product(block[o, c], left, done[p, c])
                        done[o, c] = minus_product(value, right, done[q, c])
                        if o > q:
                            done[c, o] = (done[o, c][0], -done[o, c][1])
            block.update(done)
        for t in range(len(tiles)):
            tile = tiles[t]
            for b in range(PIVOTS):
                tile = minus_product(tile, columns[t][b], rows[b])
            if t == home:
                for b in range(PIVOTS):
                    here = sublane == at + b
                    tile = tuple(jnp.where(here, rows[b][k], tile[k]) for k in range(2))
            tiles[t] = tile
        yield
    for part in range(2):
        result.append(jnp.concatenate([tile[part] for tile in tiles], 0)[:, :size])


def interleave(*steps):
    steps = list(steps)
    while steps:
        steps = [step for step in steps if next(step, steps) is not steps]


def core_kernel(
    dims,
    order,
    back_order,
    x_ref,
    omega_ref,
    analysis_high,
    analysis_low,
    sketch_high,
    sketch_low,
    basis_high,
    basis_low,
    window_high,
    window_low,
    back_high,
    back_low,
    weight_ref,
    out_ref,
    xhat,
    shat,
    bhat,
    uhat,
    dhat,
    ghat,
):
    first, second, rank = dims
    keep1, keep2 = first // 2, second // 2
    span1, span2 = first - keep1 + 1, second - keep2 + 1
    own = lax.axis_index("narrow")
    half = CELLS
    tiles = rank // 8
    pieces = CELLS // LANES
    small = keep1 * keep2 * span1 * span2 <= 64

    def sweep(count, body, carry):
        if small:
            for i in range(count):
                carry = body(i, carry)
            return carry
        return lax.fori_loop(0, count, body, carry)

    def rows(start, count=8):
        if isinstance(start, int):
            return pl.ds(start, count)
        return pl.ds(pl.multiple_of(start, 8), count)

    def lanes(part, piece):
        start = part * half + piece * LANES
        return pl.ds(start, LANES)

    planes = first * second
    spectrum = jnp.concatenate(
        [
            jnp.concatenate([x_ref[:, part * pieces + piece, :] for piece in range(pieces)], 1)
            for part in range(2)
        ],
        0,
    )
    both = wide_dot(spectrum, analysis_high[...], analysis_low[...])
    hats = (
        both[:planes, :half] + both[planes:, half:],
        both[planes:, :half] - both[:planes, half:],
    )
    hats = (*hats, hats[0] + hats[1])
    for part in range(3):
        for piece in range(pieces):
            values = hats[part][:, piece * LANES : (piece + 1) * LANES]
            for p in range(planes):
                xhat[order[p], part * pieces + piece] = jnp.broadcast_to(
                    values[p : p + 1], (8, LANES)
                )

    def load_x(g1, g2, piece, parts=2):
        row = g2 * first + g1
        return tuple(xhat[row, part * pieces + piece] for part in range(parts))

    for piece in range(pieces):
        cache = {}

        def cached_x(g1, g2):
            if not small:
                return load_x(g1, g2, piece, 3)
            if (g1, g2) not in cache:
                cache[g1, g2] = load_x(g1, g2, piece, 3)
            return cache[g1, g2]

        def sketch_tile(tile, carry):
            def first_keep(l1, carry):
                zero = jnp.zeros((8, LANES), jnp.float32)

                def columns(k1, sums):
                    def column(k2, sums):
                        start = (k1 * span2 + k2) * rank + tile * 8
                        weights = [omega_ref[rows(start), lanes(k, piece)] for k in range(3)]
                        sums = list(sums)
                        for l2 in range(keep2):
                            x_real, x_imag, x_sum = cached_x(l1 + k1, l2 + k2)
                            common, less_real, less_imag = sums[l2]
                            sums[l2] = (
                                common + x_sum * weights[0],
                                less_real + x_imag * weights[1],
                                less_imag + x_real * weights[2],
                            )
                        return tuple(sums)

                    return sweep(span2, column, sums)

                sums = sweep(span1, columns, ((zero, zero, zero),) * keep2)
                for l2 in range(keep2):
                    start = (l1 * keep2 + l2) * rank + tile * 8
                    common, less_real, less_imag = sums[l2]
                    shat[rows(start), lanes(0, piece)] = common - less_real
                    shat[rows(start), lanes(1, piece)] = common - less_imag
                return carry

            return sweep(keep1, first_keep, carry)

        sweep(tiles, sketch_tile, 0)

    blocks = keep1 * keep2
    sketch = wide_dot(shat[...], sketch_high[...], sketch_low[...])
    straight = jnp.concatenate(
        [sketch[b * rank : (b + 1) * rank, : 2 * ROWS] for b in range(blocks)], 1
    )
    turned = jnp.concatenate(
        [sketch[b * rank : (b + 1) * rank, 2 * ROWS :] for b in range(blocks)], 1
    )
    contract = (((1,), (1,)), ((), ()))
    space = jnp.zeros_like(straight)

    def gram(right):
        return lax.dot_general(
            straight,
            jnp.concatenate([space, right], 0),
            contract,
            precision=highest,
            preferred_element_type=jnp.float32,
        )

    row_index = lax.broadcasted_iota(jnp.int32, (rank, 2 * rank), 0)
    column_index = lax.broadcasted_iota(jnp.int32, (rank, 2 * rank), 1)
    unit = 1.0 / jnp.max(jnp.abs(spectrum), keepdims=True)
    gram_real = gram(straight) * unit * unit
    gram_imag = gram(turned) * unit * unit
    gram_real = jnp.where(row_index == column_index, 1.0, gram_real)

    def partner(a):
        k1 = own - a
        valid = jnp.logical_and(k1 >= 0, k1 < span1).astype(jnp.float32)
        return jnp.clip(k1, 0, span1 - 1), valid

    def own_columns(a):
        k1, _ = partner(a)
        for piece in range(pieces):
            cache = {}

            def cached_x(l1, g2):
                if not small:
                    return load_x(l1 + k1, g2, piece)
                if (l1, g2) not in cache:
                    cache[l1, g2] = load_x(l1 + k1, g2, piece)
                return cache[l1, g2]

            def column_tile(tile, carry):
                zero = jnp.zeros((8, LANES), jnp.float32)

                def first_keep(l1, sums):
                    sums = list(sums)
                    for l2 in range(keep2):
                        start = (l1 * keep2 + l2) * rank + tile * 8
                        s_real = bhat[rows(start), lanes(0, piece)]
                        s_imag = bhat[rows(start), lanes(1, piece)]
                        for k2 in range(span2):
                            x_real, x_imag = cached_x(l1, l2 + k2)
                            real, imag = sums[k2]
                            sums[k2] = (
                                real + (s_real * x_real + s_imag * x_imag),
                                imag + (s_real * x_imag - s_imag * x_real),
                            )
                    return tuple(sums)

                sums = sweep(keep1, first_keep, ((zero, zero),) * span2)
                for k2 in range(span2):
                    for part in range(2):
                        start = (part * span2 + k2) * rank + tile * 8
                        dhat[rows(start), pl.ds(piece * LANES, LANES)] = sums[k2][part]
                return carry

            if small:
                for tile in range(tiles):
                    column_tile(tile, 0)
                    yield
            else:
                sweep(tiles, column_tile, 0)
        dhat[...] = wide_dot(dhat[...], window_high[...], window_low[...])
        yield

    def own_planes(a):
        _, valid = partner(a)
        for piece in range(pieces):

            def rebuild_tile(tile, sums):
                sums = list(sums)
                us = []
                for l2 in range(keep2):
                    start = (a * keep2 + l2) * rank + tile * 8
                    us.append(
                        (
                            uhat[rows(start), lanes(0, piece)],
                            uhat[rows(start), lanes(1, piece)],
                        )
                    )
                for k2 in range(span2):
                    d_real = dhat[rows(k2 * rank + tile * 8), pl.ds(piece * LANES, LANES)]
                    d_imag = dhat[
                        rows((span2 + k2) * rank + tile * 8), pl.ds(piece * LANES, LANES)
                    ]
                    for l2 in range(keep2):
                        u_real, u_imag = us[l2]
                        real, imag = sums[l2 + k2]
                        sums[l2 + k2] = (
                            real + (u_real * d_real - u_imag * d_imag),
                            imag + (u_real * d_imag + u_imag * d_real),
                        )
                return tuple(sums)

            zero = jnp.zeros((8, LANES), jnp.float32)
            sums = sweep(tiles, rebuild_tile, ((zero, zero),) * second)
            for part in range(2):
                summed = jnp.concatenate(
                    [jnp.sum(sums[g2][part], 0, keepdims=True) for g2 in range(second)], 0
                )
                place = pl.ds(piece * LANES, LANES)
                where = pl.ds(part * second, second)
                ghat[where, place] = ghat[where, place] + summed * valid

    def own_basis():
        bhat[...] = wide_dot(sketch[:, : 2 * ROWS], basis_high[...], basis_low[...])
        yield
        if small:
            yield from own_columns(0)

    inverse = []
    interleave(invert(gram_real, gram_imag, inverse), own_basis())
    mixer = jnp.concatenate(inverse, 0) * unit * unit

    def mix(b, carry):
        where = rows(b * rank, rank)
        both = jnp.dot(
            mixer, bhat[where, :], precision=highest, preferred_element_type=jnp.float32
        )
        uhat[where, :half] = both[:rank, :half] + both[rank:, half:]
        uhat[where, half:] = both[:rank, half:] - both[rank:, :half]
        return carry

    sweep(blocks, mix, 0)
    ghat[...] = jnp.zeros_like(ghat)

    def own_pair(a, carry):
        if not (small and isinstance(a, int) and a == 0):
            for _ in own_columns(a):
                pass
        own_planes(a)
        return carry

    sweep(keep1, own_pair, 0)

    both = wide_dot(ghat[...], back_high[...], back_low[...])
    real = both[:second, :half] - both[second:, half:]
    imag = both[:second, half:] + both[second:, :half]
    weight = weight_ref[pl.ds(pl.multiple_of(own * second, 8), second), :]
    real = real * weight
    imag = imag * weight
    for j in range(second):
        row = slice(back_order[j], back_order[j] + 1)
        for piece in range(pieces):
            place = slice(piece * LANES, (piece + 1) * LANES)
            out_ref[j, pl.ds(piece, 1), :] = real[row, place]
            out_ref[j, pl.ds(pieces + piece, 1), :] = imag[row, place]


def synthesis_kernel(cells_ref, table_ref, out_ref, out, sems):
    parts = [
        jnp.concatenate([cells_ref[:, part * PIECES + piece, :] for piece in range(PIECES)], 1)
        for part in range(2)
    ]
    high, low = split(jnp.concatenate(parts, 0))
    stacked = jnp.concatenate([high, low, high], 0)
    contract = (((0,), (0,)), ((), ()))
    chunks, width, _ = out.shape
    copies = []
    for i in range(chunks):
        out[i] = lax.dot_general(
            stacked[:, i * width : (i + 1) * width],
            table_ref[...],
            contract,
            preferred_element_type=jnp.float32,
        )
        copies.append(
            pltpu.make_async_copy(out.at[i], out_ref.at[pl.ds(i * width, width)], sems.at[i])
        )
        copies[-1].start()
    for copy in copies:
        copy.wait()


def group_order(count):
    return [(3 * count // 4 - 1 - i) % count for i in range(count)]


def per_device(traces, mask, omega):
    narrow_count = lax.axis_size("narrow")
    wide_count = lax.axis_size("wide")
    assert traces.shape[:2] == (1, 1)
    first, second = narrow_count, wide_count
    freq_total = FREQ_DEV * wide_count
    keep1, keep2 = first // 2, second // 2
    span1, span2 = first - keep1 + 1, second - keep2 + 1
    rank = omega.shape[0] * narrow_count
    dests = wide_count * narrow_count
    lines = 2 * PIECES

    omegas = [omega]
    for step in range(1, narrow_count):
        ring = [(i, (i + step) % narrow_count) for i in range(narrow_count)]
        omegas.append(lax.ppermute(omega, "narrow", ring))

    order = group_order(dests)
    high, low = halves(spectrum_table(freq_total, [i // narrow_count for i in order]))
    blocks = pl.pallas_call(
        spectrum_kernel,
        out_shape=jax.ShapeDtypeStruct((dests, lines, LANES), jnp.float32),
        in_specs=[HBM] * 3,
        out_specs=VMEM,
        scratch_shapes=[
            pltpu.VMEM((CHUNKS, CELLS, S // CHUNKS), jnp.float32),
            pltpu.VMEM((1, CELLS), jnp.int32),
            pltpu.VMEM((4 * dests, S), jnp.bfloat16),
            pltpu.SemaphoreType.DMA((2 + CHUNKS,)),
        ],
        name="spectrum",
    )(traces.reshape(CELLS, S), mask.reshape(1, CELLS), np.concatenate([high, low], 0))
    grid = lax.all_to_all(
        blocks,
        ("wide", "narrow"),
        split_axis=0,
        concat_axis=0,
        axis_index_groups=[order],
        tiled=True,
    )

    if omega.shape[0] % 8:
        omegas = [jnp.concatenate(omegas, 0)]
    columns = span1 * span2
    omega_hat = pl.pallas_call(
        functools.partial(omega_kernel, columns),
        out_shape=jax.ShapeDtypeStruct((columns * rank, 3 * CELLS), jnp.float32),
        in_specs=[VMEM] * (len(omegas) + 2),
        out_specs=VMEM,
        cost_estimate=pl.CostEstimate(
            flops=6 * columns * rank * LANES * 2 * CELLS,
            bytes_accessed=4 * columns * rank * 2 * CELLS,
            transcendentals=0,
        ),
        compiler_params=pltpu.CompilerParams(vmem_limit_bytes=16 * MIB),
        name="omega",
    )(*omegas, *halves(omega_table()))

    angles = centred_angles()
    counts = (
        correlation(first, keep1)[:, None, None]
        * correlation(second, keep2)[None, :, None]
        * np.outer(correlation(G3, KEEP3), correlation(G4, KEEP4)).reshape(1, 1, CELLS)
    ).reshape(first * second, CELLS)
    forward = np.concatenate([np.cos(angles), np.sin(angles)], 1)
    backward = np.concatenate([np.cos(angles.T), np.sin(angles.T)], 1) / CELLS
    tables = (
        *halves(forward),
        *halves(sketch_table()),
        *halves(basis_table()),
        *halves(window_table()),
        *halves(backward),
        (1.0 / counts).astype(np.float32),
    )
    area = keep1 * keep2 * rank
    scratch = [
        (first * second, 3 * PIECES, 8, LANES),
        (area, 2 * CELLS),
        (area, 2 * CELLS),
        (area, 2 * CELLS),
        (2 * span2 * rank, CELLS),
        (2 * second, CELLS),
    ]
    back_order = group_order(second)
    rebuilt = pl.pallas_call(
        functools.partial(core_kernel, (first, second, rank), order, back_order),
        out_shape=jax.ShapeDtypeStruct((second, lines, LANES), jnp.float32),
        in_specs=[VMEM] * (2 + len(tables)),
        out_specs=VMEM,
        scratch_shapes=[pltpu.VMEM(shape, jnp.float32) for shape in scratch],
        compiler_params=pltpu.CompilerParams(vmem_limit_bytes=24 * MIB),
        name="core",
    )(grid, omega_hat, *tables)
    returned = lax.all_to_all(
        rebuilt,
        "wide",
        split_axis=0,
        concat_axis=0,
        axis_index_groups=[back_order],
        tiled=True,
    )

    high, low = halves(synthesis_table(freq_total, back_order))
    filtered = pl.pallas_call(
        synthesis_kernel,
        out_shape=jax.ShapeDtypeStruct((CELLS, S), jnp.float32),
        in_specs=[VMEM] * 2,
        out_specs=HBM,
        scratch_shapes=[
            pltpu.VMEM((PIECES, LANES, S), jnp.float32),
            pltpu.SemaphoreType.DMA((PIECES,)),
        ],
        compiler_params=pltpu.CompilerParams(vmem_limit_bytes=8 * MIB),
        name="synthesis",
    )(returned, np.concatenate([high, high, low], 0))
    return filtered.reshape(traces.shape)


def solution(mesh):
    return jax.shard_map(
        per_device,
        mesh=mesh,
        in_specs=(
            P(("win", "narrow"), "wide", None, None),
            P(("win", "narrow"), "wide", None),
            P("narrow", None),
        ),
        out_specs=P(("win", "narrow"), "wide", None, None),
        check_vma=False,
    )
```

```python
import functools
import math

import jax
import jax.numpy as jnp
import ml_dtypes
import numpy as np
from jax import lax
from jax.experimental import pallas as pl
from jax.experimental.pallas import tpu as pltpu
from jax.sharding import PartitionSpec as P

G3 = 16
G4 = 16
S = 1024
FREQ_DEV = 1
FIRST_BIN = 16
LANES = 128
MIB = 1 << 20
CHUNKS = 2
PIVOTS = 4
CELLS = G3 * G4
KEEP3, KEEP4 = G3 // 2, G4 // 2
SPAN3, SPAN4 = G3 - KEEP3 + 1, G4 - KEEP4 + 1
SHIFT3, SHIFT4 = (SPAN3 - 1) // 2, (SPAN4 - 1) // 2
ROWS = KEEP3 * KEEP4
COLS = SPAN3 * SPAN4
PIECES = CELLS // LANES

HBM = pl.BlockSpec(memory_space=pltpu.HBM)
VMEM = pl.BlockSpec(memory_space=pltpu.VMEM)
highest = lax.Precision.HIGHEST


def halves(table):
    table = np.asarray(table, np.float32)
    high = table.astype(ml_dtypes.bfloat16)
    low = (table - high.astype(np.float32)).astype(ml_dtypes.bfloat16)
    return high, low


def phases(freq_total):
    bins = FIRST_BIN + np.arange(freq_total)
    return 2.0 * np.pi * ((bins[:, None] * np.arange(S)[None, :]) % S) / S


def cell_angles(positions3, positions4):
    wave = np.arange(CELLS)
    turns = (
        np.outer(positions3, wave // G4) % G3 / G3 + np.outer(positions4, wave % G4) % G4 / G4
    )
    return 2.0 * np.pi * turns


def correlation(length, keep_size):
    position = np.arange(length)
    span_size = length - keep_size + 1
    return (
        np.minimum(position, keep_size - 1) - np.maximum(position - span_size + 1, 0) + 1
    ).astype(np.float64)


def spectrum_table(freq_total, owners):
    angles = phases(freq_total)[owners]
    return np.concatenate([np.cos(angles), -np.sin(angles)], 0) / math.sqrt(S)


def synthesis_table(freq_total, order):
    angles = phases(freq_total)[order]
    return np.concatenate([np.cos(angles), -np.sin(angles)], 0) * math.sqrt(2.0 / freq_total)


def centred_angles():
    cell = np.arange(CELLS)
    return cell_angles(cell // G4 - SHIFT3, cell % G4 - SHIFT4)


def omega_table():
    column = np.arange(COLS)
    angles = cell_angles(column // SPAN4, column % SPAN4)
    table = np.zeros((LANES, 2 * CELLS))
    table[:COLS] = np.concatenate([np.cos(angles), -np.sin(angles)], 1)
    return table


def sketch_table():
    row = np.arange(ROWS)
    angles = cell_angles(row // KEEP4 - SHIFT3, row % KEEP4 - SHIFT4).T
    real, imag = np.cos(angles) / CELLS, np.sin(angles) / CELLS
    from_real = np.concatenate([real, imag, imag, -real], 1)
    from_imag = np.concatenate([-imag, real, real, imag], 1)
    return np.concatenate([from_real, from_imag], 0)


def basis_table():
    row = np.arange(ROWS)
    angles = cell_angles(row // KEEP4, row % KEEP4)
    real, imag = np.cos(angles), np.sin(angles)
    return np.concatenate(
        [np.concatenate([real, -imag], 1), np.concatenate([imag, real], 1)], 0
    )


def window_table():
    parts = []
    for length, shift in ((G3, SHIFT3), (G4, SHIFT4)):
        wave = np.arange(length)
        turns = (wave[:, None] - wave[None, :])[:, :, None] * np.arange(-shift, shift + 1) / length
        parts.append(np.cos(2.0 * np.pi * turns).sum(-1) / length)
    return np.kron(parts[0], parts[1])


def split(value):
    high = value.astype(jnp.bfloat16)
    low = (value - high.astype(jnp.float32)).astype(jnp.bfloat16)
    return high, low


def dot(left, right):
    return jnp.dot(left, right, preferred_element_type=jnp.float32)


def wide_dot(value, high, low):
    rows = value.shape[0]
    value_high, value_low = split(value)
    main = dot(jnp.concatenate([value_high, value_low], 0), high)
    return main[:rows] + (main[rows:] + dot(value_high, low))


def spectrum_kernel(traces_ref, mask_ref, table_ref, out_ref, traces, mask, table, sems):
    rows = table.shape[0] // 2
    dests = rows // 2
    chunks, _, width = traces.shape
    copies = [
        pltpu.make_async_copy(table_ref, table, sems.at[0]),
        pltpu.make_async_copy(mask_ref, mask, sems.at[1]),
    ] + [
        pltpu.make_async_copy(
            traces_ref.at[:, pl.ds(i * width, width)], traces.at[i], sems.at[2 + i]
        )
        for i in range(chunks)
    ]
    for copy in copies:
        copy.start()
    copies[0].wait()
    contract = (((1,), (1,)), ((), ()))
    total = jnp.zeros((2 * rows, CELLS), jnp.float32)
    rest = jnp.zeros((rows, CELLS), jnp.float32)
    for i in range(chunks):
        copies[2 + i].wait()
        high, low = split(traces[i])
        place = pl.ds(i * width, width)
        total += lax.dot_general(
            table[:, place], high, contract, preferred_element_type=jnp.float32
        )
        rest += lax.dot_general(
            table[:rows, place], low, contract, preferred_element_type=jnp.float32
        )
    copies[1].wait()
    result = (total[:rows] + (total[rows:] + rest)) * mask[...].astype(jnp.float32)
    for part in range(2):
        for piece in range(PIECES):
            out_ref[:, part * PIECES + piece, :] = result[
                part * dests : (part + 1) * dests, piece * LANES : (piece + 1) * LANES
            ]


def omega_kernel(columns, *refs):
    omega_refs = refs[:-3]
    high_ref, low_ref, out_ref = refs[-3:]
    omega = jnp.concatenate([ref[...] for ref in omega_refs], 0)
    pad = jnp.zeros((omega.shape[0], LANES - COLS), jnp.float32)
    blocks = [
        jnp.concatenate([omega[:, k * COLS : (k + 1) * COLS], pad], 1) for k in range(columns)
    ]
    hats = wide_dot(jnp.concatenate(blocks, 0), high_ref[...], low_ref[...])
    real, imag = hats[:, :CELLS], hats[:, CELLS:]
    out_ref[:, :CELLS] = real
    out_ref[:, CELLS : 2 * CELLS] = real - imag
    out_ref[:, 2 * CELLS :] = real + imag


def minus_product(value, left, right):
    return (
        value[0] - (left[0] * right[0] - left[1] * right[1]),
        value[1] - (left[0] * right[1] + left[1] * right[0]),
    )


def pivot_pair(upper, lower, corner, other, cross, scale):
    turned = (cross[0], -cross[1])
    first = minus_product(tuple(other * v for v in upper), cross, lower)
    second = minus_product(tuple(corner * v for v in lower), turned, upper)
    return tuple(v * scale for v in first), tuple(v * scale for v in second)


def invert(real, imag, result):
    size = real.shape[0]
    width = 2 * size
    tiles = [(real[t : t + 8], imag[t : t + 8]) for t in range(0, size, 8)]
    sublane = lax.broadcasted_iota(jnp.int32, (8, width), 0)
    for start in range(0, size, PIVOTS):
        home, at = start // 8, start % 8
        lane = size + start

        def spread(value, b, height):
            return jnp.broadcast_to(value[:, lane + b : lane + b + 1], (height, width))

        rows = [tuple(v[at + a : at + a + 1] for v in tiles[home]) for a in range(PIVOTS)]
        block = {}
        for a in range(PIVOTS):
            block[a, a] = (spread(rows[a][0], a, 1),)
            for b in range(a + 1, PIVOTS):
                block[a, b] = tuple(spread(v, b, 1) for v in rows[a])
                block[b, a] = (block[a, b][0], -block[a, b][1])
        columns = [
            [tuple(spread(v, b, 8) for v in tile) for b in range(PIVOTS)] for tile in tiles
        ]
        for p in range(0, PIVOTS, 2):
            q = p + 1
            corner, other, cross = block[p, p][0], block[q, q][0], block[p, q]
            scale = 1.0 / (corner * other - (cross[0] * cross[0] + cross[1] * cross[1]))
            pair = (corner, other, cross, scale)
            rows[p], rows[q] = pivot_pair(rows[p], rows[q], *pair)
            later = range(p + 2, PIVOTS)
            done = {}
            for c in later:
                done[p, c], done[q, c] = pivot_pair(block[p, c], block[q, c], *pair)
            for o in range(PIVOTS):
                if o in (p, q):
                    continue
                left, right = block[o, p], block[o, q]
                rows[o] = minus_product(minus_product(rows[o], left, rows[p]), right, rows[q])
                for c in later:
                    if o == c:
                        first, second = done[p, c], done[q, c]
                        value = block[o, o][0]
                        value = value - (left[0] * first[0] - left[1] * first[1])
                        value = value - (right[0] * second[0] - right[1] * second[1])
                        done[o, o] = (value,)
                    elif o < c:
                        value = minus_product(block[o, c], left, done[p, c])
                        done[o, c] = minus_product(value, right, done[q, c])
                        if o > q:
                            done[c, o] = (done[o, c][0], -done[o, c][1])
            block.update(done)
        for t in range(len(tiles)):
            tile = tiles[t]
            for b in range(PIVOTS):
                tile = minus_product(tile, columns[t][b], rows[b])
            if t == home:
                for b in range(PIVOTS):
                    here = sublane == at + b
                    tile = tuple(jnp.where(here, rows[b][k], tile[k]) for k in range(2))
            tiles[t] = tile
        yield
    for part in range(2):
        result.append(jnp.concatenate([tile[part] for tile in tiles], 0)[:, :size])


def interleave(*steps):
    steps = list(steps)
    while steps:
        steps = [step for step in steps if next(step, steps) is not steps]


def core_kernel(
    dims,
    order,
    back_order,
    x_ref,
    omega_ref,
    analysis_high,
    analysis_low,
    sketch_high,
    sketch_low,
    basis_high,
    basis_low,
    window_high,
    window_low,
    back_high,
    back_low,
    weight_ref,
    out_ref,
    xhat,
    shat,
    bhat,
    uhat,
    dhat,
    ghat,
):
    first, second, rank = dims
    keep1, keep2 = first // 2, second // 2
    span1, span2 = first - keep1 + 1, second - keep2 + 1
    own = lax.axis_index("narrow")
    half = CELLS
    tiles = rank // 8
    pieces = CELLS // LANES
    small = keep1 * keep2 * span1 * span2 <= 64

    def sweep(count, body, carry):
        if small:
            for i in range(count):
                carry = body(i, carry)
            return carry
        return lax.fori_loop(0, count, body, carry)

    def rows(start, count=8):
        if isinstance(start, int):
            return pl.ds(start, count)
        return pl.ds(pl.multiple_of(start, 8), count)

    def lanes(part, piece):
        start = part * half + piece * LANES
        return pl.ds(start, LANES)

    planes = first * second
    spectrum = jnp.concatenate(
        [
            jnp.concatenate([x_ref[:, part * pieces + piece, :] for piece in range(pieces)], 1)
            for part in range(2)
        ],
        0,
    )
    both = wide_dot(spectrum, analysis_high[...], analysis_low[...])
    hats = (
        both[:planes, :half] + both[planes:, half:],
        both[planes:, :half] - both[:planes, half:],
    )
    hats = (*hats, hats[0] + hats[1])
    for part in range(3):
        for piece in range(pieces):
            values = hats[part][:, piece * LANES : (piece + 1) * LANES]
            for p in range(planes):
                xhat[order[p], part * pieces + piece] = jnp.broadcast_to(
                    values[p : p + 1], (8, LANES)
                )

    def load_x(g1, g2, piece, parts=2):
        row = g2 * first + g1
        return tuple(xhat[row, part * pieces + piece] for part in range(parts))

    for piece in range(pieces):
        cache = {}

        def cached_x(g1, g2):
            if not small:
                return load_x(g1, g2, piece, 3)
            if (g1, g2) not in cache:
                cache[g1, g2] = load_x(g1, g2, piece, 3)
            return cache[g1, g2]

        def sketch_tile(tile, carry):
            def first_keep(l1, carry):
                zero = jnp.zeros((8, LANES), jnp.float32)

                def columns(k1, sums):
                    def column(k2, sums):
                        start = (k1 * span2 + k2) * rank + tile * 8
                        weights = [omega_ref[rows(start), lanes(k, piece)] for k in range(3)]
                        sums = list(sums)
                        for l2 in range(keep2):
                            x_real, x_imag, x_sum = cached_x(l1 + k1, l2 + k2)
                            common, less_real, less_imag = sums[l2]
                            sums[l2] = (
                                common + x_sum * weights[0],
                                less_real + x_imag * weights[1],
                                less_imag + x_real * weights[2],
                            )
                        return tuple(sums)

                    return sweep(span2, column, sums)

                sums = sweep(span1, columns, ((zero, zero, zero),) * keep2)
                for l2 in range(keep2):
                    start = (l1 * keep2 + l2) * rank + tile * 8
                    common, less_real, less_imag = sums[l2]
                    shat[rows(start), lanes(0, piece)] = common - less_real
                    shat[rows(start), lanes(1, piece)] = common - less_imag
                return carry

            return sweep(keep1, first_keep, carry)

        sweep(tiles, sketch_tile, 0)

    blocks = keep1 * keep2
    sketch = wide_dot(shat[...], sketch_high[...], sketch_low[...])
    straight = jnp.concatenate(
        [sketch[b * rank : (b + 1) * rank, : 2 * ROWS] for b in range(blocks)], 1
    )
    turned = jnp.concatenate(
        [sketch[b * rank : (b + 1) * rank, 2 * ROWS :] for b in range(blocks)], 1
    )
    contract = (((1,), (1,)), ((), ()))
    space = jnp.zeros_like(straight)

    def gram(right):
        return lax.dot_general(
            straight,
            jnp.concatenate([space, right], 0),
            contract,
            precision=highest,
            preferred_element_type=jnp.float32,
        )

    row_index = lax.broadcasted_iota(jnp.int32, (rank, 2 * rank), 0)
    column_index = lax.broadcasted_iota(jnp.int32, (rank, 2 * rank), 1)
    unit = 1.0 / jnp.max(jnp.abs(spectrum), keepdims=True)
    gram_real = gram(straight) * unit * unit
    gram_imag = gram(turned) * unit * unit
    gram_real = jnp.where(row_index == column_index, 1.0, gram_real)

    def partner(a):
        k1 = own - a
        valid = jnp.logical_and(k1 >= 0, k1 < span1).astype(jnp.float32)
        return jnp.clip(k1, 0, span1 - 1), valid

    def own_columns(a):
        k1, _ = partner(a)
        for piece in range(pieces):
            cache = {}

            def cached_x(l1, g2):
                if not small:
                    return load_x(l1 + k1, g2, piece)
                if (l1, g2) not in cache:
                    cache[l1, g2] = load_x(l1 + k1, g2, piece)
                return cache[l1, g2]

            def column_tile(tile, carry):
                zero = jnp.zeros((8, LANES), jnp.float32)

                def first_keep(l1, sums):
                    sums = list(sums)
                    for l2 in range(keep2):
                        start = (l1 * keep2 + l2) * rank + tile * 8
                        s_real = bhat[rows(start), lanes(0, piece)]
                        s_imag = bhat[rows(start), lanes(1, piece)]
                        for k2 in range(span2):
                            x_real, x_imag = cached_x(l1, l2 + k2)
                            real, imag = sums[k2]
                            sums[k2] = (
                                real + (s_real * x_real + s_imag * x_imag),
                                imag + (s_real * x_imag - s_imag * x_real),
                            )
                    return tuple(sums)

                sums = sweep(keep1, first_keep, ((zero, zero),) * span2)
                for k2 in range(span2):
                    for part in range(2):
                        start = (part * span2 + k2) * rank + tile * 8
                        dhat[rows(start), pl.ds(piece * LANES, LANES)] = sums[k2][part]
                return carry

            if small:
                for tile in range(tiles):
                    column_tile(tile, 0)
                    yield
            else:
                sweep(tiles, column_tile, 0)
        dhat[...] = wide_dot(dhat[...], window_high[...], window_low[...])
        yield

    def own_planes(a):
        _, valid = partner(a)
        for piece in range(pieces):

            def rebuild_tile(tile, sums):
                sums = list(sums)
                us = []
                for l2 in range(keep2):
                    start = (a * keep2 + l2) * rank + tile * 8
                    us.append(
                        (
                            uhat[rows(start), lanes(0, piece)],
                            uhat[rows(start), lanes(1, piece)],
                        )
                    )
                for k2 in range(span2):
                    d_real = dhat[rows(k2 * rank + tile * 8), pl.ds(piece * LANES, LANES)]
                    d_imag = dhat[
                        rows((span2 + k2) * rank + tile * 8), pl.ds(piece * LANES, LANES)
                    ]
                    for l2 in range(keep2):
                        u_real, u_imag = us[l2]
                        real, imag = sums[l2 + k2]
                        sums[l2 + k2] = (
                            real + (u_real * d_real - u_imag * d_imag),
                            imag + (u_real * d_imag + u_imag * d_real),
                        )
                return tuple(sums)

            zero = jnp.zeros((8, LANES), jnp.float32)
            sums = sweep(tiles, rebuild_tile, ((zero, zero),) * second)
            for part in range(2):
                summed = jnp.concatenate(
                    [jnp.sum(sums[g2][part], 0, keepdims=True) for g2 in range(second)], 0
                )
                place = pl.ds(piece * LANES, LANES)
                where = pl.ds(part * second, second)
                ghat[where, place] = ghat[where, place] + summed * valid

    def own_basis():
        bhat[...] = wide_dot(sketch[:, : 2 * ROWS], basis_high[...], basis_low[...])
        yield
        if small:
            yield from own_columns(0)

    inverse = []
    interleave(invert(gram_real, gram_imag, inverse), own_basis())
    mixer = jnp.concatenate(inverse, 0) * unit * unit

    def mix(b, carry):
        where = rows(b * rank, rank)
        both = jnp.dot(
            mixer, bhat[where, :], precision=highest, preferred_element_type=jnp.float32
        )
        uhat[where, :half] = both[:rank, :half] + both[rank:, half:]
        uhat[where, half:] = both[:rank, half:] - both[rank:, :half]
        return carry

    sweep(blocks, mix, 0)
    ghat[...] = jnp.zeros_like(ghat)

    def own_pair(a, carry):
        if not (small and isinstance(a, int) and a == 0):
            for _ in own_columns(a):
                pass
        own_planes(a)
        return carry

    sweep(keep1, own_pair, 0)

    both = wide_dot(ghat[...], back_high[...], back_low[...])
    real = both[:second, :half] - both[second:, half:]
    imag = both[:second, half:] + both[second:, :half]
    weight = weight_ref[pl.ds(pl.multiple_of(own * second, 8), second), :]
    real = real * weight
    imag = imag * weight
    for j in range(second):
        row = slice(back_order[j], back_order[j] + 1)
        for piece in range(pieces):
            place = slice(piece * LANES, (piece + 1) * LANES)
            out_ref[j, pl.ds(piece, 1), :] = real[row, place]
            out_ref[j, pl.ds(pieces + piece, 1), :] = imag[row, place]


def synthesis_kernel(cells_ref, table_ref, out_ref, out, sems):
    parts = [
        jnp.concatenate([cells_ref[:, part * PIECES + piece, :] for piece in range(PIECES)], 1)
        for part in range(2)
    ]
    high, low = split(jnp.concatenate(parts, 0))
    stacked = jnp.concatenate([high, low, high], 0)
    contract = (((0,), (0,)), ((), ()))
    chunks, width, _ = out.shape
    copies = []
    for i in range(chunks):
        out[i] = lax.dot_general(
            stacked[:, i * width : (i + 1) * width],
            table_ref[...],
            contract,
            preferred_element_type=jnp.float32,
        )
        copies.append(
            pltpu.make_async_copy(out.at[i], out_ref.at[pl.ds(i * width, width)], sems.at[i])
        )
        copies[-1].start()
    for copy in copies:
        copy.wait()


def group_order(count):
    return [(3 * count // 4 - 1 - i) % count for i in range(count)]


def per_device(traces, mask, omega):
    narrow_count = lax.axis_size("narrow")
    wide_count = lax.axis_size("wide")
    assert traces.shape[:2] == (1, 1)
    first, second = narrow_count, wide_count
    freq_total = FREQ_DEV * wide_count
    keep1, keep2 = first // 2, second // 2
    span1, span2 = first - keep1 + 1, second - keep2 + 1
    rank = omega.shape[0] * narrow_count
    dests = wide_count * narrow_count
    lines = 2 * PIECES

    order = group_order(dests)
    high, low = halves(spectrum_table(freq_total, [i // narrow_count for i in order]))
    blocks = pl.pallas_call(
        spectrum_kernel,
        out_shape=jax.ShapeDtypeStruct((dests, lines, LANES), jnp.float32),
        in_specs=[HBM] * 3,
        out_specs=VMEM,
        scratch_shapes=[
            pltpu.VMEM((CHUNKS, CELLS, S // CHUNKS), jnp.float32),
            pltpu.VMEM((1, CELLS), jnp.int32),
            pltpu.VMEM((4 * dests, S), jnp.bfloat16),
            pltpu.SemaphoreType.DMA((2 + CHUNKS,)),
        ],
        name="spectrum",
    )(traces.reshape(CELLS, S), mask.reshape(1, CELLS), np.concatenate([high, low], 0))
    blocks, omega = lax.optimization_barrier((blocks, omega))
    omegas = [omega]
    for step in range(1, narrow_count):
        ring = [(i, (i + step) % narrow_count) for i in range(narrow_count)]
        omegas.append(lax.ppermute(omega, "narrow", ring))

    grid = lax.all_to_all(
        blocks,
        ("wide", "narrow"),
        split_axis=0,
        concat_axis=0,
        axis_index_groups=[order],
        tiled=True,
    )

    if omega.shape[0] % 8:
        omegas = [jnp.concatenate(omegas, 0)]
    columns = span1 * span2
    omega_hat = pl.pallas_call(
        functools.partial(omega_kernel, columns),
        out_shape=jax.ShapeDtypeStruct((columns * rank, 3 * CELLS), jnp.float32),
        in_specs=[VMEM] * (len(omegas) + 2),
        out_specs=VMEM,
        cost_estimate=pl.CostEstimate(
            flops=6 * columns * rank * LANES * 2 * CELLS,
            bytes_accessed=4 * columns * rank * 2 * CELLS,
            transcendentals=0,
        ),
        compiler_params=pltpu.CompilerParams(vmem_limit_bytes=16 * MIB),
        name="omega",
    )(*omegas, *halves(omega_table()))

    angles = centred_angles()
    counts = (
        correlation(first, keep1)[:, None, None]
        * correlation(second, keep2)[None, :, None]
        * np.outer(correlation(G3, KEEP3), correlation(G4, KEEP4)).reshape(1, 1, CELLS)
    ).reshape(first * second, CELLS)
    forward = np.concatenate([np.cos(angles), np.sin(angles)], 1)
    backward = np.concatenate([np.cos(angles.T), np.sin(angles.T)], 1) / CELLS
    tables = (
        *halves(forward),
        *halves(sketch_table()),
        *halves(basis_table()),
        *halves(window_table()),
        *halves(backward),
        (1.0 / counts).astype(np.float32),
    )
    area = keep1 * keep2 * rank
    scratch = [
        (first * second, 3 * PIECES, 8, LANES),
        (area, 2 * CELLS),
        (area, 2 * CELLS),
        (area, 2 * CELLS),
        (2 * span2 * rank, CELLS),
        (2 * second, CELLS),
    ]
    back_order = group_order(second)
    rebuilt = pl.pallas_call(
        functools.partial(core_kernel, (first, second, rank), order, back_order),
        out_shape=jax.ShapeDtypeStruct((second, lines, LANES), jnp.float32),
        in_specs=[VMEM] * (2 + len(tables)),
        out_specs=VMEM,
        scratch_shapes=[pltpu.VMEM(shape, jnp.float32) for shape in scratch],
        compiler_params=pltpu.CompilerParams(vmem_limit_bytes=24 * MIB),
        name="core",
    )(grid, omega_hat, *tables)
    returned = lax.all_to_all(
        rebuilt,
        "wide",
        split_axis=0,
        concat_axis=0,
        axis_index_groups=[back_order],
        tiled=True,
    )

    high, low = halves(synthesis_table(freq_total, back_order))
    filtered = pl.pallas_call(
        synthesis_kernel,
        out_shape=jax.ShapeDtypeStruct((CELLS, S), jnp.float32),
        in_specs=[VMEM] * 2,
        out_specs=HBM,
        scratch_shapes=[
            pltpu.VMEM((PIECES, LANES, S), jnp.float32),
            pltpu.SemaphoreType.DMA((PIECES,)),
        ],
        compiler_params=pltpu.CompilerParams(vmem_limit_bytes=8 * MIB),
        name="synthesis",
    )(returned, np.concatenate([high, high, low], 0))
    return filtered.reshape(traces.shape)


def solution(mesh):
    return jax.shard_map(
        per_device,
        mesh=mesh,
        in_specs=(
            P(("win", "narrow"), "wide", None, None),
            P(("win", "narrow"), "wide", None),
            P("narrow", None),
        ),
        out_specs=P(("win", "narrow"), "wide", None, None),
        check_vma=False,
    )
```

```python
import functools
import math

import jax
import jax.numpy as jnp
import ml_dtypes
import numpy as np
from jax import lax
from jax.experimental import pallas as pl
from jax.experimental.pallas import tpu as pltpu
from jax.sharding import PartitionSpec as P

G3 = 16
G4 = 16
S = 1024
FREQ_DEV = 1
FIRST_BIN = 16
LANES = 128
MIB = 1 << 20
CHUNKS = 2
PIVOTS = 4
CELLS = G3 * G4
KEEP3, KEEP4 = G3 // 2, G4 // 2
SPAN3, SPAN4 = G3 - KEEP3 + 1, G4 - KEEP4 + 1
SHIFT3, SHIFT4 = (SPAN3 - 1) // 2, (SPAN4 - 1) // 2
ROWS = KEEP3 * KEEP4
COLS = SPAN3 * SPAN4
PIECES = CELLS // LANES

HBM = pl.BlockSpec(memory_space=pltpu.HBM)
VMEM = pl.BlockSpec(memory_space=pltpu.VMEM)
highest = lax.Precision.HIGHEST


def halves(table):
    table = np.asarray(table, np.float32)
    high = table.astype(ml_dtypes.bfloat16)
    low = (table - high.astype(np.float32)).astype(ml_dtypes.bfloat16)
    return high, low


def phases(freq_total):
    bins = FIRST_BIN + np.arange(freq_total)
    return 2.0 * np.pi * ((bins[:, None] * np.arange(S)[None, :]) % S) / S


def cell_angles(positions3, positions4):
    wave = np.arange(CELLS)
    turns = (
        np.outer(positions3, wave // G4) % G3 / G3 + np.outer(positions4, wave % G4) % G4 / G4
    )
    return 2.0 * np.pi * turns


def correlation(length, keep_size):
    position = np.arange(length)
    span_size = length - keep_size + 1
    return (
        np.minimum(position, keep_size - 1) - np.maximum(position - span_size + 1, 0) + 1
    ).astype(np.float64)


def spectrum_table(freq_total, owners):
    angles = phases(freq_total)[owners]
    return np.concatenate([np.cos(angles), -np.sin(angles)], 0) / math.sqrt(S)


def synthesis_table(freq_total, order):
    angles = phases(freq_total)[order]
    return np.concatenate([np.cos(angles), -np.sin(angles)], 0) * math.sqrt(2.0 / freq_total)


def centred_angles():
    cell = np.arange(CELLS)
    return cell_angles(cell // G4 - SHIFT3, cell % G4 - SHIFT4)


def omega_table():
    column = np.arange(COLS)
    angles = cell_angles(column // SPAN4, column % SPAN4)
    table = np.zeros((LANES, 2 * CELLS))
    table[:COLS] = np.concatenate([np.cos(angles), -np.sin(angles)], 1)
    return table


def sketch_table():
    row = np.arange(ROWS)
    angles = cell_angles(row // KEEP4 - SHIFT3, row % KEEP4 - SHIFT4).T
    real, imag = np.cos(angles) / CELLS, np.sin(angles) / CELLS
    from_real = np.concatenate([real, imag, imag, -real], 1)
    from_imag = np.concatenate([-imag, real, real, imag], 1)
    return np.concatenate([from_real, from_imag], 0)


def basis_table():
    row = np.arange(ROWS)
    angles = cell_angles(row // KEEP4, row % KEEP4)
    real, imag = np.cos(angles), np.sin(angles)
    return np.concatenate(
        [np.concatenate([real, -imag], 1), np.concatenate([imag, real], 1)], 0
    )


def window_table():
    parts = []
    for length, shift in ((G3, SHIFT3), (G4, SHIFT4)):
        wave = np.arange(length)
        turns = (wave[:, None] - wave[None, :])[:, :, None] * np.arange(-shift, shift + 1) / length
        parts.append(np.cos(2.0 * np.pi * turns).sum(-1) / length)
    return np.kron(parts[0], parts[1])


def split(value):
    high = value.astype(jnp.bfloat16)
    low = (value - high.astype(jnp.float32)).astype(jnp.bfloat16)
    return high, low


def dot(left, right):
    return jnp.dot(left, right, preferred_element_type=jnp.float32)


def wide_dot(value, high, low):
    rows = value.shape[0]
    value_high, value_low = split(value)
    main = dot(jnp.concatenate([value_high, value_low], 0), high)
    return main[:rows] + (main[rows:] + dot(value_high, low))


def spectrum_kernel(traces_ref, mask_ref, table_ref, out_ref, traces, mask, table, sems):
    rows = table.shape[0] // 2
    dests = rows // 2
    chunks, _, width = traces.shape
    copies = [
        pltpu.make_async_copy(table_ref, table, sems.at[0]),
        pltpu.make_async_copy(mask_ref, mask, sems.at[1]),
    ] + [
        pltpu.make_async_copy(
            traces_ref.at[:, pl.ds(i * width, width)], traces.at[i], sems.at[2 + i]
        )
        for i in range(chunks)
    ]
    for copy in copies:
        copy.start()
    copies[0].wait()
    contract = (((1,), (1,)), ((), ()))
    total = jnp.zeros((2 * rows, CELLS), jnp.float32)
    rest = jnp.zeros((rows, CELLS), jnp.float32)
    for i in range(chunks):
        copies[2 + i].wait()
        high, low = split(traces[i])
        place = pl.ds(i * width, width)
        total += lax.dot_general(
            table[:, place], high, contract, preferred_element_type=jnp.float32
        )
        rest += lax.dot_general(
            table[:rows, place], low, contract, preferred_element_type=jnp.float32
        )
    copies[1].wait()
    result = (total[:rows] + (total[rows:] + rest)) * mask[...].astype(jnp.float32)
    for part in range(2):
        for piece in range(PIECES):
            out_ref[:, part * PIECES + piece, :] = result[
                part * dests : (part + 1) * dests, piece * LANES : (piece + 1) * LANES
            ]


def omega_kernel(columns, *refs):
    omega_refs = refs[:-3]
    high_ref, low_ref, out_ref = refs[-3:]
    omega = jnp.concatenate([ref[...] for ref in omega_refs], 0)
    pad = jnp.zeros((omega.shape[0], LANES - COLS), jnp.float32)
    blocks = [
        jnp.concatenate([omega[:, k * COLS : (k + 1) * COLS], pad], 1) for k in range(columns)
    ]
    hats = wide_dot(jnp.concatenate(blocks, 0), high_ref[...], low_ref[...])
    real, imag = hats[:, :CELLS], hats[:, CELLS:]
    out_ref[:, :CELLS] = real
    out_ref[:, CELLS : 2 * CELLS] = real - imag
    out_ref[:, 2 * CELLS :] = real + imag


def minus_product(value, left, right):
    return (
        value[0] - (left[0] * right[0] - left[1] * right[1]),
        value[1] - (left[0] * right[1] + left[1] * right[0]),
    )


def pivot_pair(upper, lower, corner, other, cross, scale):
    turned = (cross[0], -cross[1])
    first = minus_product(tuple(other * v for v in upper), cross, lower)
    second = minus_product(tuple(corner * v for v in lower), turned, upper)
    return tuple(v * scale for v in first), tuple(v * scale for v in second)


def invert(real, imag, result):
    size = real.shape[0]
    width = 2 * size
    tiles = [(real[t : t + 8], imag[t : t + 8]) for t in range(0, size, 8)]
    sublane = lax.broadcasted_iota(jnp.int32, (8, width), 0)
    for start in range(0, size, PIVOTS):
        home, at = start // 8, start % 8
        lane = size + start

        def spread(value, b, height):
            return jnp.broadcast_to(value[:, lane + b : lane + b + 1], (height, width))

        rows = [tuple(v[at + a : at + a + 1] for v in tiles[home]) for a in range(PIVOTS)]
        block = {}
        for a in range(PIVOTS):
            block[a, a] = (spread(rows[a][0], a, 1),)
            for b in range(a + 1, PIVOTS):
                block[a, b] = tuple(spread(v, b, 1) for v in rows[a])
                block[b, a] = (block[a, b][0], -block[a, b][1])
        columns = [
            [tuple(spread(v, b, 8) for v in tile) for b in range(PIVOTS)] for tile in tiles
        ]
        for p in range(0, PIVOTS, 2):
            q = p + 1
            corner, other, cross = block[p, p][0], block[q, q][0], block[p, q]
            scale = 1.0 / (corner * other - (cross[0] * cross[0] + cross[1] * cross[1]))
            pair = (corner, other, cross, scale)
            rows[p], rows[q] = pivot_pair(rows[p], rows[q], *pair)
            later = range(p + 2, PIVOTS)
            done = {}
            for c in later:
                done[p, c], done[q, c] = pivot_pair(block[p, c], block[q, c], *pair)
            for o in range(PIVOTS):
                if o in (p, q):
                    continue
                left, right = block[o, p], block[o, q]
                rows[o] = minus_product(minus_product(rows[o], left, rows[p]), right, rows[q])
                for c in later:
                    if o == c:
                        first, second = done[p, c], done[q, c]
                        value = block[o, o][0]
                        value = value - (left[0] * first[0] - left[1] * first[1])
                        value = value - (right[0] * second[0] - right[1] * second[1])
                        done[o, o] = (value,)
                    elif o < c:
                        value = minus_product(block[o, c], left, done[p, c])
                        done[o, c] = minus_product(value, right, done[q, c])
                        if o > q:
                            done[c, o] = (done[o, c][0], -done[o, c][1])
            block.update(done)
        for t in range(len(tiles)):
            tile = tiles[t]
            for b in range(PIVOTS):
                tile = minus_product(tile, columns[t][b], rows[b])
            if t == home:
                for b in range(PIVOTS):
                    here = sublane == at + b
                    tile = tuple(jnp.where(here, rows[b][k], tile[k]) for k in range(2))
            tiles[t] = tile
        yield
    for part in range(2):
        result.append(jnp.concatenate([tile[part] for tile in tiles], 0)[:, :size])


def interleave(*steps):
    steps = list(steps)
    while steps:
        steps = [step for step in steps if next(step, steps) is not steps]


def core_kernel(
    dims,
    order,
    back_order,
    x_ref,
    omega_ref,
    analysis_high,
    analysis_low,
    sketch_high,
    sketch_low,
    basis_high,
    basis_low,
    window_high,
    window_low,
    back_high,
    back_low,
    weight_ref,
    out_ref,
    xhat,
    shat,
    bhat,
    uhat,
    dhat,
    ghat,
):
    first, second, rank = dims
    keep1, keep2 = first // 2, second // 2
    span1, span2 = first - keep1 + 1, second - keep2 + 1
    own = lax.axis_index("narrow")
    half = CELLS
    tiles = rank // 8
    pieces = CELLS // LANES
    small = keep1 * keep2 * span1 * span2 <= 64

    def sweep(count, body, carry):
        if small:
            for i in range(count):
                carry = body(i, carry)
            return carry
        return lax.fori_loop(0, count, body, carry)

    def rows(start, count=8):
        if isinstance(start, int):
            return pl.ds(start, count)
        return pl.ds(pl.multiple_of(start, 8), count)

    def lanes(part, piece):
        start = part * half + piece * LANES
        return pl.ds(start, LANES)

    planes = first * second
    spectrum = jnp.concatenate(
        [
            jnp.concatenate([x_ref[:, part * pieces + piece, :] for piece in range(pieces)], 1)
            for part in range(2)
        ],
        0,
    )
    both = wide_dot(spectrum, analysis_high[...], analysis_low[...])
    hats = (
        both[:planes, :half] + both[planes:, half:],
        both[planes:, :half] - both[:planes, half:],
    )
    hats = (*hats, hats[0] + hats[1])
    for part in range(3):
        for piece in range(pieces):
            values = hats[part][:, piece * LANES : (piece + 1) * LANES]
            for p in range(planes):
                xhat[order[p], part * pieces + piece] = jnp.broadcast_to(
                    values[p : p + 1], (8, LANES)
                )

    def load_x(g1, g2, piece, parts=2):
        row = g2 * first + g1
        return tuple(xhat[row, part * pieces + piece] for part in range(parts))

    for piece in range(pieces):
        cache = {}

        def cached_x(g1, g2):
            if not small:
                return load_x(g1, g2, piece, 3)
            if (g1, g2) not in cache:
                cache[g1, g2] = load_x(g1, g2, piece, 3)
            return cache[g1, g2]

        def sketch_tile(tile, carry):
            def first_keep(l1, carry):
                zero = jnp.zeros((8, LANES), jnp.float32)

                def columns(k1, sums):
                    def column(k2, sums):
                        start = (k1 * span2 + k2) * rank + tile * 8
                        weights = [omega_ref[rows(start), lanes(k, piece)] for k in range(3)]
                        sums = list(sums)
                        for l2 in range(keep2):
                            x_real, x_imag, x_sum = cached_x(l1 + k1, l2 + k2)
                            common, less_real, less_imag = sums[l2]
                            sums[l2] = (
                                common + x_sum * weights[0],
                                less_real + x_imag * weights[1],
                                less_imag + x_real * weights[2],
                            )
                        return tuple(sums)

                    return sweep(span2, column, sums)

                sums = sweep(span1, columns, ((zero, zero, zero),) * keep2)
                for l2 in range(keep2):
                    start = (l1 * keep2 + l2) * rank + tile * 8
                    common, less_real, less_imag = sums[l2]
                    shat[rows(start), lanes(0, piece)] = common - less_real
                    shat[rows(start), lanes(1, piece)] = common - less_imag
                return carry

            return sweep(keep1, first_keep, carry)

        sweep(tiles, sketch_tile, 0)

    blocks = keep1 * keep2
    sketch = wide_dot(shat[...], sketch_high[...], sketch_low[...])
    straight = jnp.concatenate(
        [sketch[b * rank : (b + 1) * rank, : 2 * ROWS] for b in range(blocks)], 1
    )
    turned = jnp.concatenate(
        [sketch[b * rank : (b + 1) * rank, 2 * ROWS :] for b in range(blocks)], 1
    )
    contract = (((1,), (1,)), ((), ()))
    space = jnp.zeros_like(straight)

    def gram(right):
        return lax.dot_general(
            straight,
            jnp.concatenate([space, right], 0),
            contract,
            precision=highest,
            preferred_element_type=jnp.float32,
        )

    row_index = lax.broadcasted_iota(jnp.int32, (rank, 2 * rank), 0)
    column_index = lax.broadcasted_iota(jnp.int32, (rank, 2 * rank), 1)
    unit = 1.0 / jnp.max(jnp.abs(spectrum), keepdims=True)
    gram_real = gram(straight) * unit * unit
    gram_imag = gram(turned) * unit * unit
    gram_real = jnp.where(row_index == column_index, 1.0, gram_real)

    def partner(a):
        k1 = own - a
        valid = jnp.logical_and(k1 >= 0, k1 < span1).astype(jnp.float32)
        return jnp.clip(k1, 0, span1 - 1), valid

    def own_columns(a):
        k1, _ = partner(a)
        for piece in range(pieces):
            cache = {}

            def cached_x(l1, g2):
                if not small:
                    return load_x(l1 + k1, g2, piece, 3)
                if (l1, g2) not in cache:
                    cache[l1, g2] = load_x(l1 + k1, g2, piece, 3)
                return cache[l1, g2]

            def column_tile(tile, carry):
                zero = jnp.zeros((8, LANES), jnp.float32)

                def first_keep(l1, sums):
                    sums = list(sums)
                    for l2 in range(keep2):
                        start = (l1 * keep2 + l2) * rank + tile * 8
                        s_real = bhat[rows(start), lanes(0, piece)]
                        s_imag = bhat[rows(start), lanes(1, piece)]
                        s_less, s_more = s_real - s_imag, s_real + s_imag
                        for k2 in range(span2):
                            x_real, x_imag, x_sum = cached_x(l1, l2 + k2)
                            common, less_real, less_imag = sums[k2]
                            sums[k2] = (
                                common + x_sum * s_real,
                                less_real + x_imag * s_less,
                                less_imag + x_real * s_more,
                            )
                    return tuple(sums)

                sums = sweep(keep1, first_keep, ((zero, zero, zero),) * span2)
                for k2 in range(span2):
                    for part in range(2):
                        start = (part * span2 + k2) * rank + tile * 8
                        dhat[rows(start), pl.ds(piece * LANES, LANES)] = (
                            sums[k2][0] - sums[k2][1 + part]
                        )
                return carry

            if small:
                for tile in range(tiles):
                    column_tile(tile, 0)
                    yield
            else:
                sweep(tiles, column_tile, 0)
        dhat[...] = wide_dot(dhat[...], window_high[...], window_low[...])
        yield

    def own_planes(a):
        _, valid = partner(a)
        for piece in range(pieces):

            def rebuild_tile(tile, sums):
                sums = list(sums)
                us = []
                for l2 in range(keep2):
                    start = (a * keep2 + l2) * rank + tile * 8
                    us.append(
                        (
                            uhat[rows(start), lanes(0, piece)],
                            uhat[rows(start), lanes(1, piece)],
                        )
                    )
                for k2 in range(span2):
                    d_real = dhat[rows(k2 * rank + tile * 8), pl.ds(piece * LANES, LANES)]
                    d_imag = dhat[
                        rows((span2 + k2) * rank + tile * 8), pl.ds(piece * LANES, LANES)
                    ]
                    for l2 in range(keep2):
                        u_real, u_imag = us[l2]
                        real, imag = sums[l2 + k2]
                        sums[l2 + k2] = (
                            real + (u_real * d_real - u_imag * d_imag),
                            imag + (u_real * d_imag + u_imag * d_real),
                        )
                return tuple(sums)

            zero = jnp.zeros((8, LANES), jnp.float32)
            sums = sweep(tiles, rebuild_tile, ((zero, zero),) * second)
            for part in range(2):
                summed = jnp.concatenate(
                    [jnp.sum(sums[g2][part], 0, keepdims=True) for g2 in range(second)], 0
                )
                place = pl.ds(piece * LANES, LANES)
                where = pl.ds(part * second, second)
                ghat[where, place] = ghat[where, place] + summed * valid

    def own_basis():
        bhat[...] = wide_dot(sketch[:, : 2 * ROWS], basis_high[...], basis_low[...])
        yield
        if small:
            yield from own_columns(0)

    inverse = []
    interleave(invert(gram_real, gram_imag, inverse), own_basis())
    mixer = jnp.concatenate(inverse, 0) * unit * unit

    def mix(b, carry):
        where = rows(b * rank, rank)
        both = jnp.dot(
            mixer, bhat[where, :], precision=highest, preferred_element_type=jnp.float32
        )
        uhat[where, :half] = both[:rank, :half] + both[rank:, half:]
        uhat[where, half:] = both[:rank, half:] - both[rank:, :half]
        return carry

    sweep(blocks, mix, 0)
    ghat[...] = jnp.zeros_like(ghat)

    def own_pair(a, carry):
        if not (small and isinstance(a, int) and a == 0):
            for _ in own_columns(a):
                pass
        own_planes(a)
        return carry

    sweep(keep1, own_pair, 0)

    both = wide_dot(ghat[...], back_high[...], back_low[...])
    real = both[:second, :half] - both[second:, half:]
    imag = both[:second, half:] + both[second:, :half]
    weight = weight_ref[pl.ds(pl.multiple_of(own * second, 8), second), :]
    real = real * weight
    imag = imag * weight
    for j in range(second):
        row = slice(back_order[j], back_order[j] + 1)
        for piece in range(pieces):
            place = slice(piece * LANES, (piece + 1) * LANES)
            out_ref[j, pl.ds(piece, 1), :] = real[row, place]
            out_ref[j, pl.ds(pieces + piece, 1), :] = imag[row, place]


def synthesis_kernel(cells_ref, table_ref, out_ref, out, sems):
    parts = [
        jnp.concatenate([cells_ref[:, part * PIECES + piece, :] for piece in range(PIECES)], 1)
        for part in range(2)
    ]
    high, low = split(jnp.concatenate(parts, 0))
    stacked = jnp.concatenate([high, low, high], 0)
    contract = (((0,), (0,)), ((), ()))
    chunks, width, _ = out.shape
    copies = []
    for i in range(chunks):
        out[i] = lax.dot_general(
            stacked[:, i * width : (i + 1) * width],
            table_ref[...],
            contract,
            preferred_element_type=jnp.float32,
        )
        copies.append(
            pltpu.make_async_copy(out.at[i], out_ref.at[pl.ds(i * width, width)], sems.at[i])
        )
        copies[-1].start()
    for copy in copies:
        copy.wait()


def group_order(count):
    return [(3 * count // 4 - 1 - i) % count for i in range(count)]


def per_device(traces, mask, omega):
    narrow_count = lax.axis_size("narrow")
    wide_count = lax.axis_size("wide")
    assert traces.shape[:2] == (1, 1)
    first, second = narrow_count, wide_count
    freq_total = FREQ_DEV * wide_count
    keep1, keep2 = first // 2, second // 2
    span1, span2 = first - keep1 + 1, second - keep2 + 1
    rank = omega.shape[0] * narrow_count
    dests = wide_count * narrow_count
    lines = 2 * PIECES

    order = group_order(dests)
    high, low = halves(spectrum_table(freq_total, [i // narrow_count for i in order]))
    blocks = pl.pallas_call(
        spectrum_kernel,
        out_shape=jax.ShapeDtypeStruct((dests, lines, LANES), jnp.float32),
        in_specs=[HBM] * 3,
        out_specs=VMEM,
        scratch_shapes=[
            pltpu.VMEM((CHUNKS, CELLS, S // CHUNKS), jnp.float32),
            pltpu.VMEM((1, CELLS), jnp.int32),
            pltpu.VMEM((4 * dests, S), jnp.bfloat16),
            pltpu.SemaphoreType.DMA((2 + CHUNKS,)),
        ],
        name="spectrum",
    )(traces.reshape(CELLS, S), mask.reshape(1, CELLS), np.concatenate([high, low], 0))
    blocks, omega = lax.optimization_barrier((blocks, omega))
    omegas = [omega]
    for step in range(1, narrow_count):
        ring = [(i, (i + step) % narrow_count) for i in range(narrow_count)]
        omegas.append(lax.ppermute(omega, "narrow", ring))

    grid = lax.all_to_all(
        blocks,
        ("wide", "narrow"),
        split_axis=0,
        concat_axis=0,
        axis_index_groups=[order],
        tiled=True,
    )

    if omega.shape[0] % 8:
        omegas = [jnp.concatenate(omegas, 0)]
    columns = span1 * span2
    omega_hat = pl.pallas_call(
        functools.partial(omega_kernel, columns),
        out_shape=jax.ShapeDtypeStruct((columns * rank, 3 * CELLS), jnp.float32),
        in_specs=[VMEM] * (len(omegas) + 2),
        out_specs=VMEM,
        cost_estimate=pl.CostEstimate(
            flops=6 * columns * rank * LANES * 2 * CELLS,
            bytes_accessed=4 * columns * rank * 2 * CELLS,
            transcendentals=0,
        ),
        compiler_params=pltpu.CompilerParams(vmem_limit_bytes=16 * MIB),
        name="omega",
    )(*omegas, *halves(omega_table()))

    angles = centred_angles()
    counts = (
        correlation(first, keep1)[:, None, None]
        * correlation(second, keep2)[None, :, None]
        * np.outer(correlation(G3, KEEP3), correlation(G4, KEEP4)).reshape(1, 1, CELLS)
    ).reshape(first * second, CELLS)
    forward = np.concatenate([np.cos(angles), np.sin(angles)], 1)
    backward = np.concatenate([np.cos(angles.T), np.sin(angles.T)], 1) / CELLS
    tables = (
        *halves(forward),
        *halves(sketch_table()),
        *halves(basis_table()),
        *halves(window_table()),
        *halves(backward),
        (1.0 / counts).astype(np.float32),
    )
    area = keep1 * keep2 * rank
    scratch = [
        (first * second, 3 * PIECES, 8, LANES),
        (area, 2 * CELLS),
        (area, 2 * CELLS),
        (area, 2 * CELLS),
        (2 * span2 * rank, CELLS),
        (2 * second, CELLS),
    ]
    back_order = group_order(second)
    rebuilt = pl.pallas_call(
        functools.partial(core_kernel, (first, second, rank), order, back_order),
        out_shape=jax.ShapeDtypeStruct((second, lines, LANES), jnp.float32),
        in_specs=[VMEM] * (2 + len(tables)),
        out_specs=VMEM,
        scratch_shapes=[pltpu.VMEM(shape, jnp.float32) for shape in scratch],
        compiler_params=pltpu.CompilerParams(vmem_limit_bytes=24 * MIB),
        name="core",
    )(grid, omega_hat, *tables)
    returned = lax.all_to_all(
        rebuilt,
        "wide",
        split_axis=0,
        concat_axis=0,
        axis_index_groups=[back_order],
        tiled=True,
    )

    high, low = halves(synthesis_table(freq_total, back_order))
    filtered = pl.pallas_call(
        synthesis_kernel,
        out_shape=jax.ShapeDtypeStruct((CELLS, S), jnp.float32),
        in_specs=[VMEM] * 2,
        out_specs=HBM,
        scratch_shapes=[
            pltpu.VMEM((PIECES, LANES, S), jnp.float32),
            pltpu.SemaphoreType.DMA((PIECES,)),
        ],
        compiler_params=pltpu.CompilerParams(vmem_limit_bytes=8 * MIB),
        name="synthesis",
    )(returned, np.concatenate([high, high, low], 0))
    return filtered.reshape(traces.shape)


def solution(mesh):
    return jax.shard_map(
        per_device,
        mesh=mesh,
        in_specs=(
            P(("win", "narrow"), "wide", None, None),
            P(("win", "narrow"), "wide", None),
            P("narrow", None),
        ),
        out_specs=P(("win", "narrow"), "wide", None, None),
        check_vma=False,
    )
```

```python
import functools
import math

import jax
import jax.numpy as jnp
import ml_dtypes
import numpy as np
from jax import lax
from jax.experimental import pallas as pl
from jax.experimental.pallas import tpu as pltpu
from jax.sharding import PartitionSpec as P

G3 = 16
G4 = 16
S = 1024
FREQ_DEV = 1
FIRST_BIN = 16
LANES = 128
MIB = 1 << 20
CHUNKS = 2
PIVOTS = 4
CELLS = G3 * G4
KEEP3, KEEP4 = G3 // 2, G4 // 2
SPAN3, SPAN4 = G3 - KEEP3 + 1, G4 - KEEP4 + 1
SHIFT3, SHIFT4 = (SPAN3 - 1) // 2, (SPAN4 - 1) // 2
ROWS = KEEP3 * KEEP4
COLS = SPAN3 * SPAN4
PIECES = CELLS // LANES

HBM = pl.BlockSpec(memory_space=pltpu.HBM)
VMEM = pl.BlockSpec(memory_space=pltpu.VMEM)
highest = lax.Precision.HIGHEST


def halves(table):
    table = np.asarray(table, np.float32)
    high = table.astype(ml_dtypes.bfloat16)
    low = (table - high.astype(np.float32)).astype(ml_dtypes.bfloat16)
    return high, low


def phases(freq_total):
    bins = FIRST_BIN + np.arange(freq_total)
    return 2.0 * np.pi * ((bins[:, None] * np.arange(S)[None, :]) % S) / S


def cell_angles(positions3, positions4):
    wave = np.arange(CELLS)
    turns = (
        np.outer(positions3, wave // G4) % G3 / G3 + np.outer(positions4, wave % G4) % G4 / G4
    )
    return 2.0 * np.pi * turns


def correlation(length, keep_size):
    position = np.arange(length)
    span_size = length - keep_size + 1
    return (
        np.minimum(position, keep_size - 1) - np.maximum(position - span_size + 1, 0) + 1
    ).astype(np.float64)


def spectrum_table(freq_total, owners):
    angles = phases(freq_total)[owners]
    return np.concatenate([np.cos(angles), -np.sin(angles)], 0) / math.sqrt(S)


def synthesis_table(freq_total, order):
    angles = phases(freq_total)[order]
    return np.concatenate([np.cos(angles), -np.sin(angles)], 0) * math.sqrt(2.0 / freq_total)


def centred_angles():
    cell = np.arange(CELLS)
    return cell_angles(cell // G4 - SHIFT3, cell % G4 - SHIFT4)


def omega_table():
    column = np.arange(COLS)
    angles = cell_angles(column // SPAN4, column % SPAN4)
    table = np.zeros((LANES, 2 * CELLS))
    table[:COLS] = np.concatenate([np.cos(angles), -np.sin(angles)], 1)
    return table


def sketch_table():
    row = np.arange(ROWS)
    angles = cell_angles(row // KEEP4 - SHIFT3, row % KEEP4 - SHIFT4).T
    real, imag = np.cos(angles) / CELLS, np.sin(angles) / CELLS
    from_real = np.concatenate([real, imag, imag, -real], 1)
    from_imag = np.concatenate([-imag, real, real, imag], 1)
    return np.concatenate([from_real, from_imag], 0)


def basis_table():
    row = np.arange(ROWS)
    angles = cell_angles(row // KEEP4, row % KEEP4)
    real, imag = np.cos(angles), np.sin(angles)
    return np.concatenate(
        [np.concatenate([real, -imag], 1), np.concatenate([imag, real], 1)], 0
    )


def window_table():
    parts = []
    for length, shift in ((G3, SHIFT3), (G4, SHIFT4)):
        wave = np.arange(length)
        turns = (wave[:, None] - wave[None, :])[:, :, None] * np.arange(-shift, shift + 1) / length
        parts.append(np.cos(2.0 * np.pi * turns).sum(-1) / length)
    return np.kron(parts[0], parts[1])


def split(value):
    high = value.astype(jnp.bfloat16)
    low = (value - high.astype(jnp.float32)).astype(jnp.bfloat16)
    return high, low


def dot(left, right):
    return jnp.dot(left, right, preferred_element_type=jnp.float32)


def wide_dot(value, high, low):
    rows = value.shape[0]
    value_high, value_low = split(value)
    main = dot(jnp.concatenate([value_high, value_low], 0), high)
    return main[:rows] + (main[rows:] + dot(value_high, low))


def spectrum_kernel(traces_ref, mask_ref, table_ref, out_ref, traces, mask, table, sems):
    rows = table.shape[0] // 2
    dests = rows // 2
    chunks, _, width = traces.shape
    copies = [
        pltpu.make_async_copy(table_ref, table, sems.at[0]),
        pltpu.make_async_copy(mask_ref, mask, sems.at[1]),
    ] + [
        pltpu.make_async_copy(
            traces_ref.at[:, pl.ds(i * width, width)], traces.at[i], sems.at[2 + i]
        )
        for i in range(chunks)
    ]
    for copy in copies:
        copy.start()
    copies[0].wait()
    contract = (((1,), (1,)), ((), ()))
    total = jnp.zeros((2 * rows, CELLS), jnp.float32)
    rest = jnp.zeros((rows, CELLS), jnp.float32)
    for i in range(chunks):
        copies[2 + i].wait()
        high, low = split(traces[i])
        place = pl.ds(i * width, width)
        total += lax.dot_general(
            table[:, place], high, contract, preferred_element_type=jnp.float32
        )
        rest += lax.dot_general(
            table[:rows, place], low, contract, preferred_element_type=jnp.float32
        )
    copies[1].wait()
    result = (total[:rows] + (total[rows:] + rest)) * mask[...].astype(jnp.float32)
    for part in range(2):
        for piece in range(PIECES):
            out_ref[:, part * PIECES + piece, :] = result[
                part * dests : (part + 1) * dests, piece * LANES : (piece + 1) * LANES
            ]


def omega_kernel(columns, *refs):
    omega_refs = refs[:-3]
    high_ref, low_ref, out_ref = refs[-3:]
    omega = jnp.concatenate([ref[...] for ref in omega_refs], 0)
    pad = jnp.zeros((omega.shape[0], LANES - COLS), jnp.float32)
    blocks = [
        jnp.concatenate([omega[:, k * COLS : (k + 1) * COLS], pad], 1) for k in range(columns)
    ]
    hats = wide_dot(jnp.concatenate(blocks, 0), high_ref[...], low_ref[...])
    real, imag = hats[:, :CELLS], hats[:, CELLS:]
    out_ref[:, :CELLS] = real
    out_ref[:, CELLS : 2 * CELLS] = real - imag
    out_ref[:, 2 * CELLS :] = real + imag


def minus_product(value, left, right):
    return (
        value[0] - (left[0] * right[0] - left[1] * right[1]),
        value[1] - (left[0] * right[1] + left[1] * right[0]),
    )


def pivot_pair(upper, lower, corner, other, cross, scale):
    turned = (cross[0], -cross[1])
    first = minus_product(tuple(other * v for v in upper), cross, lower)
    second = minus_product(tuple(corner * v for v in lower), turned, upper)
    return tuple(v * scale for v in first), tuple(v * scale for v in second)


def invert(real, imag, result):
    size = real.shape[0]
    width = 2 * size
    tiles = [(real[t : t + 8], imag[t : t + 8]) for t in range(0, size, 8)]
    sublane = lax.broadcasted_iota(jnp.int32, (8, width), 0)
    for start in range(0, size, PIVOTS):
        home, at = start // 8, start % 8
        lane = size + start

        def spread(value, b, height):
            return jnp.broadcast_to(value[:, lane + b : lane + b + 1], (height, width))

        rows = [tuple(v[at + a : at + a + 1] for v in tiles[home]) for a in range(PIVOTS)]
        block = {}
        for a in range(PIVOTS):
            block[a, a] = (spread(rows[a][0], a, 1),)
            for b in range(a + 1, PIVOTS):
                block[a, b] = tuple(spread(v, b, 1) for v in rows[a])
                block[b, a] = (block[a, b][0], -block[a, b][1])
        columns = [
            [tuple(spread(v, b, 8) for v in tile) for b in range(PIVOTS)] for tile in tiles
        ]
        for p in range(0, PIVOTS, 2):
            q = p + 1
            corner, other, cross = block[p, p][0], block[q, q][0], block[p, q]
            scale = 1.0 / (corner * other - (cross[0] * cross[0] + cross[1] * cross[1]))
            pair = (corner, other, cross, scale)
            rows[p], rows[q] = pivot_pair(rows[p], rows[q], *pair)
            later = range(p + 2, PIVOTS)
            done = {}
            for c in later:
                done[p, c], done[q, c] = pivot_pair(block[p, c], block[q, c], *pair)
            for o in range(PIVOTS):
                if o in (p, q):
                    continue
                left, right = block[o, p], block[o, q]
                rows[o] = minus_product(minus_product(rows[o], left, rows[p]), right, rows[q])
                for c in later:
                    if o == c:
                        first, second = done[p, c], done[q, c]
                        value = block[o, o][0]
                        value = value - (left[0] * first[0] - left[1] * first[1])
                        value = value - (right[0] * second[0] - right[1] * second[1])
                        done[o, o] = (value,)
                    elif o < c:
                        value = minus_product(block[o, c], left, done[p, c])
                        done[o, c] = minus_product(value, right, done[q, c])
                        if o > q:
                            done[c, o] = (done[o, c][0], -done[o, c][1])
            block.update(done)
        for t in range(len(tiles)):
            tile = tiles[t]
            for b in range(PIVOTS):
                tile = minus_product(tile, columns[t][b], rows[b])
            if t == home:
                for b in range(PIVOTS):
                    here = sublane == at + b
                    tile = tuple(jnp.where(here, rows[b][k], tile[k]) for k in range(2))
            tiles[t] = tile
        yield
    for part in range(2):
        result.append(jnp.concatenate([tile[part] for tile in tiles], 0)[:, :size])


def interleave(*steps):
    steps = list(steps)
    while steps:
        steps = [step for step in steps if next(step, steps) is not steps]


def core_kernel(
    dims,
    order,
    back_order,
    x_ref,
    omega_ref,
    analysis_high,
    analysis_low,
    sketch_high,
    sketch_low,
    basis_high,
    basis_low,
    window_high,
    window_low,
    back_high,
    back_low,
    weight_ref,
    out_ref,
    xhat,
    shat,
    bhat,
    uhat,
    dhat,
    ghat,
):
    first, second, rank = dims
    keep1, keep2 = first // 2, second // 2
    span1, span2 = first - keep1 + 1, second - keep2 + 1
    own = lax.axis_index("narrow")
    half = CELLS
    tiles = rank // 8
    pieces = CELLS // LANES
    small = keep1 * keep2 * span1 * span2 <= 64

    def sweep(count, body, carry):
        if small:
            for i in range(count):
                carry = body(i, carry)
            return carry
        return lax.fori_loop(0, count, body, carry)

    def rows(start, count=8):
        if isinstance(start, int):
            return pl.ds(start, count)
        return pl.ds(pl.multiple_of(start, 8), count)

    def lanes(part, piece):
        start = part * half + piece * LANES
        return pl.ds(start, LANES)

    planes = first * second
    spectrum = jnp.concatenate(
        [
            jnp.concatenate([x_ref[:, part * pieces + piece, :] for piece in range(pieces)], 1)
            for part in range(2)
        ],
        0,
    )
    both = wide_dot(spectrum, analysis_high[...], analysis_low[...])
    hats = (
        both[:planes, :half] + both[planes:, half:],
        both[planes:, :half] - both[:planes, half:],
    )
    hats = (*hats, hats[0] + hats[1])
    for part in range(3):
        for piece in range(pieces):
            values = hats[part][:, piece * LANES : (piece + 1) * LANES]
            for p in range(planes):
                xhat[order[p], part * pieces + piece] = jnp.broadcast_to(
                    values[p : p + 1], (8, LANES)
                )

    def load_x(g1, g2, piece, parts=2):
        row = g2 * first + g1
        return tuple(xhat[row, part * pieces + piece] for part in range(parts))

    for piece in range(pieces):
        cache = {}

        def cached_x(g1, g2):
            if not small:
                return load_x(g1, g2, piece, 3)
            if (g1, g2) not in cache:
                cache[g1, g2] = load_x(g1, g2, piece, 3)
            return cache[g1, g2]

        def sketch_tile(tile, carry):
            def first_keep(l1, carry):
                zero = jnp.zeros((8, LANES), jnp.float32)

                def columns(k1, sums):
                    def column(k2, sums):
                        start = (k1 * span2 + k2) * rank + tile * 8
                        weights = [omega_ref[rows(start), lanes(k, piece)] for k in range(3)]
                        sums = list(sums)
                        for l2 in range(keep2):
                            x_real, x_imag, x_sum = cached_x(l1 + k1, l2 + k2)
                            common, less_real, less_imag = sums[l2]
                            sums[l2] = (
                                common + x_sum * weights[0],
                                less_real + x_imag * weights[1],
                                less_imag + x_real * weights[2],
                            )
                        return tuple(sums)

                    return sweep(span2, column, sums)

                sums = sweep(span1, columns, ((zero, zero, zero),) * keep2)
                for l2 in range(keep2):
                    start = (l1 * keep2 + l2) * rank + tile * 8
                    common, less_real, less_imag = sums[l2]
                    shat[rows(start), lanes(0, piece)] = common - less_real
                    shat[rows(start), lanes(1, piece)] = common - less_imag
                return carry

            return sweep(keep1, first_keep, carry)

        sweep(tiles, sketch_tile, 0)

    blocks = keep1 * keep2
    sketch = wide_dot(shat[...], sketch_high[...], sketch_low[...])
    straight = jnp.concatenate(
        [sketch[b * rank : (b + 1) * rank, : 2 * ROWS] for b in range(blocks)], 1
    )
    turned = jnp.concatenate(
        [sketch[b * rank : (b + 1) * rank, 2 * ROWS :] for b in range(blocks)], 1
    )
    contract = (((1,), (1,)), ((), ()))
    space = jnp.zeros_like(straight)

    def gram(right):
        return lax.dot_general(
            straight,
            jnp.concatenate([space, right], 0),
            contract,
            precision=highest,
            preferred_element_type=jnp.float32,
        )

    row_index = lax.broadcasted_iota(jnp.int32, (rank, 2 * rank), 0)
    column_index = lax.broadcasted_iota(jnp.int32, (rank, 2 * rank), 1)
    unit = 1.0 / jnp.max(jnp.abs(spectrum), keepdims=True)
    gram_real = gram(straight) * unit * unit
    gram_imag = gram(turned) * unit * unit
    gram_real = jnp.where(row_index == column_index, 1.0, gram_real)

    def partner(a):
        k1 = own - a
        valid = jnp.logical_and(k1 >= 0, k1 < span1).astype(jnp.float32)
        return jnp.clip(k1, 0, span1 - 1), valid

    def own_columns(a):
        k1, _ = partner(a)
        for piece in range(pieces):
            cache = {}

            def cached_x(l1, g2):
                if not small:
                    return load_x(l1 + k1, g2, piece, 3)
                if (l1, g2) not in cache:
                    cache[l1, g2] = load_x(l1 + k1, g2, piece, 3)
                return cache[l1, g2]

            def column_tile(tile, carry):
                zero = jnp.zeros((8, LANES), jnp.float32)

                def first_keep(l1, sums):
                    sums = list(sums)
                    for l2 in range(keep2):
                        start = (l1 * keep2 + l2) * rank + tile * 8
                        s_real = bhat[rows(start), lanes(0, piece)]
                        s_imag = bhat[rows(start), lanes(1, piece)]
                        s_less, s_more = s_real - s_imag, s_real + s_imag
                        for k2 in range(span2):
                            x_real, x_imag, x_sum = cached_x(l1, l2 + k2)
                            common, less_real, less_imag = sums[k2]
                            sums[k2] = (
                                common + x_sum * s_real,
                                less_real + x_imag * s_less,
                                less_imag + x_real * s_more,
                            )
                    return tuple(sums)

                sums = sweep(keep1, first_keep, ((zero, zero, zero),) * span2)
                for k2 in range(span2):
                    for part in range(2):
                        start = (part * span2 + k2) * rank + tile * 8
                        dhat[rows(start), pl.ds(piece * LANES, LANES)] = (
                            sums[k2][0] - sums[k2][1 + part]
                        )
                return carry

            if small:
                for tile in range(tiles):
                    column_tile(tile, 0)
                    yield
            else:
                sweep(tiles, column_tile, 0)
        dhat[...] = wide_dot(dhat[...], window_high[...], window_low[...])
        yield

    def own_planes(a):
        _, valid = partner(a)
        for piece in range(pieces):

            def rebuild_tile(tile, sums):
                sums = list(sums)
                us = []
                for l2 in range(keep2):
                    start = (a * keep2 + l2) * rank + tile * 8
                    u_real = uhat[rows(start), lanes(0, piece)]
                    u_imag = uhat[rows(start), lanes(1, piece)]
                    us.append((u_real, u_real + u_imag, u_imag - u_real))
                for k2 in range(span2):
                    d_real = dhat[rows(k2 * rank + tile * 8), pl.ds(piece * LANES, LANES)]
                    d_imag = dhat[
                        rows((span2 + k2) * rank + tile * 8), pl.ds(piece * LANES, LANES)
                    ]
                    d_sum = d_real + d_imag
                    for l2 in range(keep2):
                        u_real, u_more, u_less = us[l2]
                        common, less_real, more_imag = sums[l2 + k2]
                        sums[l2 + k2] = (
                            common + u_real * d_sum,
                            less_real + u_more * d_imag,
                            more_imag + u_less * d_real,
                        )
                return tuple(sums)

            zero = jnp.zeros((8, LANES), jnp.float32)
            sums = sweep(tiles, rebuild_tile, ((zero, zero, zero),) * second)
            sums = [(common - less, common + more) for common, less, more in sums]
            for part in range(2):
                summed = jnp.concatenate(
                    [jnp.sum(sums[g2][part], 0, keepdims=True) for g2 in range(second)], 0
                )
                place = pl.ds(piece * LANES, LANES)
                where = pl.ds(part * second, second)
                ghat[where, place] = ghat[where, place] + summed * valid

    def own_basis():
        bhat[...] = wide_dot(sketch[:, : 2 * ROWS], basis_high[...], basis_low[...])
        yield
        if small:
            yield from own_columns(0)

    inverse = []
    interleave(invert(gram_real, gram_imag, inverse), own_basis())
    mixer = jnp.concatenate(inverse, 0) * unit * unit

    def mix(b, carry):
        where = rows(b * rank, rank)
        both = jnp.dot(
            mixer, bhat[where, :], precision=highest, preferred_element_type=jnp.float32
        )
        uhat[where, :half] = both[:rank, :half] + both[rank:, half:]
        uhat[where, half:] = both[:rank, half:] - both[rank:, :half]
        return carry

    sweep(blocks, mix, 0)
    ghat[...] = jnp.zeros_like(ghat)

    def own_pair(a, carry):
        if not (small and isinstance(a, int) and a == 0):
            for _ in own_columns(a):
                pass
        own_planes(a)
        return carry

    sweep(keep1, own_pair, 0)

    both = wide_dot(ghat[...], back_high[...], back_low[...])
    real = both[:second, :half] - both[second:, half:]
    imag = both[:second, half:] + both[second:, :half]
    weight = weight_ref[pl.ds(pl.multiple_of(own * second, 8), second), :]
    real = real * weight
    imag = imag * weight
    for j in range(second):
        row = slice(back_order[j], back_order[j] + 1)
        for piece in range(pieces):
            place = slice(piece * LANES, (piece + 1) * LANES)
            out_ref[j, pl.ds(piece, 1), :] = real[row, place]
            out_ref[j, pl.ds(pieces + piece, 1), :] = imag[row, place]


def synthesis_kernel(cells_ref, table_ref, out_ref, out, sems):
    parts = [
        jnp.concatenate([cells_ref[:, part * PIECES + piece, :] for piece in range(PIECES)], 1)
        for part in range(2)
    ]
    high, low = split(jnp.concatenate(parts, 0))
    stacked = jnp.concatenate([high, low, high], 0)
    contract = (((0,), (0,)), ((), ()))
    chunks, width, _ = out.shape
    copies = []
    for i in range(chunks):
        out[i] = lax.dot_general(
            stacked[:, i * width : (i + 1) * width],
            table_ref[...],
            contract,
            preferred_element_type=jnp.float32,
        )
        copies.append(
            pltpu.make_async_copy(out.at[i], out_ref.at[pl.ds(i * width, width)], sems.at[i])
        )
        copies[-1].start()
    for copy in copies:
        copy.wait()


def group_order(count):
    return [(3 * count // 4 - 1 - i) % count for i in range(count)]


def per_device(traces, mask, omega):
    narrow_count = lax.axis_size("narrow")
    wide_count = lax.axis_size("wide")
    assert traces.shape[:2] == (1, 1)
    first, second = narrow_count, wide_count
    freq_total = FREQ_DEV * wide_count
    keep1, keep2 = first // 2, second // 2
    span1, span2 = first - keep1 + 1, second - keep2 + 1
    rank = omega.shape[0] * narrow_count
    dests = wide_count * narrow_count
    lines = 2 * PIECES

    order = group_order(dests)
    high, low = halves(spectrum_table(freq_total, [i // narrow_count for i in order]))
    blocks = pl.pallas_call(
        spectrum_kernel,
        out_shape=jax.ShapeDtypeStruct((dests, lines, LANES), jnp.float32),
        in_specs=[HBM] * 3,
        out_specs=VMEM,
        scratch_shapes=[
            pltpu.VMEM((CHUNKS, CELLS, S // CHUNKS), jnp.float32),
            pltpu.VMEM((1, CELLS), jnp.int32),
            pltpu.VMEM((4 * dests, S), jnp.bfloat16),
            pltpu.SemaphoreType.DMA((2 + CHUNKS,)),
        ],
        name="spectrum",
    )(traces.reshape(CELLS, S), mask.reshape(1, CELLS), np.concatenate([high, low], 0))
    blocks, omega = lax.optimization_barrier((blocks, omega))
    omegas = [omega]
    for step in range(1, narrow_count):
        ring = [(i, (i + step) % narrow_count) for i in range(narrow_count)]
        omegas.append(lax.ppermute(omega, "narrow", ring))

    grid = lax.all_to_all(
        blocks,
        ("wide", "narrow"),
        split_axis=0,
        concat_axis=0,
        axis_index_groups=[order],
        tiled=True,
    )

    if omega.shape[0] % 8:
        omegas = [jnp.concatenate(omegas, 0)]
    columns = span1 * span2
    omega_hat = pl.pallas_call(
        functools.partial(omega_kernel, columns),
        out_shape=jax.ShapeDtypeStruct((columns * rank, 3 * CELLS), jnp.float32),
        in_specs=[VMEM] * (len(omegas) + 2),
        out_specs=VMEM,
        cost_estimate=pl.CostEstimate(
            flops=6 * columns * rank * LANES * 2 * CELLS,
            bytes_accessed=4 * columns * rank * 2 * CELLS,
            transcendentals=0,
        ),
        compiler_params=pltpu.CompilerParams(vmem_limit_bytes=16 * MIB),
        name="omega",
    )(*omegas, *halves(omega_table()))

    angles = centred_angles()
    counts = (
        correlation(first, keep1)[:, None, None]
        * correlation(second, keep2)[None, :, None]
        * np.outer(correlation(G3, KEEP3), correlation(G4, KEEP4)).reshape(1, 1, CELLS)
    ).reshape(first * second, CELLS)
    forward = np.concatenate([np.cos(angles), np.sin(angles)], 1)
    backward = np.concatenate([np.cos(angles.T), np.sin(angles.T)], 1) / CELLS
    tables = (
        *halves(forward),
        *halves(sketch_table()),
        *halves(basis_table()),
        *halves(window_table()),
        *halves(backward),
        (1.0 / counts).astype(np.float32),
    )
    area = keep1 * keep2 * rank
    scratch = [
        (first * second, 3 * PIECES, 8, LANES),
        (area, 2 * CELLS),
        (area, 2 * CELLS),
        (area, 2 * CELLS),
        (2 * span2 * rank, CELLS),
        (2 * second, CELLS),
    ]
    back_order = group_order(second)
    rebuilt = pl.pallas_call(
        functools.partial(core_kernel, (first, second, rank), order, back_order),
        out_shape=jax.ShapeDtypeStruct((second, lines, LANES), jnp.float32),
        in_specs=[VMEM] * (2 + len(tables)),
        out_specs=VMEM,
        scratch_shapes=[pltpu.VMEM(shape, jnp.float32) for shape in scratch],
        compiler_params=pltpu.CompilerParams(vmem_limit_bytes=24 * MIB),
        name="core",
    )(grid, omega_hat, *tables)
    returned = lax.all_to_all(
        rebuilt,
        "wide",
        split_axis=0,
        concat_axis=0,
        axis_index_groups=[back_order],
        tiled=True,
    )

    high, low = halves(synthesis_table(freq_total, back_order))
    filtered = pl.pallas_call(
        synthesis_kernel,
        out_shape=jax.ShapeDtypeStruct((CELLS, S), jnp.float32),
        in_specs=[VMEM] * 2,
        out_specs=HBM,
        scratch_shapes=[
            pltpu.VMEM((PIECES, LANES, S), jnp.float32),
            pltpu.SemaphoreType.DMA((PIECES,)),
        ],
        compiler_params=pltpu.CompilerParams(vmem_limit_bytes=8 * MIB),
        name="synthesis",
    )(returned, np.concatenate([high, high, low], 0))
    return filtered.reshape(traces.shape)


def solution(mesh):
    return jax.shard_map(
        per_device,
        mesh=mesh,
        in_specs=(
            P(("win", "narrow"), "wide", None, None),
            P(("win", "narrow"), "wide", None),
            P("narrow", None),
        ),
        out_specs=P(("win", "narrow"), "wide", None, None),
        check_vma=False,
    )
```
